128 devices in a mesh: fsdp: 2 (over core), ctx: 64 (over z, x, y).
Axes of the slice: x: 4, y: 4, z: 4, core: 2. Of those that a mesh axis runs over, the one named last changes fastest.
Arguments:
- token_ids: int32 [2, 8192], P('fsdp', 'ctx'), may hold values from 0 to 511
- embedding: bfloat16 [512, 4096], P(None, 'fsdp'), may hold values from -5 to 5
- conv_taps: float32 [3, 3, 4096], replicated, may hold values from -2.5 to 2.5
- residues: float32 [4096, 16], replicated, may hold values from -1.2 to 1.2
- decays: float32 [4096, 16], replicated, may hold values from 2.4414062e-06 to 0.05
- filter_seed: int32 [4096, 16], replicated, may hold values from 0 to 4095
- skip_gain: float32 [4096], replicated, may hold values from 0.5 to 1.5
- cotangent: float32 [2, 4096, 8192], P('fsdp', None, 'ctx'), may hold values from -6 to 6
Outputs:
- mixer_out: float32 [2, 4096, 8192], P('fsdp', None, 'ctx')
- embed_grad: float32 [512, 4096], P(None, 'fsdp')
The draws below stay inside these ranges and needn't reach their ends.
All inputs are finite; a program needn't handle non-finite values.
Results may differ from the reference program's by a relative error of at most 0.0006.
Values may be sent and summed in bfloat16 or wider, within the bound.
A program may use at most 320 MiB of HBM per device.

```python
import math
import jax
import jax.numpy as jnp

D = 4096
VOCAB = 512
MODES = 16
PERIOD = 4096
SEQ = 8192
BATCH = 2


def touch_ends(drawn, stream_key, least, high):
    longest = drawn.shape.index(max(drawn.shape))
    spots = []
    for shift in (0, 1):
        where = [jax.random.randint(jax.random.fold_in(stream_key, axis), (), 0, length) for axis, length in enumerate(drawn.shape)]
        where[longest] = (where[longest] + shift) % drawn.shape[longest]
        spots.append(tuple(where))
    return drawn.at[spots[0]].set(least).at[spots[1]].set(high)


def shard_levels(stream_key, dims, split, least, high):
    gain = 1.0
    for axis_at, shards_of in split:
        heights = jax.random.uniform(jax.random.fold_in(jax.random.fold_in(stream_key, 6), axis_at), (shards_of,), jnp.float32, least / len(split), high / len(split))
        gain = gain * jnp.repeat(jnp.exp(heights), dims[axis_at] // shards_of).reshape((-1,) + (1,) * (len(dims) - 1 - axis_at))
    return gain


def scatter_about(rng, dims, deviation, bound, pieces=(), kind=jnp.bfloat16):
    factor_of = shard_levels(rng, dims, pieces, -0.22, 0.18) if pieces else 1.0
    entries = jax.random.normal(rng, dims, jnp.float32) * deviation * factor_of
    return jnp.minimum(jnp.maximum(entries, -bound), bound).astype(kind)


def setup_inputs(seed: int = 0) -> dict:
    streams_of = jax.random.split(jax.random.key(seed), 9)
    token_ids = touch_ends(jax.random.randint(streams_of[0], (BATCH, SEQ), 0, VOCAB), jax.random.fold_in(streams_of[0], 1), 0, VOCAB - 1).astype(jnp.int32)
    embedding = scatter_about(streams_of[1], (VOCAB, D), 1.0, 5.0, ((1, 2),))
    conv_taps = scatter_about(streams_of[2], (3, 3, D), 0.6, 2.5, (), jnp.float32)
    residues = scatter_about(streams_of[3], (D, MODES), 0.3, 1.2, (), jnp.float32)
    decays = jnp.clip(jnp.exp(jax.random.uniform(streams_of[4], (D, MODES), jnp.float32, math.log(2.441406195430318e-06), math.log(0.05))), 2.441406195430318e-06, 0.05)
    filter_seed = touch_ends(jax.random.randint(streams_of[5], (D, MODES), 0, PERIOD), jax.random.fold_in(streams_of[5], 1), 0, PERIOD - 1).astype(jnp.int32)
    skip_gain = jnp.clip(jax.random.uniform(streams_of[6], (D,), jnp.float32, 0.5, 1.5), 0.5, 1.5)
    cotangent = scatter_about(streams_of[7], (BATCH, D, SEQ), 1.0, 6.0, ((0, 2), (2, 64)), jnp.float32)
    return {"token_ids": token_ids, "embedding": embedding, "conv_taps": conv_taps, "residues": residues, "decays": decays, "filter_seed": filter_seed, "skip_gain": skip_gain, "cotangent": cotangent}


TWO_PI = 2.0 * math.pi

def filter_kernel(residues, decays, filter_seed):
    positions = jnp.arange(SEQ, dtype=jnp.int32)
    time_float = positions.astype(jnp.float32)
    kernel = jnp.zeros((D, SEQ), jnp.float32)
    for mode_index in range(MODES):
        decay_rate = decays[:, mode_index][:, None]
        phase_int = filter_seed[:, mode_index][:, None] * positions[None, :] % PERIOD
        phase_angle = TWO_PI / PERIOD * phase_int.astype(jnp.float32)
        weight = residues[:, mode_index][:, None] * jnp.sqrt(decay_rate + 1.0 / SEQ)
        kernel = kernel + weight * jnp.exp(-decay_rate * time_float[None, :]) * jnp.cos(phase_angle)
    return kernel

def causal_mix(signal, tap_set):
    padded = jnp.pad(signal, ((0, 0), (2, 0)))
    return tap_set[0][:, None] * signal + tap_set[1][:, None] * padded[:, 1:SEQ + 1] + tap_set[2][:, None] * padded[:, :SEQ]

def reverse_mix(gradient, tap_set):
    padded = jnp.pad(gradient, ((0, 0), (0, 2)))
    return tap_set[0][:, None] * gradient + tap_set[1][:, None] * padded[:, 1:SEQ + 1] + tap_set[2][:, None] * padded[:, 2:SEQ + 2]

def reference(token_ids, embedding, conv_taps, residues, decays, filter_seed, skip_gain, cotangent):
    kernel = filter_kernel(residues, decays, filter_seed)
    length = 2 * SEQ
    spectrum = jnp.fft.rfft(kernel, n=length, axis=-1)
    skip_column = skip_gain[:, None]
    outputs = []
    grad_table = jnp.zeros((VOCAB, D), jnp.float32)
    for seq_index in range(BATCH):
        signal = jnp.take(embedding, token_ids[seq_index], axis=0).astype(jnp.float32).T
        query_stream = causal_mix(signal, conv_taps[0])
        key_stream = causal_mix(signal, conv_taps[1])
        value_stream = causal_mix(signal, conv_taps[2])
        mixed_in = key_stream * value_stream
        conv_full = jnp.fft.irfft(jnp.fft.rfft(mixed_in, n=length, axis=-1) * spectrum, n=length, axis=-1)[:, :SEQ]
        long_out = conv_full + skip_column * mixed_in
        outputs.append(query_stream * long_out)
        grad_long = cotangent[seq_index] * query_stream
        grad_query = cotangent[seq_index] * long_out
        correlated = jnp.fft.irfft(jnp.conj(spectrum) * jnp.fft.rfft(grad_long, n=length, axis=-1), n=length, axis=-1)[:, :SEQ]
        grad_mixed = correlated + skip_column * grad_long
        grad_signal = reverse_mix(grad_query, conv_taps[0]) + reverse_mix(grad_mixed * value_stream, conv_taps[1]) + reverse_mix(grad_mixed * key_stream, conv_taps[2])
        grad_table = grad_table + jax.ops.segment_sum(grad_signal.T, token_ids[seq_index], num_segments=VOCAB)
    return (jnp.stack(outputs), grad_table)
```

```python
import functools
import math

import jax
import jax.numpy as jnp
from jax import lax
from jax.experimental import pallas as pl
from jax.experimental.pallas import tpu as pltpu
from jax.sharding import PartitionSpec as P

PERIOD = 4096
F32 = jnp.float32
BF16 = jnp.bfloat16
LANES = 128
GROUP = 8


def iota(shape, dim):
    return lax.broadcasted_iota(jnp.int32, shape, dim)


def split(value):
    high = value.astype(BF16)
    return high, (value - high.astype(F32)).astype(BF16)


def cis(phase):
    quarter = PERIOD // 4
    turn = (phase + quarter // 2) // quarter
    a = (phase - turn * quarter).astype(F32) * (2.0 * math.pi / PERIOD)
    b = a * a
    s = a * (1.0 + b * (-1 / 6 + b * (1 / 120 + b * (-1 / 5040 + b * (1 / 362880)))))
    c = 1.0 + b * (-0.5 + b * (1 / 24 + b * (-1 / 720 + b * (1 / 40320))))
    odd = turn % 2 == 1
    re = jnp.where(odd, s, c)
    im = jnp.where(odd, c, s)
    re = jnp.where((turn == 1) | (turn == 2), -re, re)
    im = jnp.where((turn == 2) | (turn == 3), -im, im)
    return re, im


def power(rate, seed, steps):
    mag = jnp.exp(-rate * steps.astype(F32))
    re, im = cis((seed * steps) % PERIOD)
    return mag * re, mag * im


def nn(a, b):
    return jnp.dot(a, b, preferred_element_type=F32)


def nt(a, b):
    return lax.dot_general(a, b, (((1,), (1,)), ((), ())), preferred_element_type=F32)


def three(dot, left, right):
    left_high, left_low = left
    right_high, right_low = right
    rows = left_high.shape[0]
    both = dot(jnp.concatenate([left_high, left_low], axis=0), right_high)
    return both[:rows] + both[rows:] + dot(left_high, right_low)


def block_kernel(
    chunks, modes, seq_len,
    tok, table, taps, residues, decays, seeds, cot,
    mixed_out, table_grad,
    query, key, value, mix, long_out,
    bank, toeplitz, diag, state_rows,
):
    rows = tok.shape[0]
    slab = table.shape[0]
    vocab = table.shape[1]
    groups = slab // GROUP
    wide = GROUP * modes

    spread = (iota((slab * modes, slab), 0) // modes == iota((slab * modes, slab), 1)).astype(F32)
    pick = iota((slab * modes, modes), 0) % modes == iota((slab * modes, modes), 1)

    def column(part):
        wide_part = jnp.dot(spread, part, precision=lax.Precision.HIGHEST, preferred_element_type=F32)
        return jnp.sum(jnp.where(pick, wide_part, 0.0), axis=1, keepdims=True)

    rate = column(decays[...])
    seed = column(seeds[...].astype(F32))
    res = column(residues[...])
    weight = res * jnp.sqrt(rate + 1.0 / seq_len)
    seed_int = (seed + 0.5).astype(jnp.int32)
    rate_b = jnp.broadcast_to(rate, (slab * modes, LANES))
    seed_b = jnp.broadcast_to(seed_int, (slab * modes, LANES))
    lane = iota((slab * modes, LANES), 1)
    up = power(rate_b, seed_b, lane)
    down = power(rate_b, seed_b, LANES - 1 - lane)
    for place, part in enumerate((*up, *down)):
        high, low = split(part)
        bank[2 * place] = high
        bank[2 * place + 1] = low
    kernel_head = jnp.sum((up[0] * weight).reshape(slab, modes, LANES), axis=1)
    kernel_head = kernel_head + jnp.where(iota((slab, LANES), 1) == 0, taps[9], 0.0)

    upper = iota((LANES, LANES), 1) >= iota((LANES, LANES), 0)
    for c in range(slab):
        line = jnp.broadcast_to(kernel_head[c : c + 1], (LANES, LANES))
        rolled = pltpu.roll(line, 0, 1, stride=1, stride_axis=0)
        high, low = split(jnp.where(upper, rolled, 0.0))
        toeplitz[0, c] = high
        toeplitz[1, c] = low

    eye = iota((wide, LANES), 0) == iota((wide, LANES), 1)
    step_row = iota((8, LANES), 0)
    steps = jnp.where(step_row == 6, 1, LANES * (1 << jnp.minimum(step_row, 5)))
    for g in range(groups):
        def row(part):
            piece = jnp.broadcast_to(part[g * wide : (g + 1) * wide], (wide, LANES))
            return jnp.sum(jnp.where(eye, piece, 0.0), axis=0, keepdims=True)

        rate_row = jnp.broadcast_to(row(rate), (8, LANES))
        seed_row = jnp.broadcast_to((row(seed) + 0.5).astype(jnp.int32), (8, LANES))
        weight_row = row(weight)
        re, im = power(rate_row, seed_row, steps)
        scale = jnp.where(step_row == 6, jnp.broadcast_to(weight_row, (8, LANES)), 1.0)
        state_rows[g, 0] = re * scale
        state_rows[g, 1] = im * scale

    diag[...] = jnp.zeros_like(diag)

    lane_c = iota((slab, LANES), 1)
    vocab_row = iota((vocab, LANES), 0)

    def one_hot(r):
        return jnp.where(vocab_row == tok[pl.ds(r, 1), :], 1.0, 0.0).astype(BF16)

    UNROLL = 4

    def gather(step, carry):
        last_one, last_two = carry
        r0 = step * UNROLL
        hot = jnp.concatenate([one_hot(r0 + i) for i in range(UNROLL)], axis=1)
        found = nn(table[...], hot)
        fresh = (r0 % chunks) == 0
        last_one = jnp.where(fresh, 0.0, last_one)
        last_two = jnp.where(fresh, 0.0, last_two)
        for i in range(UNROLL):
            x = found[:, i * LANES : (i + 1) * LANES]
            one = pltpu.roll(x, 1, 1)
            two = pltpu.roll(x, 2, 1)
            x1 = jnp.where(lane_c < 1, last_one, one)
            x2 = jnp.where(lane_c < 2, last_two, two)
            last_one, last_two = one, two
            q, k, v = (taps[3 * s] * x + taps[3 * s + 1] * x1 + taps[3 * s + 2] * x2 for s in range(3))
            at = pl.ds(pl.multiple_of((r0 + i) * slab, slab), slab)
            query[at, :] = q
            key[at, :] = k
            value[at, :] = v
            mix[at, :] = k * v
        return last_one, last_two

    zero = jnp.zeros((slab, LANES), F32)
    lax.fori_loop(0, rows // UNROLL, gather, (zero, zero))

    row_in_seq = iota((rows, LANES), 0) % chunks

    def scan(re, im, g, backward):
        for j in range(max(1, (chunks - 1).bit_length())):
            shift = 1 << j
            amount = rows - shift if backward else shift
            keep = row_in_seq < chunks - shift if backward else row_in_seq >= shift
            old_re = jnp.where(keep, pltpu.roll(re, amount, 0), 0.0)
            old_im = jnp.where(keep, pltpu.roll(im, amount, 0), 0.0)
            a, b = state_rows[g, 0, j : j + 1, :], state_rows[g, 1, j : j + 1, :]
            re, im = re + a * old_re - b * old_im, im + a * old_im + b * old_re
        amount = rows - 1 if backward else 1
        keep = row_in_seq < chunks - 1 if backward else row_in_seq >= 1
        re = jnp.where(keep, pltpu.roll(re, amount, 0), 0.0)
        im = jnp.where(keep, pltpu.roll(im, amount, 0), 0.0)
        a, b = state_rows[g, 0, 6:7, :], state_rows[g, 1, 6:7, :]
        return a * re - b * im, -(a * im + b * re)

    def long_conv(source, target, backward):
        enter, leave = (0, 2) if backward else (2, 0)

        def per_group(g, _):
            base = g * GROUP
            for side, first in enumerate((enter, leave)):
                for c in range(GROUP):
                    at = pl.ds(pl.multiple_of(g * wide + c * modes, modes), modes)
                    for half in range(2):
                        spot = slice(half * wide + c * modes, half * wide + (c + 1) * modes)
                        for part in range(2):
                            diag[side, part, spot, c * LANES : (c + 1) * LANES] = bank[
                                2 * (first + half) + part, at, :
                            ]
            local = jnp.zeros((rows, 2 * wide), F32)
            for c in range(GROUP):
                u = split(source[pl.ds(base + c, rows, stride=slab), :])
                at = slice(c * LANES, (c + 1) * LANES)
                local = local + three(nt, u, (diag[0, 0, :, at], diag[0, 1, :, at]))
            re, im = scan(local[:, :wide], local[:, wide:], g, backward)
            state = split(jnp.concatenate([re, im], axis=1))
            for c in range(GROUP):
                u = split(source[pl.ds(base + c, rows, stride=slab), :])
                at = slice(c * LANES, (c + 1) * LANES)
                band = (toeplitz[0, base + c], toeplitz[1, base + c])
                out = three(nt if backward else nn, u, band)
                out = out + three(nn, state, (diag[1, 0, :, at], diag[1, 1, :, at]))
                target[pl.ds(base + c, rows, stride=slab), :] = out
            return 0

        lax.fori_loop(0, groups, per_group, 0)

    long_conv(mix, long_out, False)

    def emit(r, _):
        at = pl.ds(pl.multiple_of(r * slab, slab), slab)
        q = query[at, :]
        mixed_out[at, :] = q * long_out[at, :]
        mix[at, :] = cot[at, :] * q
        return 0

    lax.fori_loop(0, rows, emit, 0, unroll=4)

    grad_mixed = query
    long_conv(mix, grad_mixed, True)

    def scatter(step, carry):
        next_one, next_two, total = carry
        r0 = rows - UNROLL - step * UNROLL
        fresh = (r0 % chunks) == chunks - UNROLL
        next_one = jnp.where(fresh, 0.0, next_one)
        next_two = jnp.where(fresh, 0.0, next_two)
        pieces = [None] * UNROLL
        for i in reversed(range(UNROLL)):
            at = pl.ds(pl.multiple_of((r0 + i) * slab, slab), slab)
            gm = grad_mixed[at, :]
            gq = cot[at, :] * long_out[at, :]
            gk = gm * value[at, :]
            gv = gm * key[at, :]
            zeroth, first, second = (taps[j] * gq + taps[3 + j] * gk + taps[6 + j] * gv for j in range(3))
            one = pltpu.roll(first, LANES - 1, 1)
            two = pltpu.roll(second, LANES - 2, 1)
            gx = (
                zeroth
                + jnp.where(lane_c >= LANES - 1, next_one, one)
                + jnp.where(lane_c >= LANES - 2, next_two, two)
            )
            next_one, next_two = one, two
            pieces[i] = jnp.concatenate(split(gx), axis=0)
        hot = jnp.concatenate([one_hot(r0 + i) for i in range(UNROLL)], axis=1)
        return next_one, next_two, total + nt(jnp.concatenate(pieces, axis=1), hot)

    _, _, total = lax.fori_loop(
        0, rows // UNROLL, scatter, (zero, zero, jnp.zeros((2 * slab, vocab), F32))
    )
    table_grad[...] = total[:slab] + total[slab:]


def run_block(tok, table, taps, residues, decays, seeds, cot, chunks, seq_len):
    rows = tok.shape[0]
    slab, vocab = table.shape
    modes = residues.shape[1]
    tall = rows * slab
    vmem = pl.BlockSpec(memory_space=pltpu.VMEM)
    return pl.pallas_call(
        functools.partial(block_kernel, chunks, modes, seq_len),
        out_shape=(
            jax.ShapeDtypeStruct((tall, LANES), F32),
            jax.ShapeDtypeStruct((slab, vocab), F32),
        ),
        in_specs=[vmem] * 7,
        out_specs=(vmem, vmem),
        scratch_shapes=[pltpu.VMEM((tall, LANES), F32)] * 5
        + [
            pltpu.VMEM((8, slab * modes, LANES), BF16),
            pltpu.VMEM((2, slab, LANES, LANES), BF16),
            pltpu.VMEM((2, 2, 2 * GROUP * modes, GROUP * LANES), BF16),
            pltpu.VMEM((slab // GROUP, 2, 8, LANES), F32),
        ],
        compiler_params=pltpu.CompilerParams(vmem_limit_bytes=56 * 1024 * 1024),
        name="hyena_block",
    )(tok, table, taps, residues, decays, seeds, cot)


def pack_taps(conv_taps, skip_gain, start, slab):
    taps = lax.dynamic_slice_in_dim(conv_taps.reshape(9, -1), start, slab, 1)
    gain = lax.dynamic_slice_in_dim(skip_gain, start, slab, 0)[None]
    return jnp.broadcast_to(jnp.concatenate([taps, gain])[:, :, None], (10, slab, LANES))


def body(token_ids, embedding, conv_taps, residues, decays, filter_seed, skip_gain, cotangent):
    axes = ("fsdp", "ctx")
    ctx_size = lax.axis_size("ctx")
    count = ctx_size * lax.axis_size("fsdp")
    width = conv_taps.shape[2]
    slab = width // count
    tok_block = token_ids.shape[1]
    rank = lax.axis_index("ctx")
    start = (lax.axis_index("fsdp") * ctx_size + rank) * slab
    tok = lax.all_gather(token_ids, axes, axis=0, tiled=True)
    table = lax.dynamic_slice_in_dim(embedding, rank * slab, slab, 1).T
    taps = pack_taps(conv_taps, skip_gain, start, slab)
    part = [lax.dynamic_slice_in_dim(p, start, slab, 0) for p in (residues, decays, filter_seed)]
    cot = lax.all_to_all(
        cotangent.reshape(width, tok_block), axes, split_axis=0, concat_axis=0, tiled=True
    )
    mixed, grad = run_block(tok, table, taps, *part, cot, ctx_size, ctx_size * tok_block)
    mixer = lax.all_to_all(mixed, axes, split_axis=0, concat_axis=0, tiled=True)
    grad = lax.all_gather(grad, "ctx", axis=0, tiled=True)
    return mixer.reshape(cotangent.shape), grad.T


def solution(mesh):
    placed = (P("fsdp", "ctx"), P(None, "fsdp"), P(), P(), P(), P(), P(), P("fsdp", None, "ctx"))
    return jax.shard_map(
        body,
        mesh=mesh,
        in_specs=placed,
        out_specs=(P("fsdp", None, "ctx"), P(None, "fsdp")),
        check_vma=False,
    )
```

```python
import functools
import math

import jax
import jax.numpy as jnp
from jax import lax
from jax.experimental import pallas as pl
from jax.experimental.pallas import tpu as pltpu
from jax.sharding import PartitionSpec as P

PERIOD = 4096
F32 = jnp.float32
BF16 = jnp.bfloat16
LANES = 128
GROUP = 8


def iota(shape, dim):
    return lax.broadcasted_iota(jnp.int32, shape, dim)


def split(value):
    high = value.astype(BF16)
    return high, (value - high.astype(F32)).astype(BF16)


def cis(phase):
    quarter = PERIOD // 4
    turn = (phase + quarter // 2) // quarter
    a = (phase - turn * quarter).astype(F32) * (2.0 * math.pi / PERIOD)
    b = a * a
    s = a * (1.0 + b * (-1 / 6 + b * (1 / 120 + b * (-1 / 5040 + b * (1 / 362880)))))
    c = 1.0 + b * (-0.5 + b * (1 / 24 + b * (-1 / 720 + b * (1 / 40320))))
    odd = turn % 2 == 1
    re = jnp.where(odd, s, c)
    im = jnp.where(odd, c, s)
    re = jnp.where((turn == 1) | (turn == 2), -re, re)
    im = jnp.where((turn == 2) | (turn == 3), -im, im)
    return re, im


def power(rate, seed, steps):
    mag = jnp.exp(-rate * steps.astype(F32))
    re, im = cis((seed * steps) % PERIOD)
    return mag * re, mag * im


def nn(a, b):
    return jnp.dot(a, b, preferred_element_type=F32)


def nt(a, b):
    return lax.dot_general(a, b, (((1,), (1,)), ((), ())), preferred_element_type=F32)


def three(dot, left, right):
    left_high, left_low = left
    right_high, right_low = right
    rows = left_high.shape[0]
    both = dot(jnp.concatenate([left_high, left_low], axis=0), right_high)
    return both[:rows] + both[rows:] + dot(left_high, right_low)


MESH = pl.DeviceIdType.MESH


def block_kernel(
    chunks, seq_len,
    tok_mine, embedding, conv_taps, gains, residue_all, decay_all, seed_all, cot_mine,
    mixer, table_grad,
    query, key, value, mix, long_out, cot, mixed_out,
    tok, table, taps, residues, decays, seeds, raw_table, turned, raw_taps,
    bank, toeplitz, diag, state_rows,
    load_sems, tok_sems, cot_sems, mixer_sems,
):
    rows = tok.shape[0]
    slab = table.shape[0]
    vocab = table.shape[1]
    modes = residues.shape[1]
    groups = slab // GROUP
    wide = GROUP * modes
    ctx = lax.axis_index("ctx")
    me = lax.axis_index("fsdp") * chunks + ctx
    per_tile = LANES // slab

    def device(i):
        peer = lax.rem(me + i, rows)
        return peer, (peer // chunks, lax.rem(peer, chunks))

    def slab_rows(index):
        return pl.ds(pl.multiple_of(index * slab, slab), slab)

    barrier = pltpu.get_barrier_semaphore()

    @pl.loop(1, rows)
    def _(i):
        pl.semaphore_signal(barrier, inc=1, device_id=device(i)[1], device_id_type=MESH)

    lane_tile = pl.ds(pl.multiple_of(ctx // per_tile * LANES, LANES), LANES)
    wide_tile = pl.ds(pl.multiple_of(me // per_tile * LANES, LANES), LANES)
    loads = [
        pltpu.make_async_copy(source, target, load_sems.at[n])
        for n, (source, target) in enumerate((
            (residue_all.at[slab_rows(me)], residues),
            (decay_all.at[slab_rows(me)], decays),
            (seed_all.at[slab_rows(me)], seeds),
            (conv_taps.at[:, :, wide_tile], raw_taps),
            (embedding.at[:, lane_tile], raw_table),
        ))
    ]
    for load in loads:
        load.start()
    pl.semaphore_wait(barrier, rows - 1)

    own_tok = pltpu.make_async_copy(tok_mine, tok.at[pl.ds(me, 1)], tok_sems.at[1])
    own_tok.start()

    @pl.loop(1, rows)
    def _(i):
        pltpu.make_async_remote_copy(
            src_ref=tok_mine, dst_ref=tok.at[pl.ds(me, 1)],
            send_sem=tok_sems.at[0], recv_sem=tok_sems.at[1],
            device_id=device(i)[1], device_id_type=MESH,
        ).start()

    own_cot = pltpu.make_async_copy(cot_mine.at[slab_rows(me)], cot.at[slab_rows(me)], cot_sems.at[1])
    own_cot.start()

    @pl.loop(1, rows)
    def _(i):
        peer, where = device(i)
        pltpu.make_async_remote_copy(
            src_ref=cot_mine.at[slab_rows(peer)], dst_ref=cot.at[slab_rows(me)],
            send_sem=cot_sems.at[0], recv_sem=cot_sems.at[1],
            device_id=where, device_id_type=MESH,
        ).start()

    def wait_bytes(ref, sem):
        pltpu.make_async_copy(ref, ref, sem).wait()

    for load in loads:
        load.wait()
    sub = pl.ds(pl.multiple_of(lax.rem(ctx, per_tile) * slab, slab), slab)
    turned[...] = raw_table[...].astype(F32).T
    table[...] = turned[sub, :].astype(BF16)
    pieces = [raw_taps[s, j : j + 1, :] for s in range(3) for j in range(3)]
    pieces.append(gains[pl.ds(me // per_tile, 1), :])
    pieces.append(jnp.zeros((LANES - 10, LANES), F32))
    turned[:, :LANES] = jnp.concatenate(pieces, axis=0).T
    columns = turned[sub, :LANES]
    for j in range(10):
        taps[j] = jnp.broadcast_to(columns[:, j : j + 1], (slab, LANES))

    spread = (iota((slab * modes, slab), 0) // modes == iota((slab * modes, slab), 1)).astype(F32)
    pick = iota((slab * modes, modes), 0) % modes == iota((slab * modes, modes), 1)

    def column(part):
        wide_part = jnp.dot(spread, part, precision=lax.Precision.HIGHEST, preferred_element_type=F32)
        return jnp.sum(jnp.where(pick, wide_part, 0.0), axis=1, keepdims=True)

    rate = column(decays[...])
    seed = column(seeds[...].astype(F32))
    res = column(residues[...])
    weight = res * jnp.sqrt(rate + 1.0 / seq_len)
    seed_int = (seed + 0.5).astype(jnp.int32)
    rate_b = jnp.broadcast_to(rate, (slab * modes, LANES))
    seed_b = jnp.broadcast_to(seed_int, (slab * modes, LANES))
    lane = iota((slab * modes, LANES), 1)
    up = power(rate_b, seed_b, lane)
    down = power(rate_b, seed_b, LANES - 1 - lane)
    for place, part in enumerate((*up, *down)):
        high, low = split(part)
        bank[2 * place] = high
        bank[2 * place + 1] = low
    kernel_head = jnp.sum((up[0] * weight).reshape(slab, modes, LANES), axis=1)
    kernel_head = kernel_head + jnp.where(iota((slab, LANES), 1) == 0, taps[9], 0.0)

    upper = iota((LANES, LANES), 1) >= iota((LANES, LANES), 0)
    for c in range(slab):
        line = jnp.broadcast_to(kernel_head[c : c + 1], (LANES, LANES))
        rolled = pltpu.roll(line, 0, 1, stride=1, stride_axis=0)
        high, low = split(jnp.where(upper, rolled, 0.0))
        toeplitz[0, c] = high
        toeplitz[1, c] = low

    eye = iota((wide, LANES), 0) == iota((wide, LANES), 1)
    step_row = iota((8, LANES), 0)
    steps = jnp.where(step_row == 6, 1, LANES * (1 << jnp.minimum(step_row, 5)))
    for g in range(groups):
        def row(part):
            piece = jnp.broadcast_to(part[g * wide : (g + 1) * wide], (wide, LANES))
            return jnp.sum(jnp.where(eye, piece, 0.0), axis=0, keepdims=True)

        rate_row = jnp.broadcast_to(row(rate), (8, LANES))
        seed_row = jnp.broadcast_to((row(seed) + 0.5).astype(jnp.int32), (8, LANES))
        weight_row = row(weight)
        re, im = power(rate_row, seed_row, steps)
        scale = jnp.where(step_row == 6, jnp.broadcast_to(weight_row, (8, LANES)), 1.0)
        state_rows[g, 0] = re * scale
        state_rows[g, 1] = im * scale

    diag[...] = jnp.zeros_like(diag)

    wait_bytes(tok, tok_sems.at[1])
    lane_c = iota((slab, LANES), 1)
    vocab_row = iota((vocab, LANES), 0)

    def one_hot(r):
        return jnp.where(vocab_row == tok[pl.ds(r, 1), :], 1.0, 0.0).astype(BF16)

    UNROLL = 4

    def gather(step, carry):
        last_one, last_two = carry
        r0 = step * UNROLL
        hot = jnp.concatenate([one_hot(r0 + i) for i in range(UNROLL)], axis=1)
        found = nn(table[...], hot)
        fresh = (r0 % chunks) == 0
        last_one = jnp.where(fresh, 0.0, last_one)
        last_two = jnp.where(fresh, 0.0, last_two)
        for i in range(UNROLL):
            x = found[:, i * LANES : (i + 1) * LANES]
            one = pltpu.roll(x, 1, 1)
            two = pltpu.roll(x, 2, 1)
            x1 = jnp.where(lane_c < 1, last_one, one)
            x2 = jnp.where(lane_c < 2, last_two, two)
            last_one, last_two = one, two
            q, k, v = (taps[3 * s] * x + taps[3 * s + 1] * x1 + taps[3 * s + 2] * x2 for s in range(3))
            at = pl.ds(pl.multiple_of((r0 + i) * slab, slab), slab)
            query[at, :] = q
            key[at, :] = k
            value[at, :] = v
            mix[at, :] = k * v
        return last_one, last_two

    zero = jnp.zeros((slab, LANES), F32)
    lax.fori_loop(0, rows // UNROLL, gather, (zero, zero))

    row_in_seq = iota((rows, LANES), 0) % chunks

    def scan(re, im, g, backward):
        for j in range(max(1, (chunks - 1).bit_length())):
            shift = 1 << j
            amount = rows - shift if backward else shift
            keep = row_in_seq < chunks - shift if backward else row_in_seq >= shift
            old_re = jnp.where(keep, pltpu.roll(re, amount, 0), 0.0)
            old_im = jnp.where(keep, pltpu.roll(im, amount, 0), 0.0)
            a, b = state_rows[g, 0, j : j + 1, :], state_rows[g, 1, j : j + 1, :]
            re, im = re + a * old_re - b * old_im, im + a * old_im + b * old_re
        amount = rows - 1 if backward else 1
        keep = row_in_seq < chunks - 1 if backward else row_in_seq >= 1
        re = jnp.where(keep, pltpu.roll(re, amount, 0), 0.0)
        im = jnp.where(keep, pltpu.roll(im, amount, 0), 0.0)
        a, b = state_rows[g, 0, 6:7, :], state_rows[g, 1, 6:7, :]
        return a * re - b * im, -(a * im + b * re)

    def long_conv(source, target, backward):
        enter, leave = (0, 2) if backward else (2, 0)

        def per_group(g, _):
            base = g * GROUP
            for side, first in enumerate((enter, leave)):
                for c in range(GROUP):
                    at = pl.ds(pl.multiple_of(g * wide + c * modes, modes), modes)
                    for half in range(2):
                        spot = slice(half * wide + c * modes, half * wide + (c + 1) * modes)
                        for part in range(2):
                            diag[side, part, spot, c * LANES : (c + 1) * LANES] = bank[
                                2 * (first + half) + part, at, :
                            ]
            local = jnp.zeros((rows, 2 * wide), F32)
            for c in range(GROUP):
                u = split(source[pl.ds(base + c, rows, stride=slab), :])
                at = slice(c * LANES, (c + 1) * LANES)
                local = local + three(nt, u, (diag[0, 0, :, at], diag[0, 1, :, at]))
            re, im = scan(local[:, :wide], local[:, wide:], g, backward)
            state = split(jnp.concatenate([re, im], axis=1))
            for c in range(GROUP):
                u = split(source[pl.ds(base + c, rows, stride=slab), :])
                at = slice(c * LANES, (c + 1) * LANES)
                band = (toeplitz[0, base + c], toeplitz[1, base + c])
                out = three(nt if backward else nn, u, band)
                out = out + three(nn, state, (diag[1, 0, :, at], diag[1, 1, :, at]))
                target[pl.ds(base + c, rows, stride=slab), :] = out
            return 0

        lax.fori_loop(0, groups, per_group, 0)

    long_conv(mix, long_out, False)

    def emit(i, _):
        r, where = device(i)
        at = slab_rows(r)
        mixed_out[at, :] = query[at, :] * long_out[at, :]
        pltpu.make_async_remote_copy(
            src_ref=mixed_out.at[at], dst_ref=mixer.at[slab_rows(me)],
            send_sem=mixer_sems.at[0], recv_sem=mixer_sems.at[1],
            device_id=where, device_id_type=MESH,
        ).start()
        return 0

    mixed_out[slab_rows(me), :] = query[slab_rows(me), :] * long_out[slab_rows(me), :]
    pltpu.make_async_copy(
        mixed_out.at[slab_rows(me)], mixer.at[slab_rows(me)], mixer_sems.at[1]
    ).start()
    lax.fori_loop(1, rows, emit, 0)
    wait_bytes(cot, cot_sems.at[1])

    def weigh(r, _):
        mix[slab_rows(r), :] = cot[slab_rows(r), :] * query[slab_rows(r), :]
        return 0

    lax.fori_loop(0, rows, weigh, 0, unroll=8)

    grad_mixed = query
    long_conv(mix, grad_mixed, True)

    def scatter(step, carry):
        next_one, next_two, total = carry
        r0 = rows - UNROLL - step * UNROLL
        fresh = (r0 % chunks) == chunks - UNROLL
        next_one = jnp.where(fresh, 0.0, next_one)
        next_two = jnp.where(fresh, 0.0, next_two)
        pieces = [None] * UNROLL
        for i in reversed(range(UNROLL)):
            at = pl.ds(pl.multiple_of((r0 + i) * slab, slab), slab)
            gm = grad_mixed[at, :]
            gq = cot[at, :] * long_out[at, :]
            gk = gm * value[at, :]
            gv = gm * key[at, :]
            zeroth, first, second = (taps[j] * gq + taps[3 + j] * gk + taps[6 + j] * gv for j in range(3))
            one = pltpu.roll(first, LANES - 1, 1)
            two = pltpu.roll(second, LANES - 2, 1)
            gx = (
                zeroth
                + jnp.where(lane_c >= LANES - 1, next_one, one)
                + jnp.where(lane_c >= LANES - 2, next_two, two)
            )
            next_one, next_two = one, two
            pieces[i] = jnp.concatenate(split(gx), axis=0)
        hot = jnp.concatenate([one_hot(r0 + i) for i in range(UNROLL)], axis=1)
        return next_one, next_two, total + nt(jnp.concatenate(pieces, axis=1), hot)

    _, _, total = lax.fori_loop(
        0, rows // UNROLL, scatter, (zero, zero, jnp.zeros((2 * slab, vocab), F32))
    )
    table_grad[...] = total[:slab] + total[slab:]
    most = pl.ds(0, (rows - 1) * slab)
    wait_bytes(tok.at[pl.ds(0, rows - 1)], tok_sems.at[0])
    wait_bytes(cot.at[most], cot_sems.at[0])
    wait_bytes(mixed_out.at[most], mixer_sems.at[0])
    wait_bytes(mixer, mixer_sems.at[1])


def run_block(tok, embedding, conv_taps, gains, residues, decays, seeds, cot, chunks):
    width, modes = residues.shape
    vocab = embedding.shape[0]
    rows = width // (embedding.shape[1] // chunks)
    slab = width // rows
    tall = rows * slab
    vmem = pl.BlockSpec(memory_space=pltpu.VMEM)
    hbm = pl.BlockSpec(memory_space=pl.ANY)
    dma = pltpu.SemaphoreType.DMA
    return pl.pallas_call(
        functools.partial(block_kernel, chunks, chunks * LANES),
        out_shape=(
            jax.ShapeDtypeStruct((tall, LANES), F32),
            jax.ShapeDtypeStruct((slab, vocab), F32),
        ),
        in_specs=[vmem, hbm, hbm, vmem, hbm, hbm, hbm, hbm],
        out_specs=(hbm, vmem),
        scratch_shapes=[pltpu.VMEM((tall, LANES), F32)] * 7
        + [
            pltpu.VMEM((rows, LANES), jnp.int32),
            pltpu.VMEM((slab, vocab), BF16),
            pltpu.VMEM((10, slab, LANES), F32),
            pltpu.VMEM((slab, modes), F32),
            pltpu.VMEM((slab, modes), F32),
            pltpu.VMEM((slab, modes), jnp.int32),
            pltpu.VMEM((vocab, LANES), BF16),
            pltpu.VMEM((LANES, vocab), F32),
            pltpu.VMEM((3, 3, LANES), F32),
            pltpu.VMEM((8, slab * modes, LANES), BF16),
            pltpu.VMEM((2, slab, LANES, LANES), BF16),
            pltpu.VMEM((2, 2, 2 * GROUP * modes, GROUP * LANES), BF16),
            pltpu.VMEM((slab // GROUP, 2, 8, LANES), F32),
            dma((5,)), dma((2,)), dma((2,)), dma((2,)),
        ],
        compiler_params=pltpu.CompilerParams(
            vmem_limit_bytes=56 * 1024 * 1024, collective_id=0, has_side_effects=True
        ),
        name="hyena_block",
    )(tok, embedding, conv_taps, gains, residues, decays, seeds, cot)


def spread_kernel(sides, mine, every, own_sem, sems):
    chunks = every.shape[0]
    ctx = lax.axis_index("ctx")
    fsdp = lax.axis_index("fsdp")
    barrier = pltpu.get_barrier_semaphore()

    def peer(i):
        return (fsdp, lax.rem(ctx + i, chunks))

    @pl.loop(1, chunks)
    def _(i):
        pl.semaphore_signal(barrier, inc=1, device_id=peer(i), device_id_type=MESH)

    own = pltpu.make_async_copy(mine, every.at[ctx], own_sem)
    own.start()
    pl.semaphore_wait(barrier, chunks - 1)

    @pl.loop(1, chunks)
    def _(i):
        pltpu.make_async_remote_copy(
            src_ref=mine, dst_ref=every.at[ctx],
            send_sem=sems.at[0], recv_sem=sems.at[1],
            device_id=peer(i), device_id_type=MESH,
        ).start()

    own.wait()
    most = every.at[pl.ds(0, chunks - 1)]
    pltpu.make_async_copy(most, most, sems.at[0]).wait()
    pltpu.make_async_copy(most, most, sems.at[1]).wait()


def spread(block, chunks):
    hbm = pl.BlockSpec(memory_space=pl.ANY)
    return pl.pallas_call(
        functools.partial(spread_kernel, None),
        out_shape=jax.ShapeDtypeStruct((chunks, *block.shape), block.dtype),
        in_specs=[pl.BlockSpec(memory_space=pltpu.VMEM)],
        out_specs=hbm,
        scratch_shapes=[pltpu.SemaphoreType.DMA, pltpu.SemaphoreType.DMA((2,))],
        compiler_params=pltpu.CompilerParams(collective_id=1, has_side_effects=True),
        name="grad_spread",
    )(block)


def body(token_ids, embedding, conv_taps, residues, decays, filter_seed, skip_gain, cotangent):
    ctx_size = lax.axis_size("ctx")
    width = conv_taps.shape[2]
    tok_block = token_ids.shape[1]
    mixer, grad = run_block(
        token_ids, embedding, conv_taps, skip_gain.reshape(-1, LANES),
        residues, decays, filter_seed, cotangent.reshape(width, tok_block), ctx_size,
    )
    grad = spread(grad, ctx_size)
    return mixer.reshape(cotangent.shape), grad.reshape(-1, grad.shape[2]).T


def solution(mesh):
    placed = (P("fsdp", "ctx"), P(None, "fsdp"), P(), P(), P(), P(), P(), P("fsdp", None, "ctx"))
    return jax.shard_map(
        body,
        mesh=mesh,
        in_specs=placed,
        out_specs=(P("fsdp", None, "ctx"), P(None, "fsdp")),
        check_vma=False,
    )
```

```python
import functools
import math

import jax
import jax.numpy as jnp
from jax import lax
from jax.experimental import pallas as pl
from jax.experimental.pallas import tpu as pltpu
from jax.sharding import PartitionSpec as P

PERIOD = 4096
F32 = jnp.float32
BF16 = jnp.bfloat16
LANES = 128
GROUP = 8


def iota(shape, dim):
    return lax.broadcasted_iota(jnp.int32, shape, dim)


def split(value):
    high = value.astype(BF16)
    return high, (value - high.astype(F32)).astype(BF16)


def cis(phase):
    quarter = PERIOD // 4
    turn = (phase + quarter // 2) // quarter
    a = (phase - turn * quarter).astype(F32) * (2.0 * math.pi / PERIOD)
    b = a * a
    s = a * (1.0 + b * (-1 / 6 + b * (1 / 120 + b * (-1 / 5040 + b * (1 / 362880)))))
    c = 1.0 + b * (-0.5 + b * (1 / 24 + b * (-1 / 720 + b * (1 / 40320))))
    odd = turn % 2 == 1
    re = jnp.where(odd, s, c)
    im = jnp.where(odd, c, s)
    re = jnp.where((turn == 1) | (turn == 2), -re, re)
    im = jnp.where((turn == 2) | (turn == 3), -im, im)
    return re, im


def power(rate, seed, steps):
    mag = jnp.exp(-rate * steps.astype(F32))
    re, im = cis((seed * steps) % PERIOD)
    return mag * re, mag * im


def nn(a, b):
    return jnp.dot(a, b, preferred_element_type=F32)


def nt(a, b):
    return lax.dot_general(a, b, (((1,), (1,)), ((), ())), preferred_element_type=F32)


def three(dot, left, right):
    left_high, left_low = left
    right_high, right_low = right
    rows = left_high.shape[0]
    both = dot(jnp.concatenate([left_high, left_low], axis=0), right_high)
    return both[:rows] + both[rows:] + dot(left_high, right_low)


MESH = pl.DeviceIdType.MESH


def block_kernel(
    chunks, seq_len,
    tok_mine, embedding, conv_taps, gains, residue_all, decay_all, seed_all, cot_mine,
    mixer, table_grad,
    query, key, value, mix, long_out, cot, mixed_out,
    tok, table, taps, residues, decays, seeds, raw_table, turned, raw_taps,
    bank, toeplitz, diag, state_rows,
    load_sems, tok_sems, cot_sems, mixer_sems,
):
    rows = tok.shape[0]
    slab = table.shape[0]
    vocab = table.shape[1]
    modes = residues.shape[0]
    groups = slab // GROUP
    wide = GROUP * modes
    ctx = lax.axis_index("ctx")
    me = lax.axis_index("fsdp") * chunks + ctx
    per_tile = LANES // slab

    def device(i):
        peer = lax.rem(me + i, rows)
        return peer, (peer // chunks, lax.rem(peer, chunks))

    def slab_rows(index):
        return pl.ds(pl.multiple_of(index * slab, slab), slab)

    barrier = pltpu.get_barrier_semaphore()

    @pl.loop(1, rows)
    def _(i):
        pl.semaphore_signal(barrier, inc=1, device_id=device(i)[1], device_id_type=MESH)

    lane_tile = pl.ds(pl.multiple_of(ctx // per_tile * LANES, LANES), LANES)
    wide_tile = pl.ds(pl.multiple_of(me // per_tile * LANES, LANES), LANES)
    loads = [
        pltpu.make_async_copy(source, target, load_sems.at[n])
        for n, (source, target) in enumerate((
            (residue_all.at[:, wide_tile], residues),
            (decay_all.at[:, wide_tile], decays),
            (seed_all.at[:, wide_tile], seeds),
            (conv_taps.at[:, :, wide_tile], raw_taps),
            (embedding.at[:, lane_tile], raw_table),
        ))
    ]
    for load in loads:
        load.start()
    pl.semaphore_wait(barrier, rows - 1)

    own_tok = pltpu.make_async_copy(tok_mine, tok.at[pl.ds(me, 1)], tok_sems.at[1])
    own_tok.start()

    @pl.loop(1, rows)
    def _(i):
        pltpu.make_async_remote_copy(
            src_ref=tok_mine, dst_ref=tok.at[pl.ds(me, 1)],
            send_sem=tok_sems.at[0], recv_sem=tok_sems.at[1],
            device_id=device(i)[1], device_id_type=MESH,
        ).start()

    own_cot = pltpu.make_async_copy(cot_mine.at[slab_rows(me)], cot.at[slab_rows(me)], cot_sems.at[1])
    own_cot.start()

    @pl.loop(1, rows)
    def _(i):
        peer, where = device(i)
        pltpu.make_async_remote_copy(
            src_ref=cot_mine.at[slab_rows(peer)], dst_ref=cot.at[slab_rows(me)],
            send_sem=cot_sems.at[0], recv_sem=cot_sems.at[1],
            device_id=where, device_id_type=MESH,
        ).start()

    def wait_bytes(ref, sem):
        pltpu.make_async_copy(ref, ref, sem).wait()

    for load in loads:
        load.wait()
    sub = pl.ds(pl.multiple_of(lax.rem(ctx, per_tile) * slab, slab), slab)
    turned[...] = raw_table[...].astype(F32).T
    table[...] = turned[sub, :].astype(BF16)
    pieces = [residues[...], decays[...], seeds[...].astype(F32)]
    pieces += [raw_taps[s, j : j + 1, :] for s in range(3) for j in range(3)]
    pieces.append(gains[pl.ds(me // per_tile, 1), :])
    pieces.append(jnp.zeros((LANES - 10 - 3 * modes, LANES), F32))
    turned[:, :LANES] = jnp.concatenate(pieces, axis=0).T
    columns = turned[sub, :LANES]
    for j in range(10):
        taps[j] = jnp.broadcast_to(columns[:, 3 * modes + j : 3 * modes + j + 1], (slab, LANES))

    spread = (iota((slab * modes, slab), 0) // modes == iota((slab * modes, slab), 1)).astype(F32)
    pick = iota((slab * modes, modes), 0) % modes == iota((slab * modes, modes), 1)

    def column(part):
        wide_part = jnp.dot(spread, part, precision=lax.Precision.HIGHEST, preferred_element_type=F32)
        return jnp.sum(jnp.where(pick, wide_part, 0.0), axis=1, keepdims=True)

    rate = column(columns[:, modes : 2 * modes])
    seed = column(columns[:, 2 * modes : 3 * modes])
    res = column(columns[:, :modes])
    weight = res * jnp.sqrt(rate + 1.0 / seq_len)
    seed_int = (seed + 0.5).astype(jnp.int32)
    rate_b = jnp.broadcast_to(rate, (slab * modes, LANES))
    seed_b = jnp.broadcast_to(seed_int, (slab * modes, LANES))
    lane = iota((slab * modes, LANES), 1)
    up = power(rate_b, seed_b, lane)
    down = power(rate_b, seed_b, LANES - 1 - lane)
    for place, part in enumerate((*up, *down)):
        high, low = split(part)
        bank[2 * place] = high
        bank[2 * place + 1] = low
    kernel_head = jnp.sum((up[0] * weight).reshape(slab, modes, LANES), axis=1)
    kernel_head = kernel_head + jnp.where(iota((slab, LANES), 1) == 0, taps[9], 0.0)

    upper = iota((LANES, LANES), 1) >= iota((LANES, LANES), 0)
    for c in range(slab):
        line = jnp.broadcast_to(kernel_head[c : c + 1], (LANES, LANES))
        rolled = pltpu.roll(line, 0, 1, stride=1, stride_axis=0)
        high, low = split(jnp.where(upper, rolled, 0.0))
        toeplitz[0, c] = high
        toeplitz[1, c] = low

    eye = iota((wide, LANES), 0) == iota((wide, LANES), 1)
    step_row = iota((8, LANES), 0)
    steps = jnp.where(step_row == 6, 1, LANES * (1 << jnp.minimum(step_row, 5)))
    for g in range(groups):
        def row(part):
            piece = jnp.broadcast_to(part[g * wide : (g + 1) * wide], (wide, LANES))
            return jnp.sum(jnp.where(eye, piece, 0.0), axis=0, keepdims=True)

        rate_row = jnp.broadcast_to(row(rate), (8, LANES))
        seed_row = jnp.broadcast_to((row(seed) + 0.5).astype(jnp.int32), (8, LANES))
        weight_row = row(weight)
        re, im = power(rate_row, seed_row, steps)
        scale = jnp.where(step_row == 6, jnp.broadcast_to(weight_row, (8, LANES)), 1.0)
        state_rows[g, 0] = re * scale
        state_rows[g, 1] = im * scale

    diag[...] = jnp.zeros_like(diag)

    wait_bytes(tok, tok_sems.at[1])
    lane_c = iota((slab, LANES), 1)
    vocab_row = iota((vocab, LANES), 0)

    def one_hot(r):
        return jnp.where(vocab_row == tok[pl.ds(r, 1), :], 1.0, 0.0).astype(BF16)

    UNROLL = 4

    def gather(step, carry):
        last_one, last_two = carry
        r0 = step * UNROLL
        hot = jnp.concatenate([one_hot(r0 + i) for i in range(UNROLL)], axis=1)
        found = nn(table[...], hot)
        fresh = (r0 % chunks) == 0
        last_one = jnp.where(fresh, 0.0, last_one)
        last_two = jnp.where(fresh, 0.0, last_two)
        for i in range(UNROLL):
            x = found[:, i * LANES : (i + 1) * LANES]
            one = pltpu.roll(x, 1, 1)
            two = pltpu.roll(x, 2, 1)
            x1 = jnp.where(lane_c < 1, last_one, one)
            x2 = jnp.where(lane_c < 2, last_two, two)
            last_one, last_two = one, two
            q, k, v = (taps[3 * s] * x + taps[3 * s + 1] * x1 + taps[3 * s + 2] * x2 for s in range(3))
            at = pl.ds(pl.multiple_of((r0 + i) * slab, slab), slab)
            query[at, :] = q
            key[at, :] = k
            value[at, :] = v
            mix[at, :] = k * v
        return last_one, last_two

    zero = jnp.zeros((slab, LANES), F32)
    lax.fori_loop(0, rows // UNROLL, gather, (zero, zero))

    row_in_seq = iota((rows, LANES), 0) % chunks

    def scan(re, im, g, backward):
        for j in range(max(1, (chunks - 1).bit_length())):
            shift = 1 << j
            amount = rows - shift if backward else shift
            keep = row_in_seq < chunks - shift if backward else row_in_seq >= shift
            old_re = jnp.where(keep, pltpu.roll(re, amount, 0), 0.0)
            old_im = jnp.where(keep, pltpu.roll(im, amount, 0), 0.0)
            a, b = state_rows[g, 0, j : j + 1, :], state_rows[g, 1, j : j + 1, :]
            re, im = re + a * old_re - b * old_im, im + a * old_im + b * old_re
        amount = rows - 1 if backward else 1
        keep = row_in_seq < chunks - 1 if backward else row_in_seq >= 1
        re = jnp.where(keep, pltpu.roll(re, amount, 0), 0.0)
        im = jnp.where(keep, pltpu.roll(im, amount, 0), 0.0)
        a, b = state_rows[g, 0, 6:7, :], state_rows[g, 1, 6:7, :]
        return a * re - b * im, -(a * im + b * re)

    def long_conv(source, target, backward):
        enter, leave = (0, 2) if backward else (2, 0)

        def per_group(g, _):
            base = g * GROUP
            for side, first in enumerate((enter, leave)):
                for c in range(GROUP):
                    at = pl.ds(pl.multiple_of(g * wide + c * modes, modes), modes)
                    for half in range(2):
                        spot = slice(half * wide + c * modes, half * wide + (c + 1) * modes)
                        for part in range(2):
                            diag[side, part, spot, c * LANES : (c + 1) * LANES] = bank[
                                2 * (first + half) + part, at, :
                            ]
            local = jnp.zeros((rows, 2 * wide), F32)
            for c in range(GROUP):
                u = split(source[pl.ds(base + c, rows, stride=slab), :])
                at = slice(c * LANES, (c + 1) * LANES)
                local = local + three(nt, u, (diag[0, 0, :, at], diag[0, 1, :, at]))
            re, im = scan(local[:, :wide], local[:, wide:], g, backward)
            state = split(jnp.concatenate([re, im], axis=1))
            for c in range(GROUP):
                u = split(source[pl.ds(base + c, rows, stride=slab), :])
                at = slice(c * LANES, (c + 1) * LANES)
                band = (toeplitz[0, base + c], toeplitz[1, base + c])
                out = three(nt if backward else nn, u, band)
                out = out + three(nn, state, (diag[1, 0, :, at], diag[1, 1, :, at]))
                target[pl.ds(base + c, rows, stride=slab), :] = out
            return 0

        lax.fori_loop(0, groups, per_group, 0)

    long_conv(mix, long_out, False)

    def emit(i, _):
        r, where = device(i)
        at = slab_rows(r)
        mixed_out[at, :] = query[at, :] * long_out[at, :]
        pltpu.make_async_remote_copy(
            src_ref=mixed_out.at[at], dst_ref=mixer.at[slab_rows(me)],
            send_sem=mixer_sems.at[0], recv_sem=mixer_sems.at[1],
            device_id=where, device_id_type=MESH,
        ).start()
        return 0

    mixed_out[slab_rows(me), :] = query[slab_rows(me), :] * long_out[slab_rows(me), :]
    pltpu.make_async_copy(
        mixed_out.at[slab_rows(me)], mixer.at[slab_rows(me)], mixer_sems.at[1]
    ).start()
    lax.fori_loop(1, rows, emit, 0)
    wait_bytes(cot, cot_sems.at[1])

    def weigh(r, _):
        mix[slab_rows(r), :] = cot[slab_rows(r), :] * query[slab_rows(r), :]
        return 0

    lax.fori_loop(0, rows, weigh, 0, unroll=8)

    grad_mixed = query
    long_conv(mix, grad_mixed, True)

    def scatter(step, carry):
        next_one, next_two, total = carry
        r0 = rows - UNROLL - step * UNROLL
        fresh = (r0 % chunks) == chunks - UNROLL
        next_one = jnp.where(fresh, 0.0, next_one)
        next_two = jnp.where(fresh, 0.0, next_two)
        pieces = [None] * UNROLL
        for i in reversed(range(UNROLL)):
            at = pl.ds(pl.multiple_of((r0 + i) * slab, slab), slab)
            gm = grad_mixed[at, :]
            gq = cot[at, :] * long_out[at, :]
            gk = gm * value[at, :]
            gv = gm * key[at, :]
            zeroth, first, second = (taps[j] * gq + taps[3 + j] * gk + taps[6 + j] * gv for j in range(3))
            one = pltpu.roll(first, LANES - 1, 1)
            two = pltpu.roll(second, LANES - 2, 1)
            gx = (
                zeroth
                + jnp.where(lane_c >= LANES - 1, next_one, one)
                + jnp.where(lane_c >= LANES - 2, next_two, two)
            )
            next_one, next_two = one, two
            pieces[i] = jnp.concatenate(split(gx), axis=0)
        hot = jnp.concatenate([one_hot(r0 + i) for i in range(UNROLL)], axis=1)
        return next_one, next_two, total + nt(jnp.concatenate(pieces, axis=1), hot)

    _, _, total = lax.fori_loop(
        0, rows // UNROLL, scatter, (zero, zero, jnp.zeros((2 * slab, vocab), F32))
    )
    total = total[:slab] + total[slab:]
    for i in range(slab // 8):
        for j in range(vocab // LANES):
            table_grad[i * (vocab // LANES) + j] = total[i * 8 : (i + 1) * 8, j * LANES : (j + 1) * LANES]
    most = pl.ds(0, (rows - 1) * slab)
    wait_bytes(tok.at[pl.ds(0, rows - 1)], tok_sems.at[0])
    wait_bytes(cot.at[most], cot_sems.at[0])
    wait_bytes(mixed_out.at[most], mixer_sems.at[0])
    wait_bytes(mixer, mixer_sems.at[1])


def run_block(tok, embedding, conv_taps, gains, residues, decays, seeds, cot, chunks):
    modes, width = residues.shape
    vocab = embedding.shape[0]
    rows = width // (embedding.shape[1] // chunks)
    slab = width // rows
    tall = rows * slab
    vmem = pl.BlockSpec(memory_space=pltpu.VMEM)
    hbm = pl.BlockSpec(memory_space=pl.ANY)
    dma = pltpu.SemaphoreType.DMA
    return pl.pallas_call(
        functools.partial(block_kernel, chunks, chunks * LANES),
        out_shape=(
            jax.ShapeDtypeStruct((tall, LANES), F32),
            jax.ShapeDtypeStruct((slab * vocab // (8 * LANES), 8, LANES), F32),
        ),
        in_specs=[vmem, hbm, hbm, vmem, hbm, hbm, hbm, hbm],
        out_specs=(hbm, vmem),
        scratch_shapes=[pltpu.VMEM((tall, LANES), F32)] * 7
        + [
            pltpu.VMEM((rows, LANES), jnp.int32),
            pltpu.VMEM((slab, vocab), BF16),
            pltpu.VMEM((10, slab, LANES), F32),
            pltpu.VMEM((modes, LANES), F32),
            pltpu.VMEM((modes, LANES), F32),
            pltpu.VMEM((modes, LANES), jnp.int32),
            pltpu.VMEM((vocab, LANES), BF16),
            pltpu.VMEM((LANES, vocab), F32),
            pltpu.VMEM((3, 3, LANES), F32),
            pltpu.VMEM((8, slab * modes, LANES), BF16),
            pltpu.VMEM((2, slab, LANES, LANES), BF16),
            pltpu.VMEM((2, 2, 2 * GROUP * modes, GROUP * LANES), BF16),
            pltpu.VMEM((slab // GROUP, 2, 8, LANES), F32),
            dma((5,)), dma((2,)), dma((2,)), dma((2,)),
        ],
        compiler_params=pltpu.CompilerParams(
            vmem_limit_bytes=56 * 1024 * 1024, collective_id=0, has_side_effects=True
        ),
        name="hyena_block",
    )(tok, embedding, conv_taps, gains, residues, decays, seeds, cot)


AXES = ("z", "x", "y")


def spread_kernel(sides, parts, mine, every, own_sem, send_sems, recv_sems):
    ctx = lax.axis_index("ctx")
    fsdp = lax.axis_index("fsdp")
    spans = (sides[1] * sides[2], sides[2], 1)
    here = [lax.rem(ctx // span, side) for span, side in zip(spans, sides)]

    def device(axis, hop):
        there = lax.rem(here[axis] + hop + sides[axis], sides[axis])
        return (fsdp, ctx + (there - here[axis]) * spans[axis])

    def at(axis, hop, done, first, size):
        index = []
        for n in range(3):
            if n == axis:
                index.append(pl.ds(lax.rem(here[n] + hop + sides[n], sides[n]), 1))
            elif n in done:
                index.append(slice(None))
            else:
                index.append(pl.ds(here[n], 1))
        return every.at[(*index, pl.ds(first, size))]

    barrier = pltpu.get_barrier_semaphore()
    for axis in range(3):
        for hop in (1, -1, 2):
            pl.semaphore_signal(barrier, inc=1, device_id=device(axis, hop), device_id_type=MESH)
    own = pltpu.make_async_copy(mine, every.at[here[0], here[1], here[2]], own_sem)
    own.start()
    pl.semaphore_wait(barrier, 9)
    own.wait()

    sent = []

    def copy(part, phase, slot, source, where):
        made = pltpu.make_async_remote_copy(
            src_ref=source, dst_ref=source,
            send_sem=send_sems.at[part, phase, slot], recv_sem=recv_sems.at[part, phase, slot],
            device_id=where, device_id_type=MESH,
        )
        made.start()
        sent.append(made)

    def landed(part, phase, slot, place):
        pltpu.make_async_copy(place, place, recv_sems.at[part, phase, slot]).wait()

    for phase in range(3):
        plan = []
        for part, (first, size) in enumerate(parts):
            order = [(2 - part + n) % 3 for n in range(3)]
            axis, done = order[phase], order[:phase]
            plan.append((part, axis, done, first, size))
            block = at(axis, 0, done, first, size)
            copy(part, phase, 0, block, device(axis, 1))
            copy(part, phase, 1, block, device(axis, -1))
            if phase < 2:
                copy(part, phase, 2, block, device(axis, 2))
        for part, axis, done, first, size in plan:
            half = size // 2
            landed(part, phase, 0, at(axis, -1, done, first, size))
            if phase == 2:
                copy(part, phase, 2, at(axis, -1, done, first, half), device(axis, 1))
            landed(part, phase, 1, at(axis, 1, done, first, size))
            if phase == 2:
                copy(part, phase, 3, at(axis, 1, done, first + half, size - half), device(axis, -1))
        for part, axis, done, first, size in plan:
            half = size // 2
            if phase < 2:
                landed(part, phase, 2, at(axis, 2, done, first, size))
            else:
                landed(part, phase, 2, at(axis, 2, done, first, half))
                landed(part, phase, 3, at(axis, 2, done, first + half, size - half))
    for made in sent:
        made.wait_send()


def spread(block, chunks):
    side = round(chunks ** (1 / 3))
    tiles = block.shape[0]
    third = tiles // 3
    parts = ((0, third), (third, third), (2 * third, tiles - 2 * third))
    dma = pltpu.SemaphoreType.DMA
    return pl.pallas_call(
        functools.partial(spread_kernel, (side,) * 3, parts),
        out_shape=jax.ShapeDtypeStruct((side,) * 3 + block.shape, block.dtype),
        in_specs=[pl.BlockSpec(memory_space=pltpu.VMEM)],
        out_specs=pl.BlockSpec(memory_space=pltpu.VMEM),
        scratch_shapes=[dma, dma((3, 3, 4)), dma((3, 3, 4))],
        compiler_params=pltpu.CompilerParams(collective_id=1, has_side_effects=True),
        name="grad_spread",
    )(block)


def turn_kernel(tiles, out):
    per, count = tiles.shape[0], tiles.shape[1]
    across = out.shape[0] // LANES
    for j in range(across):
        rows = [tiles[s, i * across + j] for s in range(per) for i in range(count // across)]
        out[j * LANES : (j + 1) * LANES, :] = jnp.concatenate(rows, axis=0).T


def turn(every, vocab):
    sources, tiles = math.prod(every.shape[:3]), every.shape[3]
    slab = tiles * 8 * LANES // vocab
    per = LANES // slab
    return pl.pallas_call(
        turn_kernel,
        grid=(sources // per,),
        out_shape=jax.ShapeDtypeStruct((vocab, sources * slab), every.dtype),
        in_specs=[pl.BlockSpec((per, tiles, 8, LANES), lambda n: (n, 0, 0, 0))],
        out_specs=pl.BlockSpec((vocab, LANES), lambda n: (0, n)),
        name="grad_turn",
    )(every.reshape(sources, tiles, 8, LANES))


def body(token_ids, embedding, conv_taps, residues, decays, filter_seed, skip_gain, cotangent):
    ctx_size = lax.axis_size("ctx")
    width = conv_taps.shape[2]
    tok_block = token_ids.shape[1]
    mixer, grad = run_block(
        token_ids, embedding, conv_taps, skip_gain.reshape(-1, LANES),
        residues.T, decays.T, filter_seed.T, cotangent.reshape(width, tok_block), ctx_size,
    )
    grad = turn(spread(grad, ctx_size), embedding.shape[0])
    return mixer.reshape(cotangent.shape), grad


def solution(mesh):
    placed = (P("fsdp", "ctx"), P(None, "fsdp"), P(), P(), P(), P(), P(), P("fsdp", None, "ctx"))
    return jax.shard_map(
        body,
        mesh=mesh,
        in_specs=placed,
        out_specs=(P("fsdp", None, "ctx"), P(None, "fsdp")),
        check_vma=False,
    )
```

```python
import functools
import math

import jax
import jax.numpy as jnp
from jax import lax
from jax.experimental import pallas as pl
from jax.experimental.pallas import tpu as pltpu
from jax.sharding import PartitionSpec as P

PERIOD = 4096
F32 = jnp.float32
BF16 = jnp.bfloat16
LANES = 128
GROUP = 8


def iota(shape, dim):
    return lax.broadcasted_iota(jnp.int32, shape, dim)


def split(value):
    high = value.astype(BF16)
    return high, (value - high.astype(F32)).astype(BF16)


def cis(phase):
    quarter = PERIOD // 4
    turn = (phase + quarter // 2) // quarter
    a = (phase - turn * quarter).astype(F32) * (2.0 * math.pi / PERIOD)
    b = a * a
    s = a * (1.0 + b * (-1 / 6 + b * (1 / 120 + b * (-1 / 5040 + b * (1 / 362880)))))
    c = 1.0 + b * (-0.5 + b * (1 / 24 + b * (-1 / 720 + b * (1 / 40320))))
    odd = turn % 2 == 1
    re = jnp.where(odd, s, c)
    im = jnp.where(odd, c, s)
    re = jnp.where((turn == 1) | (turn == 2), -re, re)
    im = jnp.where((turn == 2) | (turn == 3), -im, im)
    return re, im


def power(rate, seed, steps):
    mag = jnp.exp(-rate * steps.astype(F32))
    re, im = cis((seed * steps) % PERIOD)
    return mag * re, mag * im


def nn(a, b):
    return jnp.dot(a, b, preferred_element_type=F32)


def nt(a, b):
    return lax.dot_general(a, b, (((1,), (1,)), ((), ())), preferred_element_type=F32)


def three(dot, left, right):
    left_high, left_low = left
    right_high, right_low = right
    rows = left_high.shape[0]
    both = dot(jnp.concatenate([left_high, left_low], axis=0), right_high)
    return both[:rows] + both[rows:] + dot(left_high, right_low)


MESH = pl.DeviceIdType.MESH


LEVELS = 32767.0


def gather_grad(total, chunks, quarters, columns_of, every, scales, turn_sems, send_sems, recv_sems):
    sides = every.shape[:3]
    ctx = lax.axis_index("ctx")
    fsdp = lax.axis_index("fsdp")
    spans = (sides[1] * sides[2], sides[2], 1)
    here = [lax.rem(ctx // span, side) for span, side in zip(spans, sides)]
    slab = total.shape[0]
    sent = []

    def neighbour(axis, hop):
        there = lax.rem(here[axis] + hop + sides[axis], sides[axis])
        return there, (fsdp, ctx + (there - here[axis]) * spans[axis])

    def send(source, target, sender, receiver, where):
        made = pltpu.make_async_remote_copy(
            src_ref=source, dst_ref=target, send_sem=sender, recv_sem=receiver,
            device_id=where, device_id_type=MESH,
        )
        made.start()
        sent.append(made)

    def landed(place, sem):
        pltpu.make_async_copy(place, place, sem).wait()

    for j in range(sides[2]):
        quarters[j] = total[:, j * LANES : (j + 1) * LANES]
    strip = pl.ds(pl.multiple_of(here[2] * slab, slab), slab)
    for n, hop in enumerate((1, -1, 2)):
        there, where = neighbour(2, hop)
        send(quarters.at[there], columns_of.at[strip], turn_sems.at[0, n], turn_sems.at[1, n], where)
    columns_of[strip, :] = quarters[here[2]]
    for n, hop in enumerate((-1, 1, 2)):
        there = neighbour(2, hop)[0]
        landed(columns_of.at[pl.ds(pl.multiple_of(there * slab, slab), slab)], turn_sems.at[1, n])
    block = columns_of[...].T
    peak = jnp.max(jnp.abs(block), axis=0, keepdims=True)
    block = jnp.round(block * (LEVELS / jnp.maximum(peak, 1e-30))).astype(jnp.int32).astype(jnp.int16)
    tiles = every.shape[3]
    every[here[0], here[1], here[2]] = block.reshape(tiles, LANES // tiles, LANES)
    scales[here[0], here[1], here[2]] = peak * (1.0 / LEVELS)

    def at(ref, axis, hop, done, *rest):
        index = []
        for n in range(3):
            if n == axis:
                index.append(pl.ds(lax.rem(here[n] + hop + sides[n], sides[n]), 1))
            elif n in done:
                index.append(slice(None))
            else:
                index.append(pl.ds(here[n], 1))
        return ref.at[(*index, *rest)]

    third = -(-tiles // 3)
    cuts = (0, third, 2 * third, tiles)
    for phase in range(3):
        plan = []
        for part in range(3):
            order = [(2 - part + n) % 3 for n in range(3)]
            axis, done = order[phase], order[:phase]
            first, size = cuts[part], cuts[part + 1] - cuts[part]
            half = size // 2
            whole, low, high = pl.ds(first, size), pl.ds(first, half), pl.ds(first + half, size - half)
            plan.append((part, axis, done, whole, low, high))
            right, left = neighbour(axis, 1)[1], neighbour(axis, -1)[1]
            mine = at(every, axis, 0, done, whole)
            sems = (send_sems.at[part, phase], recv_sems.at[part, phase])
            send(mine, mine, sems[0].at[0], sems[1].at[0], right)
            send(mine, mine, sems[0].at[1], sems[1].at[1], left)
            if phase < 2:
                send(mine, mine, sems[0].at[2], sems[1].at[2], neighbour(axis, 2)[1])
            if part == 2:
                level = at(scales, axis, 0, done)
                for n, hop in enumerate((1, -1, 2)):
                    send(level, level, sems[0].at[4 + n], sems[1].at[4 + n], neighbour(axis, hop)[1])
        for part, axis, done, whole, low, high in plan:
            sems = (send_sems.at[part, phase], recv_sems.at[part, phase])
            landed(at(every, axis, -1, done, whole), sems[1].at[0])
            if phase == 2:
                piece = at(every, axis, -1, done, low)
                send(piece, piece, sems[0].at[2], sems[1].at[2], neighbour(axis, 1)[1])
            landed(at(every, axis, 1, done, whole), sems[1].at[1])
            if phase == 2:
                piece = at(every, axis, 1, done, high)
                send(piece, piece, sems[0].at[3], sems[1].at[3], neighbour(axis, -1)[1])
        for part, axis, done, whole, low, high in plan:
            sem = recv_sems.at[part, phase]
            if phase < 2:
                landed(at(every, axis, 2, done, whole), sem.at[2])
            else:
                landed(at(every, axis, 2, done, low), sem.at[2])
                landed(at(every, axis, 2, done, high), sem.at[3])
            if part == 2:
                for n, hop in enumerate((-1, 1, 2)):
                    landed(at(scales, axis, hop, done), sem.at[4 + n])
    for made in sent:
        made.wait_send()


def block_kernel(
    chunks, seq_len,
    tok_mine, embedding, conv_taps, gains, residue_all, decay_all, seed_all, cot_mine,
    mixer, every, scales,
    query, key, value, mix, long_out, cot, mixed_out,
    tok, table, taps, residues, decays, seeds, raw_table, turned, raw_taps,
    bank, toeplitz, diag, state_rows, quarters, columns_of,
    load_sems, tok_sems, cot_sems, mixer_sems, turn_sems, send_sems, recv_sems,
):
    rows = tok.shape[0]
    slab = table.shape[0]
    vocab = table.shape[1]
    modes = residues.shape[0]
    groups = slab // GROUP
    wide = GROUP * modes
    ctx = lax.axis_index("ctx")
    me = lax.axis_index("fsdp") * chunks + ctx
    per_tile = LANES // slab

    def device(i):
        peer = lax.rem(me + i, rows)
        return peer, (peer // chunks, lax.rem(peer, chunks))

    def slab_rows(index):
        return pl.ds(pl.multiple_of(index * slab, slab), slab)

    barrier = pltpu.get_barrier_semaphore()

    @pl.loop(1, rows)
    def _(i):
        pl.semaphore_signal(barrier, inc=1, device_id=device(i)[1], device_id_type=MESH)

    lane_tile = pl.ds(pl.multiple_of(ctx // per_tile * LANES, LANES), LANES)
    wide_tile = pl.ds(pl.multiple_of(me // per_tile * LANES, LANES), LANES)
    loads = [
        pltpu.make_async_copy(source, target, load_sems.at[n])
        for n, (source, target) in enumerate((
            (residue_all.at[:, wide_tile], residues),
            (decay_all.at[:, wide_tile], decays),
            (seed_all.at[:, wide_tile], seeds),
            (conv_taps.at[:, :, wide_tile], raw_taps),
            (embedding.at[:, lane_tile], raw_table),
        ))
    ]
    for load in loads:
        load.start()
    pl.semaphore_wait(barrier, rows - 1)

    own_tok = pltpu.make_async_copy(tok_mine, tok.at[pl.ds(me, 1)], tok_sems.at[1])
    own_tok.start()

    @pl.loop(1, rows)
    def _(i):
        pltpu.make_async_remote_copy(
            src_ref=tok_mine, dst_ref=tok.at[pl.ds(me, 1)],
            send_sem=tok_sems.at[0], recv_sem=tok_sems.at[1],
            device_id=device(i)[1], device_id_type=MESH,
        ).start()

    own_cot = pltpu.make_async_copy(cot_mine.at[slab_rows(me)], cot.at[slab_rows(me)], cot_sems.at[1])
    own_cot.start()

    @pl.loop(1, rows)
    def _(i):
        peer, where = device(i)
        pltpu.make_async_remote_copy(
            src_ref=cot_mine.at[slab_rows(peer)], dst_ref=cot.at[slab_rows(me)],
            send_sem=cot_sems.at[0], recv_sem=cot_sems.at[1],
            device_id=where, device_id_type=MESH,
        ).start()

    def wait_bytes(ref, sem):
        pltpu.make_async_copy(ref, ref, sem).wait()

    for load in loads:
        load.wait()
    sub = pl.ds(pl.multiple_of(lax.rem(ctx, per_tile) * slab, slab), slab)
    turned[...] = raw_table[...].astype(F32).T
    table[...] = turned[sub, :].astype(BF16)
    pieces = [residues[...], decays[...], seeds[...].astype(F32)]
    pieces += [raw_taps[s, j : j + 1, :] for s in range(3) for j in range(3)]
    pieces.append(gains[pl.ds(me // per_tile, 1), :])
    pieces.append(jnp.zeros((LANES - 10 - 3 * modes, LANES), F32))
    turned[:, :LANES] = jnp.concatenate(pieces, axis=0).T
    columns = turned[sub, :LANES]
    for j in range(10):
        taps[j] = jnp.broadcast_to(columns[:, 3 * modes + j : 3 * modes + j + 1], (slab, LANES))

    spread = (iota((slab * modes, slab), 0) // modes == iota((slab * modes, slab), 1)).astype(F32)
    pick = iota((slab * modes, modes), 0) % modes == iota((slab * modes, modes), 1)

    def column(part):
        wide_part = jnp.dot(spread, part, precision=lax.Precision.HIGHEST, preferred_element_type=F32)
        return jnp.sum(jnp.where(pick, wide_part, 0.0), axis=1, keepdims=True)

    rate = column(columns[:, modes : 2 * modes])
    seed = column(columns[:, 2 * modes : 3 * modes])
    res = column(columns[:, :modes])
    weight = res * jnp.sqrt(rate + 1.0 / seq_len)
    seed_int = (seed + 0.5).astype(jnp.int32)
    rate_b = jnp.broadcast_to(rate, (slab * modes, LANES))
    seed_b = jnp.broadcast_to(seed_int, (slab * modes, LANES))
    lane = iota((slab * modes, LANES), 1)
    up = power(rate_b, seed_b, lane)
    down = power(rate_b, seed_b, LANES - 1 - lane)
    for place, part in enumerate((*up, *down)):
        high, low = split(part)
        bank[2 * place] = high
        bank[2 * place + 1] = low
    kernel_head = jnp.sum((up[0] * weight).reshape(slab, modes, LANES), axis=1)
    kernel_head = kernel_head + jnp.where(iota((slab, LANES), 1) == 0, taps[9], 0.0)

    upper = iota((LANES, LANES), 1) >= iota((LANES, LANES), 0)
    for c in range(slab):
        line = jnp.broadcast_to(kernel_head[c : c + 1], (LANES, LANES))
        rolled = pltpu.roll(line, 0, 1, stride=1, stride_axis=0)
        high, low = split(jnp.where(upper, rolled, 0.0))
        toeplitz[0, c] = high
        toeplitz[1, c] = low

    eye = iota((wide, LANES), 0) == iota((wide, LANES), 1)
    step_row = iota((8, LANES), 0)
    steps = jnp.where(step_row == 6, 1, LANES * (1 << jnp.minimum(step_row, 5)))
    for g in range(groups):
        def row(part):
            piece = jnp.broadcast_to(part[g * wide : (g + 1) * wide], (wide, LANES))
            return jnp.sum(jnp.where(eye, piece, 0.0), axis=0, keepdims=True)

        rate_row = jnp.broadcast_to(row(rate), (8, LANES))
        seed_row = jnp.broadcast_to((row(seed) + 0.5).astype(jnp.int32), (8, LANES))
        weight_row = row(weight)
        re, im = power(rate_row, seed_row, steps)
        scale = jnp.where(step_row == 6, jnp.broadcast_to(weight_row, (8, LANES)), 1.0)
        state_rows[g, 0] = re * scale
        state_rows[g, 1] = im * scale

    diag[...] = jnp.zeros_like(diag)

    wait_bytes(tok, tok_sems.at[1])
    lane_c = iota((slab, LANES), 1)
    vocab_row = iota((vocab, LANES), 0)

    def one_hot(r):
        return jnp.where(vocab_row == tok[pl.ds(r, 1), :], 1.0, 0.0).astype(BF16)

    UNROLL = 4

    def gather(step, carry):
        last_one, last_two = carry
        r0 = step * UNROLL
        hot = jnp.concatenate([one_hot(r0 + i) for i in range(UNROLL)], axis=1)
        found = nn(table[...], hot)
        fresh = (r0 % chunks) == 0
        last_one = jnp.where(fresh, 0.0, last_one)
        last_two = jnp.where(fresh, 0.0, last_two)
        for i in range(UNROLL):
            x = found[:, i * LANES : (i + 1) * LANES]
            one = pltpu.roll(x, 1, 1)
            two = pltpu.roll(x, 2, 1)
            x1 = jnp.where(lane_c < 1, last_one, one)
            x2 = jnp.where(lane_c < 2, last_two, two)
            last_one, last_two = one, two
            q, k, v = (taps[3 * s] * x + taps[3 * s + 1] * x1 + taps[3 * s + 2] * x2 for s in range(3))
            at = pl.ds(pl.multiple_of((r0 + i) * slab, slab), slab)
            query[at, :] = q
            key[at, :] = k
            value[at, :] = v
            mix[at, :] = k * v
        return last_one, last_two

    zero = jnp.zeros((slab, LANES), F32)
    lax.fori_loop(0, rows // UNROLL, gather, (zero, zero))

    row_in_seq = iota((rows, LANES), 0) % chunks

    def scan(re, im, g, backward):
        for j in range(max(1, (chunks - 1).bit_length())):
            shift = 1 << j
            amount = rows - shift if backward else shift
            keep = row_in_seq < chunks - shift if backward else row_in_seq >= shift
            old_re = jnp.where(keep, pltpu.roll(re, amount, 0), 0.0)
            old_im = jnp.where(keep, pltpu.roll(im, amount, 0), 0.0)
            a, b = state_rows[g, 0, j : j + 1, :], state_rows[g, 1, j : j + 1, :]
            re, im = re + a * old_re - b * old_im, im + a * old_im + b * old_re
        amount = rows - 1 if backward else 1
        keep = row_in_seq < chunks - 1 if backward else row_in_seq >= 1
        re = jnp.where(keep, pltpu.roll(re, amount, 0), 0.0)
        im = jnp.where(keep, pltpu.roll(im, amount, 0), 0.0)
        a, b = state_rows[g, 0, 6:7, :], state_rows[g, 1, 6:7, :]
        return a * re - b * im, -(a * im + b * re)

    def long_conv(source, target, backward):
        enter, leave = (0, 2) if backward else (2, 0)

        def per_group(g, _):
            base = g * GROUP
            for side, first in enumerate((enter, leave)):
                for c in range(GROUP):
                    at = pl.ds(pl.multiple_of(g * wide + c * modes, modes), modes)
                    for half in range(2):
                        spot = slice(half * wide + c * modes, half * wide + (c + 1) * modes)
                        for part in range(2):
                            diag[side, part, spot, c * LANES : (c + 1) * LANES] = bank[
                                2 * (first + half) + part, at, :
                            ]
            local = jnp.zeros((rows, 2 * wide), F32)
            for c in range(GROUP):
                u = split(source[pl.ds(base + c, rows, stride=slab), :])
                at = slice(c * LANES, (c + 1) * LANES)
                local = local + three(nt, u, (diag[0, 0, :, at], diag[0, 1, :, at]))
            re, im = scan(local[:, :wide], local[:, wide:], g, backward)
            state = split(jnp.concatenate([re, im], axis=1))
            for c in range(GROUP):
                u = split(source[pl.ds(base + c, rows, stride=slab), :])
                at = slice(c * LANES, (c + 1) * LANES)
                band = (toeplitz[0, base + c], toeplitz[1, base + c])
                out = three(nt if backward else nn, u, band)
                out = out + three(nn, state, (diag[1, 0, :, at], diag[1, 1, :, at]))
                target[pl.ds(base + c, rows, stride=slab), :] = out
            return 0

        lax.fori_loop(0, groups, per_group, 0)

    long_conv(mix, long_out, False)

    def emit(i, _):
        r, where = device(i)
        at = slab_rows(r)
        mixed_out[at, :] = query[at, :] * long_out[at, :]
        pltpu.make_async_remote_copy(
            src_ref=mixed_out.at[at], dst_ref=mixer.at[slab_rows(me)],
            send_sem=mixer_sems.at[0], recv_sem=mixer_sems.at[1],
            device_id=where, device_id_type=MESH,
        ).start()
        return 0

    mixed_out[slab_rows(me), :] = query[slab_rows(me), :] * long_out[slab_rows(me), :]
    pltpu.make_async_copy(
        mixed_out.at[slab_rows(me)], mixer.at[slab_rows(me)], mixer_sems.at[1]
    ).start()
    lax.fori_loop(1, rows, emit, 0)
    wait_bytes(cot, cot_sems.at[1])

    def weigh(r, _):
        mix[slab_rows(r), :] = cot[slab_rows(r), :] * query[slab_rows(r), :]
        return 0

    lax.fori_loop(0, rows, weigh, 0, unroll=8)

    grad_mixed = query
    long_conv(mix, grad_mixed, True)

    def scatter(step, carry):
        next_one, next_two, total = carry
        r0 = rows - UNROLL - step * UNROLL
        fresh = (r0 % chunks) == chunks - UNROLL
        next_one = jnp.where(fresh, 0.0, next_one)
        next_two = jnp.where(fresh, 0.0, next_two)
        pieces = [None] * UNROLL
        for i in reversed(range(UNROLL)):
            at = pl.ds(pl.multiple_of((r0 + i) * slab, slab), slab)
            gm = grad_mixed[at, :]
            gq = cot[at, :] * long_out[at, :]
            gk = gm * value[at, :]
            gv = gm * key[at, :]
            zeroth, first, second = (taps[j] * gq + taps[3 + j] * gk + taps[6 + j] * gv for j in range(3))
            one = pltpu.roll(first, LANES - 1, 1)
            two = pltpu.roll(second, LANES - 2, 1)
            gx = (
                zeroth
                + jnp.where(lane_c >= LANES - 1, next_one, one)
                + jnp.where(lane_c >= LANES - 2, next_two, two)
            )
            next_one, next_two = one, two
            pieces[i] = jnp.concatenate(split(gx), axis=0)
        hot = jnp.concatenate([one_hot(r0 + i) for i in range(UNROLL)], axis=1)
        return next_one, next_two, total + nt(jnp.concatenate(pieces, axis=1), hot)

    _, _, total = lax.fori_loop(
        0, rows // UNROLL, scatter, (zero, zero, jnp.zeros((2 * slab, vocab), F32))
    )
    gather_grad(
        total[:slab] + total[slab:], chunks, quarters, columns_of, every, scales,
        turn_sems, send_sems, recv_sems,
    )
    most = pl.ds(0, (rows - 1) * slab)
    wait_bytes(tok.at[pl.ds(0, rows - 1)], tok_sems.at[0])
    wait_bytes(cot.at[most], cot_sems.at[0])
    wait_bytes(mixed_out.at[most], mixer_sems.at[0])
    wait_bytes(mixer, mixer_sems.at[1])


def run_block(tok, embedding, conv_taps, gains, residues, decays, seeds, cot, chunks):
    modes, width = residues.shape
    vocab = embedding.shape[0]
    rows = width // (embedding.shape[1] // chunks)
    slab = width // rows
    tall = rows * slab
    side = round(chunks ** (1 / 3))
    vmem = pl.BlockSpec(memory_space=pltpu.VMEM)
    hbm = pl.BlockSpec(memory_space=pl.ANY)
    dma = pltpu.SemaphoreType.DMA
    return pl.pallas_call(
        functools.partial(block_kernel, chunks, chunks * LANES),
        out_shape=(
            jax.ShapeDtypeStruct((tall, LANES), F32),
            jax.ShapeDtypeStruct((side,) * 3 + (8, LANES // 8, LANES), jnp.int16),
            jax.ShapeDtypeStruct((side,) * 3 + (1, LANES), F32),
        ),
        in_specs=[vmem, hbm, hbm, vmem, hbm, hbm, hbm, hbm],
        out_specs=(hbm, vmem, vmem),
        scratch_shapes=[pltpu.VMEM((tall, LANES), F32)] * 7
        + [
            pltpu.VMEM((rows, LANES), jnp.int32),
            pltpu.VMEM((slab, vocab), BF16),
            pltpu.VMEM((10, slab, LANES), F32),
            pltpu.VMEM((modes, LANES), F32),
            pltpu.VMEM((modes, LANES), F32),
            pltpu.VMEM((modes, LANES), jnp.int32),
            pltpu.VMEM((vocab, LANES), BF16),
            pltpu.VMEM((LANES, vocab), F32),
            pltpu.VMEM((3, 3, LANES), F32),
            pltpu.VMEM((8, slab * modes, LANES), BF16),
            pltpu.VMEM((2, slab, LANES, LANES), BF16),
            pltpu.VMEM((2, 2, 2 * GROUP * modes, GROUP * LANES), BF16),
            pltpu.VMEM((slab // GROUP, 2, 8, LANES), F32),
            pltpu.VMEM((side, slab, LANES), F32),
            pltpu.VMEM((LANES, LANES), F32),
            dma((5,)), dma((2,)), dma((2,)), dma((2,)), dma((2, 3)), dma((3, 3, 7)), dma((3, 3, 7)),
        ],
        compiler_params=pltpu.CompilerParams(
            vmem_limit_bytes=56 * 1024 * 1024, collective_id=0, has_side_effects=True
        ),
        name="hyena_block",
    )(tok, embedding, conv_taps, gains, residues, decays, seeds, cot)


def finish_kernel(every, scales, out):
    for z in range(every.shape[0]):
        for x in range(every.shape[1]):
            n = z * every.shape[1] + x
            values = every[z, x, 0].reshape(LANES, LANES).astype(jnp.int32).astype(F32)
            out[:, n * LANES : (n + 1) * LANES] = values * scales[z, x, 0]


def finish(every, scales):
    a, b, c, tiles = every.shape[:4]
    return pl.pallas_call(
        finish_kernel,
        grid=(c,),
        out_shape=jax.ShapeDtypeStruct((c * LANES, a * b * LANES), F32),
        in_specs=[
            pl.BlockSpec((a, b, 1, *every.shape[3:]), lambda n: (0, 0, n, 0, 0, 0)),
            pl.BlockSpec((a, b, 1, 1, LANES), lambda n: (0, 0, n, 0, 0)),
        ],
        out_specs=pl.BlockSpec((LANES, a * b * LANES), lambda n: (n, 0)),
        name="grad_finish",
    )(every, scales)


def body(token_ids, embedding, conv_taps, residues, decays, filter_seed, skip_gain, cotangent):
    ctx_size = lax.axis_size("ctx")
    width = conv_taps.shape[2]
    tok_block = token_ids.shape[1]
    mixer, every, scales = run_block(
        token_ids, embedding, conv_taps, skip_gain.reshape(-1, LANES),
        residues.T, decays.T, filter_seed.T, cotangent.reshape(width, tok_block), ctx_size,
    )
    return mixer.reshape(cotangent.shape), finish(every, scales)


def solution(mesh):
    placed = (P("fsdp", "ctx"), P(None, "fsdp"), P(), P(), P(), P(), P(), P("fsdp", None, "ctx"))
    return jax.shard_map(
        body,
        mesh=mesh,
        in_specs=placed,
        out_specs=(P("fsdp", None, "ctx"), P(None, "fsdp")),
        check_vma=False,
    )
```

```python
import functools
import math

import jax
import jax.numpy as jnp
from jax import lax
from jax.experimental import pallas as pl
from jax.experimental.pallas import tpu as pltpu
from jax.sharding import PartitionSpec as P

PERIOD = 4096
F32 = jnp.float32
BF16 = jnp.bfloat16
LANES = 128
GROUP = 8


def iota(shape, dim):
    return lax.broadcasted_iota(jnp.int32, shape, dim)


def split(value):
    high = value.astype(BF16)
    return high, (value - high.astype(F32)).astype(BF16)


def cis(phase):
    quarter = PERIOD // 4
    turn = (phase + quarter // 2) // quarter
    a = (phase - turn * quarter).astype(F32) * (2.0 * math.pi / PERIOD)
    b = a * a
    s = a * (1.0 + b * (-1 / 6 + b * (1 / 120 + b * (-1 / 5040 + b * (1 / 362880)))))
    c = 1.0 + b * (-0.5 + b * (1 / 24 + b * (-1 / 720 + b * (1 / 40320))))
    odd = turn % 2 == 1
    re = jnp.where(odd, s, c)
    im = jnp.where(odd, c, s)
    re = jnp.where((turn == 1) | (turn == 2), -re, re)
    im = jnp.where((turn == 2) | (turn == 3), -im, im)
    return re, im


def power(rate, seed, steps):
    mag = jnp.exp(-rate * steps.astype(F32))
    re, im = cis((seed * steps) % PERIOD)
    return mag * re, mag * im


def nn(a, b):
    return jnp.dot(a, b, preferred_element_type=F32)


def nt(a, b):
    return lax.dot_general(a, b, (((1,), (1,)), ((), ())), preferred_element_type=F32)


def three(dot, left, right):
    left_high, left_low = left
    right_high, right_low = right
    rows = left_high.shape[0]
    both = dot(jnp.concatenate([left_high, left_low], axis=0), right_high)
    return both[:rows] + both[rows:] + dot(left_high, right_low)


MESH = pl.DeviceIdType.MESH


LEVELS = 32767.0


def gather_grad(pieces, chunks, quarters, columns_of, every, scales, turn_sems, send_sems, recv_sems):
    sides = every.shape[:3]
    ctx = lax.axis_index("ctx")
    fsdp = lax.axis_index("fsdp")
    spans = (sides[1] * sides[2], sides[2], 1)
    here = [lax.rem(ctx // span, side) for span, side in zip(spans, sides)]
    slab = pieces[0].shape[0]
    sent = []

    def neighbour(axis, hop):
        there = lax.rem(here[axis] + hop + sides[axis], sides[axis])
        return there, (fsdp, ctx + (there - here[axis]) * spans[axis])

    def send(source, target, sender, receiver, where):
        made = pltpu.make_async_remote_copy(
            src_ref=source, dst_ref=target, send_sem=sender, recv_sem=receiver,
            device_id=where, device_id_type=MESH,
        )
        made.start()
        sent.append(made)

    def landed(place, sem):
        pltpu.make_async_copy(place, place, sem).wait()

    for j in range(sides[2]):
        quarters[j] = pieces[j]
    strip = pl.ds(pl.multiple_of(here[2] * slab, slab), slab)
    for n, hop in enumerate((1, -1, 2)):
        there, where = neighbour(2, hop)
        send(quarters.at[there], columns_of.at[strip], turn_sems.at[0, n], turn_sems.at[1, n], where)
    columns_of[strip, :] = quarters[here[2]]
    for n, hop in enumerate((-1, 1, 2)):
        there = neighbour(2, hop)[0]
        landed(columns_of.at[pl.ds(pl.multiple_of(there * slab, slab), slab)], turn_sems.at[1, n])
    block = columns_of[...].T
    peak = jnp.max(jnp.abs(block), axis=0, keepdims=True)
    block = jnp.round(block * (LEVELS / jnp.maximum(peak, 1e-30))).astype(jnp.int32).astype(jnp.int16)
    tiles = every.shape[3]
    every[here[0], here[1], here[2]] = block.reshape(tiles, LANES // tiles, LANES)
    scales[here[0], here[1], here[2]] = peak * (1.0 / LEVELS)

    def at(ref, axis, hop, done, *rest):
        index = []
        for n in range(3):
            if n == axis:
                index.append(pl.ds(lax.rem(here[n] + hop + sides[n], sides[n]), 1))
            elif n in done:
                index.append(slice(None))
            else:
                index.append(pl.ds(here[n], 1))
        return ref.at[(*index, *rest)]

    third = -(-tiles // 3)
    cuts = (0, third, 2 * third, tiles)
    for phase in range(3):
        plan = []
        for part in range(3):
            order = [(2 - part + n) % 3 for n in range(3)]
            axis, done = order[phase], order[:phase]
            first, size = cuts[part], cuts[part + 1] - cuts[part]
            half = size // 2
            whole, low, high = pl.ds(first, size), pl.ds(first, half), pl.ds(first + half, size - half)
            plan.append((part, axis, done, whole, low, high))
            right, left = neighbour(axis, 1)[1], neighbour(axis, -1)[1]
            mine = at(every, axis, 0, done, whole)
            sems = (send_sems.at[part, phase], recv_sems.at[part, phase])
            send(mine, mine, sems[0].at[0], sems[1].at[0], right)
            send(mine, mine, sems[0].at[1], sems[1].at[1], left)
            if phase < 2:
                send(mine, mine, sems[0].at[2], sems[1].at[2], neighbour(axis, 2)[1])
            if part == 2:
                level = at(scales, axis, 0, done)
                for n, hop in enumerate((1, -1, 2)):
                    send(level, level, sems[0].at[4 + n], sems[1].at[4 + n], neighbour(axis, hop)[1])
        for part, axis, done, whole, low, high in plan:
            sems = (send_sems.at[part, phase], recv_sems.at[part, phase])
            landed(at(every, axis, -1, done, whole), sems[1].at[0])
            if phase == 2:
                piece = at(every, axis, -1, done, low)
                send(piece, piece, sems[0].at[2], sems[1].at[2], neighbour(axis, 1)[1])
            landed(at(every, axis, 1, done, whole), sems[1].at[1])
            if phase == 2:
                piece = at(every, axis, 1, done, high)
                send(piece, piece, sems[0].at[3], sems[1].at[3], neighbour(axis, -1)[1])
        for part, axis, done, whole, low, high in plan:
            sem = recv_sems.at[part, phase]
            if phase < 2:
                landed(at(every, axis, 2, done, whole), sem.at[2])
            else:
                landed(at(every, axis, 2, done, low), sem.at[2])
                landed(at(every, axis, 2, done, high), sem.at[3])
            if part == 2:
                for n, hop in enumerate((-1, 1, 2)):
                    landed(at(scales, axis, hop, done), sem.at[4 + n])
    for made in sent:
        made.wait_send()


def block_kernel(
    chunks, seq_len,
    tok_mine, embedding, conv_taps, gains, residue_all, decay_all, seed_all, cot_mine,
    mixer, mixer_scale, every, scales,
    query, key, value, mix, long_out, cot, cot_out, cot_in, mixed_out, level_out, head_out, head_in,
    staged, table, taps, residues, decays, seeds, raw_table, turned, raw_taps,
    bank, toeplitz, diag, state_rows, quarters, columns_of,
    load_sems, head_sems, cot_sems, mixer_sems, level_sems, turn_sems, send_sems, recv_sems,
):
    vocab = embedding.shape[0]
    rows = head_in.shape[0] // 2
    slab = cot.shape[0] // rows
    modes = residues.shape[0]
    groups = slab // GROUP
    wide = GROUP * modes
    ctx = lax.axis_index("ctx")
    fsdp = lax.axis_index("fsdp")
    me = fsdp * chunks + ctx
    per_tile = LANES // slab

    def slab_rows(index):
        return pl.ds(pl.multiple_of(index * slab, slab), slab)

    def pair(index):
        return pl.ds(pl.multiple_of(2 * index, 2), 2)

    def each_peer(action):
        action((1 - fsdp) * chunks + ctx, (1 - fsdp, ctx))

        def step(i, _):
            there = ctx + i
            there = jnp.where(there >= chunks, there - chunks, there)
            for side in (fsdp, 1 - fsdp):
                action(side * chunks + there, (side, there))
            return 0

        lax.fori_loop(1, chunks, step, 0, unroll=7)

    def send(source, target, sems, where):
        pltpu.make_async_remote_copy(
            src_ref=source, dst_ref=target, send_sem=sems.at[0], recv_sem=sems.at[1],
            device_id=where, device_id_type=MESH,
        ).start()

    barrier = pltpu.get_barrier_semaphore()
    load_cot = pltpu.make_async_copy(cot_mine, cot, load_sems.at[5])
    load_cot.start()
    each_peer(lambda place, where: pl.semaphore_signal(barrier, inc=1, device_id=where, device_id_type=MESH))

    lane_tile = pl.ds(pl.multiple_of(ctx // per_tile * LANES, LANES), LANES)
    wide_tile = pl.ds(pl.multiple_of(me // per_tile * LANES, LANES), LANES)
    loads = [
        pltpu.make_async_copy(source, target, load_sems.at[n])
        for n, (source, target) in enumerate((
            (residue_all.at[:, wide_tile], residues),
            (decay_all.at[:, wide_tile], decays),
            (seed_all.at[:, wide_tile], seeds),
            (conv_taps.at[:, :, wide_tile], raw_taps),
            (embedding.at[:, lane_tile], raw_table),
        ))
    ]
    for load in loads:
        load.start()

    def fixed(block):
        peak = jnp.maximum(jnp.max(jnp.abs(block), axis=0, keepdims=True), 1e-30)
        code = jnp.round(block * (LEVELS / peak)).astype(jnp.int32).astype(jnp.int16)
        return code, peak * (1.0 / LEVELS)

    def real(code, level):
        return code.astype(jnp.int32).astype(F32) * level

    load_cot.wait()
    tokens = tok_mine[...].astype(F32)

    def encode(step, _):
        heads = []
        for i in range(16):
            r = step * 16 + i
            code, level = fixed(cot[slab_rows(r), :])
            cot_out[slab_rows(r), :] = code
            heads += [tokens, level]
        head_out[pl.ds(pl.multiple_of(step * 32, 32), 32), :] = jnp.concatenate(heads, axis=0)
        return 0

    lax.fori_loop(0, rows // 16, encode, 0)
    pl.semaphore_wait(barrier, rows - 1)
    each_peer(lambda place, where: send(head_out.at[pair(place)], head_in.at[pair(me)], head_sems, where))
    each_peer(lambda place, where: send(cot_out.at[slab_rows(place)], cot_in.at[slab_rows(me)], cot_sems, where))
    head_in[pair(me), :] = head_out[pair(me), :]
    cot_in[slab_rows(me), :] = cot_out[slab_rows(me), :]

    def wait_bytes(ref, sem):
        pltpu.make_async_copy(ref, ref, sem).wait()

    for load in loads:
        load.wait()
    sub = pl.ds(pl.multiple_of(lax.rem(ctx, per_tile) * slab, slab), slab)
    turned[...] = raw_table[...].astype(F32).T
    for b in range(vocab // LANES):
        table[b * slab : (b + 1) * slab, :] = turned[sub, b * LANES : (b + 1) * LANES].astype(BF16)
    pieces = [residues[...], decays[...], seeds[...].astype(F32)]
    pieces += [raw_taps[s, j : j + 1, :] for s in range(3) for j in range(3)]
    pieces.append(gains[pl.ds(me // per_tile, 1), :])
    pieces.append(jnp.zeros((LANES - 10 - 3 * modes, LANES), F32))
    turned[:, :LANES] = jnp.concatenate(pieces, axis=0).T
    columns = turned[sub, :LANES]
    for j in range(10):
        taps[j] = jnp.broadcast_to(columns[:, 3 * modes + j : 3 * modes + j + 1], (slab, LANES))

    spread = (iota((slab * modes, slab), 0) // modes == iota((slab * modes, slab), 1)).astype(F32)
    pick = iota((slab * modes, modes), 0) % modes == iota((slab * modes, modes), 1)

    def column(part):
        wide_part = jnp.dot(spread, part, precision=lax.Precision.HIGHEST, preferred_element_type=F32)
        return jnp.sum(jnp.where(pick, wide_part, 0.0), axis=1, keepdims=True)

    rate = column(columns[:, modes : 2 * modes])
    seed = column(columns[:, 2 * modes : 3 * modes])
    res = column(columns[:, :modes])
    weight = res * jnp.sqrt(rate + 1.0 / seq_len)
    seed_int = (seed + 0.5).astype(jnp.int32)
    rate_b = jnp.broadcast_to(rate, (slab * modes, LANES))
    seed_b = jnp.broadcast_to(seed_int, (slab * modes, LANES))
    lane = iota((slab * modes, LANES), 1)
    up = power(rate_b, seed_b, lane)
    down = power(rate_b, seed_b, LANES - 1 - lane)
    for place, part in enumerate((*up, *down)):
        high, low = split(part)
        bank[2 * place] = high
        bank[2 * place + 1] = low
    kernel_head = jnp.sum((up[0] * weight).reshape(slab, modes, LANES), axis=1)
    kernel_head = kernel_head + jnp.where(iota((slab, LANES), 1) == 0, taps[9], 0.0)

    upper = iota((LANES, LANES), 1) >= iota((LANES, LANES), 0)
    for c in range(slab):
        line = jnp.broadcast_to(kernel_head[c : c + 1], (LANES, LANES))
        rolled = pltpu.roll(line, 0, 1, stride=1, stride_axis=0)
        high, low = split(jnp.where(upper, rolled, 0.0))
        toeplitz[0, c] = high
        toeplitz[1, c] = low

    eye = iota((wide, LANES), 0) == iota((wide, LANES), 1)
    step_row = iota((8, LANES), 0)
    steps = jnp.where(step_row == 6, 1, LANES * (1 << jnp.minimum(step_row, 5)))
    for g in range(groups):
        def row(part):
            piece = jnp.broadcast_to(part[g * wide : (g + 1) * wide], (wide, LANES))
            return jnp.sum(jnp.where(eye, piece, 0.0), axis=0, keepdims=True)

        rate_row = jnp.broadcast_to(row(rate), (8, LANES))
        seed_row = jnp.broadcast_to((row(seed) + 0.5).astype(jnp.int32), (8, LANES))
        weight_row = row(weight)
        re, im = power(rate_row, seed_row, steps)
        scale = jnp.where(step_row == 6, jnp.broadcast_to(weight_row, (8, LANES)), 1.0)
        state_rows[g, 0] = re * scale
        state_rows[g, 1] = im * scale

    diag[...] = jnp.zeros_like(diag)

    wait_bytes(head_in.at[pl.ds(0, 2 * (rows - 1))], head_sems.at[1])
    lane_c = iota((slab, LANES), 1)
    low_row = iota((LANES, LANES), 0)
    banks = vocab // LANES

    def token_parts(r):
        token = (head_in[pl.ds(2 * r, 1), :] + 0.5).astype(jnp.int32)
        bank_of = token // LANES
        hot = jnp.where(low_row == token - bank_of * LANES, 1.0, 0.0).astype(BF16)
        return hot, bank_of

    UNROLL = 16

    def gather(step, carry):
        last_one, last_two = carry
        r0 = step * UNROLL
        parts = [token_parts(r0 + i) for i in range(UNROLL)]
        found = nn(table[...], jnp.concatenate([hot for hot, _ in parts], axis=1))
        fresh = (r0 % chunks) == 0
        last_one = jnp.where(fresh, 0.0, last_one)
        last_two = jnp.where(fresh, 0.0, last_two)
        for i in range(UNROLL):
            bank_of = parts[i][1]
            x = found[:slab, i * LANES : (i + 1) * LANES]
            for b in range(1, banks):
                x = jnp.where(bank_of == b, found[b * slab : (b + 1) * slab, i * LANES : (i + 1) * LANES], x)
            one = pltpu.roll(x, 1, 1)
            two = pltpu.roll(x, 2, 1)
            x1 = jnp.where(lane_c < 1, last_one, one)
            x2 = jnp.where(lane_c < 2, last_two, two)
            last_one, last_two = one, two
            q, k, v = (taps[3 * s] * x + taps[3 * s + 1] * x1 + taps[3 * s + 2] * x2 for s in range(3))
            at = pl.ds(pl.multiple_of((r0 + i) * slab, slab), slab)
            query[at, :] = q
            key[at, :] = k
            value[at, :] = v
            mix[at, :] = k * v
        return last_one, last_two

    zero = jnp.zeros((slab, LANES), F32)
    lax.fori_loop(0, rows // UNROLL, gather, (zero, zero))

    row_in_seq = iota((rows, LANES), 0) % chunks

    def scan(re, im, g, backward):
        for j in range(max(1, (chunks - 1).bit_length())):
            shift = 1 << j
            amount = rows - shift if backward else shift
            keep = row_in_seq < chunks - shift if backward else row_in_seq >= shift
            old_re = jnp.where(keep, pltpu.roll(re, amount, 0), 0.0)
            old_im = jnp.where(keep, pltpu.roll(im, amount, 0), 0.0)
            a, b = state_rows[g, 0, j : j + 1, :], state_rows[g, 1, j : j + 1, :]
            re, im = re + a * old_re - b * old_im, im + a * old_im + b * old_re
        amount = rows - 1 if backward else 1
        keep = row_in_seq < chunks - 1 if backward else row_in_seq >= 1
        re = jnp.where(keep, pltpu.roll(re, amount, 0), 0.0)
        im = jnp.where(keep, pltpu.roll(im, amount, 0), 0.0)
        a, b = state_rows[g, 0, 6:7, :], state_rows[g, 1, 6:7, :]
        return a * re - b * im, -(a * im + b * re)

    def long_conv(source, target, backward):
        enter, leave = (0, 2) if backward else (2, 0)

        def per_group(g, _):
            base = g * GROUP
            for c in range(GROUP):
                at = pl.ds(pl.multiple_of(g * wide + c * modes, modes), modes)
                for half in range(2):
                    spot = slice(half * wide + c * modes, half * wide + (c + 1) * modes)
                    for part in range(2):
                        diag[part, spot, c * LANES : (c + 1) * LANES] = bank[2 * (enter + half) + part, at, :]
            local = jnp.zeros((rows, 2 * wide), F32)
            for c in range(GROUP):
                u = split(source[pl.ds(base + c, rows, stride=slab), :])
                staged[0, base + c], staged[1, base + c] = u
                at = slice(c * LANES, (c + 1) * LANES)
                local = local + three(nt, u, (diag[0, :, at], diag[1, :, at]))
            re, im = scan(local[:, :wide], local[:, wide:], g, backward)
            state = split(jnp.concatenate([re, im], axis=1))
            for c in range(GROUP):
                u = (staged[0, base + c], staged[1, base + c])
                at = slice(c * LANES, (c + 1) * LANES)
                band = (toeplitz[0, base + c], toeplitz[1, base + c])
                out = three(nt if backward else nn, u, band)
                mine = slice(c * modes, (c + 1) * modes)
                held = [jnp.concatenate([p[:, mine], p[:, wide + c * modes : wide + (c + 1) * modes]], axis=1) for p in state]
                rows_at = pl.ds(pl.multiple_of(g * wide + c * modes, modes), modes)
                pole = [
                    jnp.concatenate([bank[2 * leave + part, rows_at, :], bank[2 * (leave + 1) + part, rows_at, :]], axis=0)
                    for part in range(2)
                ]
                out = out + three(nn, held, pole)
                target[pl.ds(base + c, rows, stride=slab), :] = out
            return 0

        lax.fori_loop(0, groups, per_group, 0, unroll=2)

    long_conv(mix, long_out, False)

    def emit(place, where):
        at = slab_rows(place)
        mixed_out[at, :], level_out[place] = fixed(query[at, :] * long_out[at, :])
        send(mixed_out.at[at], mixer.at[slab_rows(me)], mixer_sems, where)
        send(level_out.at[place], mixer_scale.at[me], level_sems, where)

    each_peer(emit)
    at = slab_rows(me)
    mixer[at, :], mixer_scale[me] = fixed(query[at, :] * long_out[at, :])
    most = pl.ds(0, (rows - 1) * slab)
    wait_bytes(cot_in.at[most], cot_sems.at[1])

    def weigh(step, _):
        for i in range(8):
            r = step * 8 + i
            at = slab_rows(r)
            value_in = real(cot_in[at, :], head_in[pl.ds(2 * r + 1, 1), :])
            cot[at, :] = value_in
            mix[at, :] = value_in * query[at, :]
        return 0

    lax.fori_loop(0, rows // 8, weigh, 0)

    grad_mixed = query
    long_conv(mix, grad_mixed, True)

    def scatter(step, carry):
        next_one, next_two, total = carry
        r0 = rows - UNROLL - step * UNROLL
        fresh = (r0 % chunks) == chunks - UNROLL
        next_one = jnp.where(fresh, 0.0, next_one)
        next_two = jnp.where(fresh, 0.0, next_two)
        pieces, hots = [None] * UNROLL, [None] * UNROLL
        for i in reversed(range(UNROLL)):
            at = pl.ds(pl.multiple_of((r0 + i) * slab, slab), slab)
            gm = grad_mixed[at, :]
            gq = cot[at, :] * long_out[at, :]
            gk = gm * value[at, :]
            gv = gm * key[at, :]
            zeroth, first, second = (taps[j] * gq + taps[3 + j] * gk + taps[6 + j] * gv for j in range(3))
            one = pltpu.roll(first, LANES - 1, 1)
            two = pltpu.roll(second, LANES - 2, 1)
            gx = (
                zeroth
                + jnp.where(lane_c >= LANES - 1, next_one, one)
                + jnp.where(lane_c >= LANES - 2, next_two, two)
            )
            next_one, next_two = one, two
            hots[i], bank_of = token_parts(r0 + i)
            both = jnp.concatenate(split(gx), axis=0)
            mask = [jnp.where(bank_of == b, 1.0, 0.0).astype(BF16) for b in range(banks)]
            pieces[i] = jnp.concatenate([both * m for m in mask], axis=0)
        hot = jnp.concatenate(hots, axis=1)
        return next_one, next_two, total + nt(jnp.concatenate(pieces, axis=1), hot)

    _, _, total = lax.fori_loop(
        0, rows // UNROLL, scatter, (zero, zero, jnp.zeros((2 * slab * banks, LANES), F32))
    )
    step = 2 * slab
    pieces = [total[b * step : b * step + slab] + total[b * step + slab : (b + 1) * step] for b in range(banks)]
    gather_grad(
        pieces, chunks, quarters, columns_of, every, scales, turn_sems, send_sems, recv_sems
    )
    wait_bytes(head_in.at[pl.ds(0, 2 * (rows - 1))], head_sems.at[0])
    wait_bytes(cot_in.at[most], cot_sems.at[0])
    for end in range(2):
        wait_bytes(mixer.at[most], mixer_sems.at[end])
        wait_bytes(mixer_scale.at[pl.ds(0, rows - 1)], level_sems.at[end])


def run_block(tok, embedding, conv_taps, gains, residues, decays, seeds, cot, chunks):
    modes, width = residues.shape
    vocab = embedding.shape[0]
    rows = width // (embedding.shape[1] // chunks)
    slab = width // rows
    tall = rows * slab
    side = round(chunks ** (1 / 3))
    vmem = pl.BlockSpec(memory_space=pltpu.VMEM)
    hbm = pl.BlockSpec(memory_space=pl.ANY)
    dma = pltpu.SemaphoreType.DMA
    return pl.pallas_call(
        functools.partial(block_kernel, chunks, chunks * LANES),
        out_shape=(
            jax.ShapeDtypeStruct((tall, LANES), jnp.int16),
            jax.ShapeDtypeStruct((rows, 1, LANES), F32),
            jax.ShapeDtypeStruct((side,) * 3 + (8, LANES // 8, LANES), jnp.int16),
            jax.ShapeDtypeStruct((side,) * 3 + (1, LANES), F32),
        ),
        in_specs=[vmem, hbm, hbm, vmem, hbm, hbm, hbm, hbm],
        out_specs=(vmem, vmem, vmem, vmem),
        scratch_shapes=[pltpu.VMEM((tall, LANES), F32)] * 6
        + [pltpu.VMEM((tall, LANES), jnp.int16)] * 3
        + [
            pltpu.VMEM((rows, 1, LANES), F32),
            pltpu.VMEM((2 * rows, LANES), F32),
            pltpu.VMEM((2 * rows, LANES), F32),
            pltpu.VMEM((2, slab, LANES, LANES), BF16),
            pltpu.VMEM((vocab // LANES * slab, LANES), BF16),
            pltpu.VMEM((10, slab, LANES), F32),
            pltpu.VMEM((modes, LANES), F32),
            pltpu.VMEM((modes, LANES), F32),
            pltpu.VMEM((modes, LANES), jnp.int32),
            pltpu.VMEM((vocab, LANES), BF16),
            pltpu.VMEM((LANES, vocab), F32),
            pltpu.VMEM((3, 3, LANES), F32),
            pltpu.VMEM((8, slab * modes, LANES), BF16),
            pltpu.VMEM((2, slab, LANES, LANES), BF16),
            pltpu.VMEM((2, 2 * GROUP * modes, GROUP * LANES), BF16),
            pltpu.VMEM((slab // GROUP, 2, 8, LANES), F32),
            pltpu.VMEM((side, slab, LANES), F32),
            pltpu.VMEM((LANES, LANES), F32),
            dma((6,)), dma((2,)), dma((2,)), dma((2,)), dma((2,)), dma((2, 3)), dma((3, 3, 7)), dma((3, 3, 7)),
        ],
        compiler_params=pltpu.CompilerParams(
            vmem_limit_bytes=56 * 1024 * 1024, collective_id=0, has_side_effects=True
        ),
        name="hyena_block",
    )(tok, embedding, conv_taps, gains, residues, decays, seeds, cot)


def finish_kernel(every, scales, mixer, mixer_scale, grad_out, mixer_out):
    for z in range(every.shape[0]):
        for x in range(every.shape[1]):
            n = z * every.shape[1] + x
            values = every[z, x, 0].reshape(LANES, LANES).astype(jnp.int32).astype(F32)
            grad_out[:, n * LANES : (n + 1) * LANES] = values * scales[z, x, 0]
    count = mixer_scale.shape[0]
    slab = mixer.shape[0] // count
    for n in range(count):
        at = slice(n * slab, (n + 1) * slab)
        mixer_out[at, :] = mixer[at, :].astype(jnp.int32).astype(F32) * mixer_scale[n]


def finish(mixer, mixer_scale, every, scales):
    a, b, c, tiles = every.shape[:4]
    tall, blocks = mixer.shape[0], mixer_scale.shape[0]
    return pl.pallas_call(
        finish_kernel,
        grid=(c,),
        out_shape=(
            jax.ShapeDtypeStruct((c * LANES, a * b * LANES), F32),
            jax.ShapeDtypeStruct(mixer.shape, F32),
        ),
        in_specs=[
            pl.BlockSpec((a, b, 1, *every.shape[3:]), lambda n: (0, 0, n, 0, 0, 0)),
            pl.BlockSpec((a, b, 1, 1, LANES), lambda n: (0, 0, n, 0, 0)),
            pl.BlockSpec((tall // c, LANES), lambda n: (n, 0)),
            pl.BlockSpec((blocks // c, 1, LANES), lambda n: (n, 0, 0)),
        ],
        out_specs=(
            pl.BlockSpec((LANES, a * b * LANES), lambda n: (n, 0)),
            pl.BlockSpec((tall // c, LANES), lambda n: (n, 0)),
        ),
        name="finish",
    )(every, scales, mixer, mixer_scale)


def body(token_ids, embedding, conv_taps, residues, decays, filter_seed, skip_gain, cotangent):
    ctx_size = lax.axis_size("ctx")
    width = conv_taps.shape[2]
    tok_block = token_ids.shape[1]
    packed = run_block(
        token_ids, embedding, conv_taps, skip_gain.reshape(-1, LANES),
        residues.T, decays.T, filter_seed.T, cotangent.reshape(width, tok_block), ctx_size,
    )
    grad, mixer = finish(*packed)
    return mixer.reshape(cotangent.shape), grad


def solution(mesh):
    placed = (P("fsdp", "ctx"), P(None, "fsdp"), P(), P(), P(), P(), P(), P("fsdp", None, "ctx"))
    return jax.shard_map(
        body,
        mesh=mesh,
        in_specs=placed,
        out_specs=(P("fsdp", None, "ctx"), P(None, "fsdp")),
        check_vma=False,
    )
```

```python
import functools
import math

import jax
import jax.numpy as jnp
from jax import lax
from jax.experimental import pallas as pl
from jax.experimental.pallas import tpu as pltpu
from jax.sharding import PartitionSpec as P

PERIOD = 4096
F32 = jnp.float32
BF16 = jnp.bfloat16
LANES = 128
GROUP = 8


def iota(shape, dim):
    return lax.broadcasted_iota(jnp.int32, shape, dim)


def split(value):
    high = value.astype(BF16)
    return high, (value - high.astype(F32)).astype(BF16)


def cis(phase):
    quarter = PERIOD // 4
    turn = (phase + quarter // 2) // quarter
    a = (phase - turn * quarter).astype(F32) * (2.0 * math.pi / PERIOD)
    b = a * a
    s = a * (1.0 + b * (-1 / 6 + b * (1 / 120 + b * (-1 / 5040 + b * (1 / 362880)))))
    c = 1.0 + b * (-0.5 + b * (1 / 24 + b * (-1 / 720 + b * (1 / 40320))))
    odd = turn % 2 == 1
    re = jnp.where(odd, s, c)
    im = jnp.where(odd, c, s)
    re = jnp.where((turn == 1) | (turn == 2), -re, re)
    im = jnp.where((turn == 2) | (turn == 3), -im, im)
    return re, im


def power(rate, seed, steps):
    mag = jnp.exp(-rate * steps.astype(F32))
    re, im = cis((seed * steps) % PERIOD)
    return mag * re, mag * im


def nn(a, b):
    return jnp.dot(a, b, preferred_element_type=F32)


def nt(a, b):
    return lax.dot_general(a, b, (((1,), (1,)), ((), ())), preferred_element_type=F32)


def three(dot, left, right):
    left_high, left_low = left
    right_high, right_low = right
    rows = left_high.shape[0]
    both = dot(jnp.concatenate([left_high, left_low], axis=0), right_high)
    return both[:rows] + both[rows:] + dot(left_high, right_low)


MESH = pl.DeviceIdType.MESH


LEVELS = 32767.0


def gather_grad(pieces, chunks, quarters, columns_of, every, scales, turn_sems, send_sems, recv_sems):
    sides = every.shape[:3]
    ctx = lax.axis_index("ctx")
    fsdp = lax.axis_index("fsdp")
    spans = (sides[1] * sides[2], sides[2], 1)
    here = [lax.rem(ctx // span, side) for span, side in zip(spans, sides)]
    slab = pieces[0].shape[0]
    sent = []

    def neighbour(axis, hop):
        there = lax.rem(here[axis] + hop + sides[axis], sides[axis])
        return there, (fsdp, ctx + (there - here[axis]) * spans[axis])

    def send(source, target, sender, receiver, where):
        made = pltpu.make_async_remote_copy(
            src_ref=source, dst_ref=target, send_sem=sender, recv_sem=receiver,
            device_id=where, device_id_type=MESH,
        )
        made.start()
        sent.append(made)

    def landed(place, sem):
        pltpu.make_async_copy(place, place, sem).wait()

    for j in range(sides[2]):
        quarters[j] = pieces[j]
    strip = pl.ds(pl.multiple_of(here[2] * slab, slab), slab)
    for n, hop in enumerate((1, -1, 2)):
        there, where = neighbour(2, hop)
        send(quarters.at[there], columns_of.at[strip], turn_sems.at[0, n], turn_sems.at[1, n], where)
    columns_of[strip, :] = quarters[here[2]]
    for n, hop in enumerate((-1, 1, 2)):
        there = neighbour(2, hop)[0]
        landed(columns_of.at[pl.ds(pl.multiple_of(there * slab, slab), slab)], turn_sems.at[1, n])
    block = columns_of[...].T
    peak = jnp.max(jnp.abs(block), axis=0, keepdims=True)
    block = jnp.round(block * (LEVELS / jnp.maximum(peak, 1e-30))).astype(jnp.int32).astype(jnp.int16)
    tiles = every.shape[3]
    every[here[0], here[1], here[2]] = block.reshape(tiles, LANES // tiles, LANES)
    scales[here[0], here[1], here[2]] = peak * (1.0 / LEVELS)

    def at(ref, axis, hop, done, *rest):
        index = []
        for n in range(3):
            if n == axis:
                index.append(pl.ds(lax.rem(here[n] + hop + sides[n], sides[n]), 1))
            elif n in done:
                index.append(slice(None))
            else:
                index.append(pl.ds(here[n], 1))
        return ref.at[(*index, *rest)]

    third = -(-tiles // 3)
    cuts = (0, third, 2 * third, tiles)
    for phase in range(3):
        plan = []
        for part in range(3):
            order = [(2 - part + n) % 3 for n in range(3)]
            axis, done = order[phase], order[:phase]
            first, size = cuts[part], cuts[part + 1] - cuts[part]
            half = size // 2
            whole, low, high = pl.ds(first, size), pl.ds(first, half), pl.ds(first + half, size - half)
            plan.append((part, axis, done, whole, low, high))
            right, left = neighbour(axis, 1)[1], neighbour(axis, -1)[1]
            mine = at(every, axis, 0, done, whole)
            sems = (send_sems.at[part, phase], recv_sems.at[part, phase])
            send(mine, mine, sems[0].at[0], sems[1].at[0], right)
            send(mine, mine, sems[0].at[1], sems[1].at[1], left)
            if phase < 2:
                send(mine, mine, sems[0].at[2], sems[1].at[2], neighbour(axis, 2)[1])
            if part == 2:
                level = at(scales, axis, 0, done)
                for n, hop in enumerate((1, -1, 2)):
                    send(level, level, sems[0].at[4 + n], sems[1].at[4 + n], neighbour(axis, hop)[1])
        for part, axis, done, whole, low, high in plan:
            sems = (send_sems.at[part, phase], recv_sems.at[part, phase])
            landed(at(every, axis, -1, done, whole), sems[1].at[0])
            if phase == 2:
                piece = at(every, axis, -1, done, low)
                send(piece, piece, sems[0].at[2], sems[1].at[2], neighbour(axis, 1)[1])
            landed(at(every, axis, 1, done, whole), sems[1].at[1])
            if phase == 2:
                piece = at(every, axis, 1, done, high)
                send(piece, piece, sems[0].at[3], sems[1].at[3], neighbour(axis, -1)[1])
        for part, axis, done, whole, low, high in plan:
            sem = recv_sems.at[part, phase]
            if phase < 2:
                landed(at(every, axis, 2, done, whole), sem.at[2])
            else:
                landed(at(every, axis, 2, done, low), sem.at[2])
                landed(at(every, axis, 2, done, high), sem.at[3])
            if part == 2:
                for n, hop in enumerate((-1, 1, 2)):
                    landed(at(scales, axis, hop, done), sem.at[4 + n])
    for made in sent:
        made.wait_send()


def block_kernel(
    chunks, seq_len,
    tok_mine, embedding, conv_taps, gains, residue_all, decay_all, seed_all, cot_mine,
    mixer, every, scales,
    query, key, value, mix, long_out, cot, cot_out, cot_in, mixed_out, tok,
    staged, table, taps, residues, decays, seeds, raw_table, turned, raw_taps,
    bank, toeplitz, diag, state_rows, quarters, columns_of,
    load_sems, tok_sems, cot_sems, mixer_sems, turn_sems, send_sems, recv_sems,
):
    vocab = embedding.shape[0]
    rows = tok.shape[0]
    slab = cot.shape[0] // rows
    modes = residues.shape[0]
    groups = slab // GROUP
    wide = GROUP * modes
    ctx = lax.axis_index("ctx")
    fsdp = lax.axis_index("fsdp")
    me = fsdp * chunks + ctx
    per_tile = LANES // slab

    def slab_rows(index):
        return pl.ds(pl.multiple_of(index * slab, slab), slab)

    def each_peer(action):
        action((1 - fsdp) * chunks + ctx, (1 - fsdp, ctx))

        def step(i, _):
            there = ctx + i
            there = jnp.where(there >= chunks, there - chunks, there)
            for side in (fsdp, 1 - fsdp):
                action(side * chunks + there, (side, there))
            return 0

        lax.fori_loop(1, chunks, step, 0, unroll=7)

    def send(source, target, sems, where):
        pltpu.make_async_remote_copy(
            src_ref=source, dst_ref=target, send_sem=sems.at[0], recv_sem=sems.at[1],
            device_id=where, device_id_type=MESH,
        ).start()

    barrier = pltpu.get_barrier_semaphore()
    load_cot = pltpu.make_async_copy(cot_mine, cot, load_sems.at[5])
    load_cot.start()
    each_peer(lambda place, where: pl.semaphore_signal(barrier, inc=1, device_id=where, device_id_type=MESH))

    lane_tile = pl.ds(pl.multiple_of(ctx // per_tile * LANES, LANES), LANES)
    wide_tile = pl.ds(pl.multiple_of(me // per_tile * LANES, LANES), LANES)
    loads = [
        pltpu.make_async_copy(source, target, load_sems.at[n])
        for n, (source, target) in enumerate((
            (residue_all.at[:, wide_tile], residues),
            (decay_all.at[:, wide_tile], decays),
            (seed_all.at[:, wide_tile], seeds),
            (conv_taps.at[:, :, wide_tile], raw_taps),
            (embedding.at[:, lane_tile], raw_table),
        ))
    ]
    for load in loads:
        load.start()

    sent_rows = pl.ds(0, slab + 2)

    def encode(target, place, block):
        peak = jnp.maximum(jnp.max(jnp.abs(block), axis=0, keepdims=True), 1e-30)
        power_of = jnp.ceil(jnp.log2(peak * (1.0 / LEVELS)))
        code = jnp.clip(jnp.round(block * jnp.exp2(-power_of)), -LEVELS, LEVELS)
        target[place, :slab, :] = code.astype(jnp.int32).astype(jnp.int16)
        exponent = jnp.broadcast_to(power_of, (16, LANES)).astype(jnp.int32).astype(jnp.int16)
        target[place, slab:, :] = exponent

    side = round(chunks ** (1 / 3))
    here = (ctx // (side * side), lax.rem(ctx // side, side), lax.rem(ctx, side))
    spans = (side * side, side, 1)

    def exchange(phase):
        axis = 2 - phase
        if axis < 0:
            other = (1 - fsdp, ctx)
            base = pl.ds(pl.multiple_of(fsdp * chunks, chunks), chunks)
            come = pl.ds(pl.multiple_of((1 - fsdp) * chunks, chunks), chunks)
            routes = [(base, come, other)]
        else:
            size = spans[axis]
            start = me // size * size
            routes = []
            for hop in (1, -1, 2):
                there = lax.rem(here[axis] + hop + side, side) - here[axis]
                back = lax.rem(here[axis] - hop + side, side) - here[axis]
                routes.append((
                    pl.ds(start, size), pl.ds(start + back * size, size), (fsdp, ctx + there * size)
                ))
        copies = []
        for n, (base, come, where) in enumerate(routes):
            made = pltpu.make_async_remote_copy(
                src_ref=tok.at[base], dst_ref=tok.at[base],
                send_sem=tok_sems.at[0, phase, n], recv_sem=tok_sems.at[1, phase, n],
                device_id=where, device_id_type=MESH,
            )
            made.start()
            copies.append((made, come))

        def arrive():
            for n, (made, come) in enumerate(copies):
                pltpu.make_async_copy(tok.at[come], tok.at[come], tok_sems.at[1, phase, n]).wait()
                made.wait_send()

        return arrive

    tok[me] = tok_mine[...]
    load_cot.wait()

    def pack(step, _):
        for i in range(16):
            r = step * 16 + i
            encode(cot_out, r, cot[slab_rows(r), :])
        return 0

    lax.fori_loop(0, rows // 16, pack, 0)
    pl.semaphore_wait(barrier, rows - 1)
    arrive = exchange(0)

    def wait_bytes(ref, sem):
        pltpu.make_async_copy(ref, ref, sem).wait()

    for load in loads:
        load.wait()
    sub = pl.ds(pl.multiple_of(lax.rem(ctx, per_tile) * slab, slab), slab)
    turned[...] = raw_table[...].astype(F32).T
    for b in range(vocab // LANES):
        table[b * slab : (b + 1) * slab, :] = turned[sub, b * LANES : (b + 1) * LANES].astype(BF16)
    pieces = [residues[...], decays[...], seeds[...].astype(F32)]
    pieces += [raw_taps[s, j : j + 1, :] for s in range(3) for j in range(3)]
    pieces.append(gains[pl.ds(me // per_tile, 1), :])
    pieces.append(jnp.zeros((LANES - 10 - 3 * modes, LANES), F32))
    turned[:, :LANES] = jnp.concatenate(pieces, axis=0).T
    columns = turned[sub, :LANES]
    for j in range(10):
        taps[j] = jnp.broadcast_to(columns[:, 3 * modes + j : 3 * modes + j + 1], (slab, LANES))

    arrive()
    arrive = exchange(1)

    spread = (iota((slab * modes, slab), 0) // modes == iota((slab * modes, slab), 1)).astype(F32)
    pick = iota((slab * modes, modes), 0) % modes == iota((slab * modes, modes), 1)

    def column(part):
        wide_part = jnp.dot(spread, part, precision=lax.Precision.HIGHEST, preferred_element_type=F32)
        return jnp.sum(jnp.where(pick, wide_part, 0.0), axis=1, keepdims=True)

    rate = column(columns[:, modes : 2 * modes])
    seed = column(columns[:, 2 * modes : 3 * modes])
    res = column(columns[:, :modes])
    weight = res * jnp.sqrt(rate + 1.0 / seq_len)
    seed_int = (seed + 0.5).astype(jnp.int32)
    rate_b = jnp.broadcast_to(rate, (slab * modes, LANES))
    seed_b = jnp.broadcast_to(seed_int, (slab * modes, LANES))
    lane = iota((slab * modes, LANES), 1)
    up = power(rate_b, seed_b, lane)
    down = power(rate_b, seed_b, LANES - 1 - lane)
    for place, part in enumerate((*up, *down)):
        high, low = split(part)
        bank[2 * place] = high
        bank[2 * place + 1] = low
    kernel_head = jnp.sum((up[0] * weight).reshape(slab, modes, LANES), axis=1)
    kernel_head = kernel_head + jnp.where(iota((slab, LANES), 1) == 0, taps[9], 0.0)

    arrive()
    arrive = exchange(2)

    upper = iota((LANES, LANES), 1) >= iota((LANES, LANES), 0)
    for c in range(slab):
        line = jnp.broadcast_to(kernel_head[c : c + 1], (LANES, LANES))
        rolled = pltpu.roll(line, 0, 1, stride=1, stride_axis=0)
        high, low = split(jnp.where(upper, rolled, 0.0))
        toeplitz[0, c] = high
        toeplitz[1, c] = low

    arrive()
    arrive = exchange(3)

    eye = iota((wide, LANES), 0) == iota((wide, LANES), 1)
    step_row = iota((8, LANES), 0)
    steps = jnp.where(step_row == 6, 1, LANES * (1 << jnp.minimum(step_row, 5)))
    for g in range(groups):
        def row(part):
            piece = jnp.broadcast_to(part[g * wide : (g + 1) * wide], (wide, LANES))
            return jnp.sum(jnp.where(eye, piece, 0.0), axis=0, keepdims=True)

        rate_row = jnp.broadcast_to(row(rate), (8, LANES))
        seed_row = jnp.broadcast_to((row(seed) + 0.5).astype(jnp.int32), (8, LANES))
        weight_row = row(weight)
        re, im = power(rate_row, seed_row, steps)
        scale = jnp.where(step_row == 6, jnp.broadcast_to(weight_row, (8, LANES)), 1.0)
        state_rows[g, 0] = re * scale
        state_rows[g, 1] = im * scale

    diag[...] = jnp.zeros_like(diag)

    arrive()
    lane_c = iota((slab, LANES), 1)
    low_row = iota((LANES, LANES), 0)
    banks = vocab // LANES

    def token_parts(r):
        token = tok[r]
        bank_of = token // LANES
        hot = jnp.where(low_row == token - bank_of * LANES, 1.0, 0.0).astype(BF16)
        return hot, bank_of

    UNROLL = 16

    def gather(step, carry):
        last_one, last_two = carry
        r0 = step * UNROLL
        parts = [token_parts(r0 + i) for i in range(UNROLL)]
        found = nn(table[...], jnp.concatenate([hot for hot, _ in parts], axis=1))
        fresh = (r0 % chunks) == 0
        last_one = jnp.where(fresh, 0.0, last_one)
        last_two = jnp.where(fresh, 0.0, last_two)
        for i in range(UNROLL):
            bank_of = parts[i][1]
            x = found[:slab, i * LANES : (i + 1) * LANES]
            for b in range(1, banks):
                x = jnp.where(bank_of == b, found[b * slab : (b + 1) * slab, i * LANES : (i + 1) * LANES], x)
            one = pltpu.roll(x, 1, 1)
            two = pltpu.roll(x, 2, 1)
            x1 = jnp.where(lane_c < 1, last_one, one)
            x2 = jnp.where(lane_c < 2, last_two, two)
            last_one, last_two = one, two
            q, k, v = (taps[3 * s] * x + taps[3 * s + 1] * x1 + taps[3 * s + 2] * x2 for s in range(3))
            at = pl.ds(pl.multiple_of((r0 + i) * slab, slab), slab)
            query[at, :] = q
            key[at, :] = k
            value[at, :] = v
            mix[at, :] = k * v
        return last_one, last_two

    def send_cot(place, where):
        send(cot_out.at[place, sent_rows], cot_in.at[me, sent_rows], cot_sems, where)

    def lookup(step, carry):
        per = chunks * UNROLL // rows
        for n in range(1, per + 1):
            i = step * per + n
            there = ctx + i
            there = jnp.where(there >= chunks, there - chunks, there)
            send_cot((1 - fsdp) * chunks + there, (1 - fsdp, there))
            if n < per:
                send_cot(fsdp * chunks + there, (fsdp, there))
            else:
                pl.when(i < chunks)(lambda: send_cot(fsdp * chunks + there, (fsdp, there)))
        return gather(step, carry)

    zero = jnp.zeros((slab, LANES), F32)
    cot_in[me] = cot_out[me]
    lax.fori_loop(0, rows // UNROLL, lookup, (zero, zero))

    row_in_seq = iota((rows, LANES), 0) % chunks

    def scan(re, im, g, backward):
        for j in range(max(1, (chunks - 1).bit_length())):
            shift = 1 << j
            amount = rows - shift if backward else shift
            keep = row_in_seq < chunks - shift if backward else row_in_seq >= shift
            old_re = jnp.where(keep, pltpu.roll(re, amount, 0), 0.0)
            old_im = jnp.where(keep, pltpu.roll(im, amount, 0), 0.0)
            a, b = state_rows[g, 0, j : j + 1, :], state_rows[g, 1, j : j + 1, :]
            re, im = re + a * old_re - b * old_im, im + a * old_im + b * old_re
        amount = rows - 1 if backward else 1
        keep = row_in_seq < chunks - 1 if backward else row_in_seq >= 1
        re = jnp.where(keep, pltpu.roll(re, amount, 0), 0.0)
        im = jnp.where(keep, pltpu.roll(im, amount, 0), 0.0)
        a, b = state_rows[g, 0, 6:7, :], state_rows[g, 1, 6:7, :]
        return a * re - b * im, -(a * im + b * re)

    def long_conv(source, target, backward):
        enter, leave = (0, 2) if backward else (2, 0)

        def per_group(g, _):
            base = g * GROUP
            for c in range(GROUP):
                at = pl.ds(pl.multiple_of(g * wide + c * modes, modes), modes)
                for half in range(2):
                    spot = slice(half * wide + c * modes, half * wide + (c + 1) * modes)
                    for part in range(2):
                        diag[part, spot, c * LANES : (c + 1) * LANES] = bank[2 * (enter + half) + part, at, :]
            local = jnp.zeros((rows, 2 * wide), F32)
            for c in range(GROUP):
                u = split(source[pl.ds(base + c, rows, stride=slab), :])
                staged[0, base + c], staged[1, base + c] = u
                at = slice(c * LANES, (c + 1) * LANES)
                local = local + three(nt, u, (diag[0, :, at], diag[1, :, at]))
            re, im = scan(local[:, :wide], local[:, wide:], g, backward)
            state = split(jnp.concatenate([re, im], axis=1))
            for c in range(GROUP):
                u = (staged[0, base + c], staged[1, base + c])
                at = slice(c * LANES, (c + 1) * LANES)
                band = (toeplitz[0, base + c], toeplitz[1, base + c])
                out = three(nt if backward else nn, u, band)
                mine = slice(c * modes, (c + 1) * modes)
                held = [jnp.concatenate([p[:, mine], p[:, wide + c * modes : wide + (c + 1) * modes]], axis=1) for p in state]
                rows_at = pl.ds(pl.multiple_of(g * wide + c * modes, modes), modes)
                pole = [
                    jnp.concatenate([bank[2 * leave + part, rows_at, :], bank[2 * (leave + 1) + part, rows_at, :]], axis=0)
                    for part in range(2)
                ]
                out = out + three(nn, held, pole)
                target[pl.ds(base + c, rows, stride=slab), :] = out
            return 0

        lax.fori_loop(0, groups, per_group, 0, unroll=2)

    long_conv(mix, long_out, False)

    def emit(place):
        at = slab_rows(place)
        q = query[at, :]
        encode(mixed_out, place, q * long_out[at, :])
        power_of = cot_in[place, slab:, :].astype(jnp.int32)[:1].astype(F32)
        value_in = cot_in[place, :slab, :].astype(jnp.int32).astype(F32) * jnp.exp2(power_of)
        cot[at, :] = value_in
        mix[at, :] = value_in * q

    def emit_send(place, where):
        emit(place)
        send(mixed_out.at[place, sent_rows], mixer.at[me, sent_rows], mixer_sems, where)

    most = pl.ds(0, rows - 1)
    wait_bytes(cot_in.at[most, sent_rows], cot_sems.at[1])
    each_peer(emit_send)
    emit(me)
    mixer[me] = mixed_out[me]

    grad_mixed = query
    long_conv(mix, grad_mixed, True)

    def scatter(step, carry):
        next_one, next_two, total = carry
        r0 = rows - UNROLL - step * UNROLL
        fresh = (r0 % chunks) == chunks - UNROLL
        next_one = jnp.where(fresh, 0.0, next_one)
        next_two = jnp.where(fresh, 0.0, next_two)
        pieces, hots = [None] * UNROLL, [None] * UNROLL
        for i in reversed(range(UNROLL)):
            at = pl.ds(pl.multiple_of((r0 + i) * slab, slab), slab)
            gm = grad_mixed[at, :]
            gq = cot[at, :] * long_out[at, :]
            gk = gm * value[at, :]
            gv = gm * key[at, :]
            zeroth, first, second = (taps[j] * gq + taps[3 + j] * gk + taps[6 + j] * gv for j in range(3))
            one = pltpu.roll(first, LANES - 1, 1)
            two = pltpu.roll(second, LANES - 2, 1)
            gx = (
                zeroth
                + jnp.where(lane_c >= LANES - 1, next_one, one)
                + jnp.where(lane_c >= LANES - 2, next_two, two)
            )
            next_one, next_two = one, two
            hots[i], bank_of = token_parts(r0 + i)
            both = jnp.concatenate(split(gx), axis=0)
            mask = [jnp.where(bank_of == b, 1.0, 0.0).astype(BF16) for b in range(banks)]
            pieces[i] = jnp.concatenate([both * m for m in mask], axis=0)
        hot = jnp.concatenate(hots, axis=1)
        return next_one, next_two, total + nt(jnp.concatenate(pieces, axis=1), hot)

    _, _, total = lax.fori_loop(
        0, rows // UNROLL, scatter, (zero, zero, jnp.zeros((2 * slab * banks, LANES), F32))
    )
    step = 2 * slab
    pieces = [total[b * step : b * step + slab] + total[b * step + slab : (b + 1) * step] for b in range(banks)]
    gather_grad(
        pieces, chunks, quarters, columns_of, every, scales, turn_sems, send_sems, recv_sems
    )
    wait_bytes(cot_in.at[most, sent_rows], cot_sems.at[0])
    for end in range(2):
        wait_bytes(mixer.at[most, sent_rows], mixer_sems.at[end])


def run_block(tok, embedding, conv_taps, gains, residues, decays, seeds, cot, chunks):
    modes, width = residues.shape
    vocab = embedding.shape[0]
    rows = width // (embedding.shape[1] // chunks)
    slab = width // rows
    tall = rows * slab
    side = round(chunks ** (1 / 3))
    vmem = pl.BlockSpec(memory_space=pltpu.VMEM)
    hbm = pl.BlockSpec(memory_space=pl.ANY)
    dma = pltpu.SemaphoreType.DMA
    return pl.pallas_call(
        functools.partial(block_kernel, chunks, chunks * LANES),
        out_shape=(
            jax.ShapeDtypeStruct((rows, slab + 16, LANES), jnp.int16),
            jax.ShapeDtypeStruct((side,) * 3 + (8, LANES // 8, LANES), jnp.int16),
            jax.ShapeDtypeStruct((side,) * 3 + (1, LANES), F32),
        ),
        in_specs=[vmem, hbm, hbm, vmem, hbm, hbm, hbm, hbm],
        out_specs=(vmem, vmem, vmem),
        scratch_shapes=[pltpu.VMEM((tall, LANES), F32)] * 6
        + [pltpu.VMEM((rows, slab + 16, LANES), jnp.int16)] * 3
        + [
            pltpu.VMEM((rows, 1, LANES), jnp.int32),
            pltpu.VMEM((2, slab, LANES, LANES), BF16),
            pltpu.VMEM((vocab // LANES * slab, LANES), BF16),
            pltpu.VMEM((10, slab, LANES), F32),
            pltpu.VMEM((modes, LANES), F32),
            pltpu.VMEM((modes, LANES), F32),
            pltpu.VMEM((modes, LANES), jnp.int32),
            pltpu.VMEM((vocab, LANES), BF16),
            pltpu.VMEM((LANES, vocab), F32),
            pltpu.VMEM((3, 3, LANES), F32),
            pltpu.VMEM((8, slab * modes, LANES), BF16),
            pltpu.VMEM((2, slab, LANES, LANES), BF16),
            pltpu.VMEM((2, 2 * GROUP * modes, GROUP * LANES), BF16),
            pltpu.VMEM((slab // GROUP, 2, 8, LANES), F32),
            pltpu.VMEM((side, slab, LANES), F32),
            pltpu.VMEM((LANES, LANES), F32),
            dma((6,)), dma((2, 4, 3)), dma((2,)), dma((2,)), dma((2, 3)), dma((3, 3, 7)), dma((3, 3, 7)),
        ],
        compiler_params=pltpu.CompilerParams(
            vmem_limit_bytes=56 * 1024 * 1024, collective_id=0, has_side_effects=True
        ),
        name="hyena_block",
    )(tok, embedding, conv_taps, gains, residues, decays, seeds, cot)


def finish_kernel(every, scales, mixer, grad_out, mixer_out):
    for z in range(every.shape[0]):
        for x in range(every.shape[1]):
            n = z * every.shape[1] + x
            values = every[z, x, 0].reshape(LANES, LANES).astype(jnp.int32).astype(F32)
            grad_out[:, n * LANES : (n + 1) * LANES] = values * scales[z, x, 0]
    slab = mixer.shape[1] - 16
    for n in range(mixer.shape[0]):
        power_of = mixer[n, slab:, :].astype(jnp.int32)[:1].astype(F32)
        value = mixer[n, :slab, :].astype(jnp.int32).astype(F32)
        mixer_out[n * slab : (n + 1) * slab, :] = value * jnp.exp2(power_of)


def finish(mixer, every, scales):
    a, b, c, tiles = every.shape[:4]
    blocks, slab = mixer.shape[0], mixer.shape[1] - 16
    tall = blocks * slab
    return pl.pallas_call(
        finish_kernel,
        grid=(c,),
        out_shape=(
            jax.ShapeDtypeStruct((c * LANES, a * b * LANES), F32),
            jax.ShapeDtypeStruct((tall, LANES), F32),
        ),
        in_specs=[
            pl.BlockSpec((a, b, 1, *every.shape[3:]), lambda n: (0, 0, n, 0, 0, 0)),
            pl.BlockSpec((a, b, 1, 1, LANES), lambda n: (0, 0, n, 0, 0)),
            pl.BlockSpec((blocks // c, *mixer.shape[1:]), lambda n: (n, 0, 0)),
        ],
        out_specs=(
            pl.BlockSpec((LANES, a * b * LANES), lambda n: (n, 0)),
            pl.BlockSpec((tall // c, LANES), lambda n: (n, 0)),
        ),
        name="finish",
    )(every, scales, mixer)


def body(token_ids, embedding, conv_taps, residues, decays, filter_seed, skip_gain, cotangent):
    ctx_size = lax.axis_size("ctx")
    width = conv_taps.shape[2]
    tok_block = token_ids.shape[1]
    packed = run_block(
        token_ids, embedding, conv_taps, skip_gain.reshape(-1, LANES),
        residues.T, decays.T, filter_seed.T, cotangent.reshape(width, tok_block), ctx_size,
    )
    grad, mixer = finish(*packed)
    return mixer.reshape(cotangent.shape), grad


def solution(mesh):
    placed = (P("fsdp", "ctx"), P(None, "fsdp"), P(), P(), P(), P(), P(), P("fsdp", None, "ctx"))
    return jax.shard_map(
        body,
        mesh=mesh,
        in_specs=placed,
        out_specs=(P("fsdp", None, "ctx"), P(None, "fsdp")),
        check_vma=False,
    )
```

```python
import functools
import math

import jax
import jax.numpy as jnp
from jax import lax
from jax.experimental import pallas as pl
from jax.experimental.pallas import tpu as pltpu
from jax.sharding import PartitionSpec as P

PERIOD = 4096
F32 = jnp.float32
BF16 = jnp.bfloat16
LANES = 128
GROUP = 8


def iota(shape, dim):
    return lax.broadcasted_iota(jnp.int32, shape, dim)


def split(value):
    high = value.astype(BF16)
    return high, (value - high.astype(F32)).astype(BF16)


def cis(phase):
    quarter = PERIOD // 4
    turn = (phase + quarter // 2) // quarter
    a = (phase - turn * quarter).astype(F32) * (2.0 * math.pi / PERIOD)
    b = a * a
    s = a * (1.0 + b * (-1 / 6 + b * (1 / 120 + b * (-1 / 5040 + b * (1 / 362880)))))
    c = 1.0 + b * (-0.5 + b * (1 / 24 + b * (-1 / 720 + b * (1 / 40320))))
    odd = turn % 2 == 1
    re = jnp.where(odd, s, c)
    im = jnp.where(odd, c, s)
    re = jnp.where((turn == 1) | (turn == 2), -re, re)
    im = jnp.where((turn == 2) | (turn == 3), -im, im)
    return re, im


def power(rate, seed, steps):
    mag = jnp.exp(-rate * steps.astype(F32))
    re, im = cis((seed * steps) % PERIOD)
    return mag * re, mag * im


def nn(a, b):
    return jnp.dot(a, b, preferred_element_type=F32)


def nt(a, b):
    return lax.dot_general(a, b, (((1,), (1,)), ((), ())), preferred_element_type=F32)


def three(dot, left, right):
    left_high, left_low = left
    right_high, right_low = right
    rows = left_high.shape[0]
    both = dot(jnp.concatenate([left_high, left_low], axis=0), right_high)
    return both[:rows] + both[rows:] + dot(left_high, right_low)


MESH = pl.DeviceIdType.MESH


LEVELS = 32767.0


def fixed(block):
    peak = jnp.maximum(jnp.max(jnp.abs(block), axis=0, keepdims=True), 1e-30)
    power_of = jnp.ceil(jnp.log2(peak * (1.0 / LEVELS)))
    code = jnp.clip(jnp.round(block * jnp.exp2(-power_of)), -LEVELS, LEVELS)
    return code.astype(jnp.int32).astype(jnp.int16), power_of


def real(code, power_of):
    scale = jnp.exp2(power_of.astype(jnp.int32)[:1].astype(F32))
    return code.astype(jnp.int32).astype(F32) * scale


def gather_grad(pieces, chunks, quarters, columns_of, every, turn_sems, send_sems, recv_sems):
    sides = every.shape[:3]
    ctx = lax.axis_index("ctx")
    fsdp = lax.axis_index("fsdp")
    spans = (sides[1] * sides[2], sides[2], 1)
    here = [lax.rem(ctx // span, side) for span, side in zip(spans, sides)]
    slab = pieces[0].shape[0]
    sent = []

    def neighbour(axis, hop):
        there = lax.rem(here[axis] + hop + sides[axis], sides[axis])
        return there, (fsdp, ctx + (there - here[axis]) * spans[axis])

    def send(source, target, sender, receiver, where):
        made = pltpu.make_async_remote_copy(
            src_ref=source, dst_ref=target, send_sem=sender, recv_sem=receiver,
            device_id=where, device_id_type=MESH,
        )
        made.start()
        sent.append(made)

    def landed(place, sem):
        pltpu.make_async_copy(place, place, sem).wait()

    for j in range(sides[2]):
        quarters[j] = pieces[j]
    strip = pl.ds(pl.multiple_of(here[2] * slab, slab), slab)
    for n, hop in enumerate((1, -1, 2)):
        there, where = neighbour(2, hop)
        send(quarters.at[there], columns_of.at[strip], turn_sems.at[0, n], turn_sems.at[1, n], where)
    columns_of[strip, :] = quarters[here[2]]
    for n, hop in enumerate((-1, 1, 2)):
        there = neighbour(2, hop)[0]
        landed(columns_of.at[pl.ds(pl.multiple_of(there * slab, slab), slab)], turn_sems.at[1, n])
    block = columns_of[...].T
    code, power_of = fixed(block)
    tiles, height = every.shape[3] - 1, every.shape[4]
    every[here[0], here[1], here[2], :tiles] = code.reshape(tiles, height, LANES)
    every[here[0], here[1], here[2], tiles] = jnp.broadcast_to(power_of, (height, LANES)).astype(jnp.int32).astype(jnp.int16)

    def at(axis, hop, done, part):
        index = []
        for n in range(3):
            if n == axis:
                index.append(pl.ds(lax.rem(here[n] + hop + sides[n], sides[n]), 1))
            elif n in done:
                index.append(slice(None))
            else:
                index.append(pl.ds(here[n], 1))
        third = (tiles + 1) // 3
        return every.at[(*index, pl.ds(part * third, third))]

    for phase in range(3):
        plan = [((2 - part + phase) % 3, [(2 - part + n) % 3 for n in range(phase)]) for part in range(3)]
        for part, (axis, done) in enumerate(plan):
            mine = at(axis, 0, done, part)
            for n, hop in enumerate((2, 1, -1)):
                send(mine, mine, send_sems.at[part, phase, n], recv_sems.at[part, phase, n], neighbour(axis, hop)[1])
        for part, (axis, done) in enumerate(plan):
            for n, hop in enumerate((2, -1, 1)):
                landed(at(axis, hop, done, part), recv_sems.at[part, phase, n])
    for made in sent:
        made.wait_send()


def block_kernel(
    chunks, seq_len,
    tok_mine, embedding, conv_taps, gains, residue_all, decay_all, seed_all, cot_mine,
    mixer, every,
    query, key, value, mix, long_out, cot, cot_out, cot_in, mixed_out, tok,
    staged, table, taps, residues, decays, seeds, raw_table, turned, raw_taps,
    bank, toeplitz, diag, state_rows, quarters, columns_of,
    load_sems, tok_sems, cot_sems, mixer_sems, turn_sems, send_sems, recv_sems,
):
    vocab = embedding.shape[0]
    rows = tok.shape[0]
    slab = cot.shape[0] // rows
    modes = residues.shape[0]
    groups = slab // GROUP
    wide = GROUP * modes
    ctx = lax.axis_index("ctx")
    fsdp = lax.axis_index("fsdp")
    me = fsdp * chunks + ctx
    per_tile = LANES // slab

    def slab_rows(index):
        return pl.ds(pl.multiple_of(index * slab, slab), slab)

    def each_peer(action):
        action((1 - fsdp) * chunks + ctx, (1 - fsdp, ctx))

        def step(i, _):
            there = ctx + i
            there = jnp.where(there >= chunks, there - chunks, there)
            for side in (fsdp, 1 - fsdp):
                action(side * chunks + there, (side, there))
            return 0

        lax.fori_loop(1, chunks, step, 0, unroll=7)

    def send(source, target, sems, where):
        pltpu.make_async_remote_copy(
            src_ref=source, dst_ref=target, send_sem=sems.at[0], recv_sem=sems.at[1],
            device_id=where, device_id_type=MESH,
        ).start()

    barrier = pltpu.get_barrier_semaphore()
    load_cot = pltpu.make_async_copy(cot_mine, cot, load_sems.at[5])
    load_cot.start()
    each_peer(lambda place, where: pl.semaphore_signal(barrier, inc=1, device_id=where, device_id_type=MESH))

    lane_tile = pl.ds(pl.multiple_of(ctx // per_tile * LANES, LANES), LANES)
    wide_tile = pl.ds(pl.multiple_of(me // per_tile * LANES, LANES), LANES)
    loads = [
        pltpu.make_async_copy(source, target, load_sems.at[n])
        for n, (source, target) in enumerate((
            (residue_all.at[:, wide_tile], residues),
            (decay_all.at[:, wide_tile], decays),
            (seed_all.at[:, wide_tile], seeds),
            (conv_taps.at[:, :, wide_tile], raw_taps),
            (embedding.at[:, lane_tile], raw_table),
        ))
    ]
    for load in loads:
        load.start()

    sent_rows = pl.ds(0, slab + 2)

    def encode(target, place, block):
        code, power_of = fixed(block)
        target[place, :slab, :] = code
        target[place, slab:, :] = jnp.broadcast_to(power_of, (16, LANES)).astype(jnp.int32).astype(jnp.int16)

    own_tok = tok_mine[...]
    load_cot.wait()

    def pack(step, _):
        for i in range(16):
            r = step * 16 + i
            encode(cot_out, r, cot[slab_rows(r), :])
        return 0

    lax.fori_loop(0, rows // 16, pack, 0)
    pl.semaphore_wait(barrier, rows - 1)
    tok[me] = own_tok

    def send_tok(i, _):
        there = ctx + i
        there = jnp.where(there >= chunks, there - chunks, there)
        send(tok_mine, tok.at[me], tok_sems.at[0], (fsdp, there))
        return 0

    lax.fori_loop(1, chunks, send_tok, 0, unroll=7)
    def send_cot(place, where):
        send(cot_out.at[place, sent_rows], cot_in.at[me, sent_rows], cot_sems, where)

    each_peer(send_cot)

    def wait_bytes(ref, sem):
        pltpu.make_async_copy(ref, ref, sem).wait()

    for load in loads:
        load.wait()
    sub = pl.ds(pl.multiple_of(lax.rem(ctx, per_tile) * slab, slab), slab)
    turned[...] = raw_table[...].astype(F32).T
    for b in range(vocab // LANES):
        table[b * slab : (b + 1) * slab, :] = turned[sub, b * LANES : (b + 1) * LANES].astype(BF16)
    pieces = [residues[...], decays[...], seeds[...].astype(F32)]
    pieces += [raw_taps[s, j : j + 1, :] for s in range(3) for j in range(3)]
    pieces.append(gains[pl.ds(me // per_tile, 1), :])
    pieces.append(jnp.zeros((LANES - 10 - 3 * modes, LANES), F32))
    turned[:, :LANES] = jnp.concatenate(pieces, axis=0).T
    columns = turned[sub, :LANES]
    for j in range(10):
        taps[j] = jnp.broadcast_to(columns[:, 3 * modes + j : 3 * modes + j + 1], (slab, LANES))

    spread = (iota((slab * modes, slab), 0) // modes == iota((slab * modes, slab), 1)).astype(F32)
    pick = iota((slab * modes, modes), 0) % modes == iota((slab * modes, modes), 1)

    def column(part):
        wide_part = jnp.dot(spread, part, precision=lax.Precision.HIGHEST, preferred_element_type=F32)
        return jnp.sum(jnp.where(pick, wide_part, 0.0), axis=1, keepdims=True)

    rate = column(columns[:, modes : 2 * modes])
    seed = column(columns[:, 2 * modes : 3 * modes])
    res = column(columns[:, :modes])
    weight = res * jnp.sqrt(rate + 1.0 / seq_len)
    seed_int = (seed + 0.5).astype(jnp.int32)
    rate_b = jnp.broadcast_to(rate, (slab * modes, LANES))
    seed_b = jnp.broadcast_to(seed_int, (slab * modes, LANES))
    lane = iota((slab * modes, LANES), 1)
    up = power(rate_b, seed_b, lane)
    down = power(rate_b, seed_b, LANES - 1 - lane)
    for place, part in enumerate((*up, *down)):
        high, low = split(part)
        bank[2 * place] = high
        bank[2 * place + 1] = low
    kernel_head = jnp.sum((up[0] * weight).reshape(slab, modes, LANES), axis=1)
    kernel_head = kernel_head + jnp.where(iota((slab, LANES), 1) == 0, taps[9], 0.0)

    upper = iota((LANES, LANES), 1) >= iota((LANES, LANES), 0)
    for c in range(slab):
        line = jnp.broadcast_to(kernel_head[c : c + 1], (LANES, LANES))
        rolled = pltpu.roll(line, 0, 1, stride=1, stride_axis=0)
        high, low = split(jnp.where(upper, rolled, 0.0))
        toeplitz[0, c] = high
        toeplitz[1, c] = low

    eye = iota((wide, LANES), 0) == iota((wide, LANES), 1)
    step_row = iota((8, LANES), 0)
    steps = jnp.where(step_row == 6, 1, LANES * (1 << jnp.minimum(step_row, 5)))
    for g in range(groups):
        def row(part):
            piece = jnp.broadcast_to(part[g * wide : (g + 1) * wide], (wide, LANES))
            return jnp.sum(jnp.where(eye, piece, 0.0), axis=0, keepdims=True)

        rate_row = jnp.broadcast_to(row(rate), (8, LANES))
        seed_row = jnp.broadcast_to((row(seed) + 0.5).astype(jnp.int32), (8, LANES))
        weight_row = row(weight)
        re, im = power(rate_row, seed_row, steps)
        scale = jnp.where(step_row == 6, jnp.broadcast_to(weight_row, (8, LANES)), 1.0)
        state_rows[g, 0] = re * scale
        state_rows[g, 1] = im * scale

    diag[...] = jnp.zeros_like(diag)

    wait_bytes(tok.at[pl.ds(0, chunks - 1)], tok_sems.at[0, 1])
    own_half = tok.at[pl.ds(pl.multiple_of(fsdp * chunks, chunks), chunks)]
    send(own_half, own_half, tok_sems.at[1], (1 - fsdp, ctx))
    lane_c = iota((slab, LANES), 1)
    low_row = iota((LANES, LANES), 0)
    banks = vocab // LANES

    def token_parts(r):
        token = tok[r]
        bank_of = token // LANES
        hot = jnp.where(low_row == token - bank_of * LANES, 1.0, 0.0).astype(BF16)
        return hot, bank_of

    UNROLL = 16

    def gather(base, step, carry):
        last_one, last_two = carry
        r0 = base + step * UNROLL
        parts = [token_parts(r0 + i) for i in range(UNROLL)]
        found = nn(table[...], jnp.concatenate([hot for hot, _ in parts], axis=1))
        for i in range(UNROLL):
            bank_of = parts[i][1]
            x = found[:slab, i * LANES : (i + 1) * LANES]
            for b in range(1, banks):
                x = jnp.where(bank_of == b, found[b * slab : (b + 1) * slab, i * LANES : (i + 1) * LANES], x)
            one = pltpu.roll(x, 1, 1)
            two = pltpu.roll(x, 2, 1)
            x1 = jnp.where(lane_c < 1, last_one, one)
            x2 = jnp.where(lane_c < 2, last_two, two)
            last_one, last_two = one, two
            q, k, v = (taps[3 * s] * x + taps[3 * s + 1] * x1 + taps[3 * s + 2] * x2 for s in range(3))
            at = pl.ds(pl.multiple_of((r0 + i) * slab, slab), slab)
            query[at, :] = q
            key[at, :] = k
            value[at, :] = v
            mix[at, :] = k * v
        return last_one, last_two

    zero = jnp.zeros((slab, LANES), F32)
    cot_in[me] = cot_out[me]
    per_sequence = chunks // UNROLL
    lax.fori_loop(0, per_sequence, functools.partial(gather, fsdp * chunks), (zero, zero))
    wait_bytes(own_half, tok_sems.at[1, 1])
    lax.fori_loop(0, per_sequence, functools.partial(gather, (1 - fsdp) * chunks), (zero, zero))

    row_in_seq = iota((rows, LANES), 0) % chunks

    def scan(re, im, g, backward):
        for j in range(max(1, (chunks - 1).bit_length())):
            shift = 1 << j
            amount = rows - shift if backward else shift
            keep = row_in_seq < chunks - shift if backward else row_in_seq >= shift
            old_re = jnp.where(keep, pltpu.roll(re, amount, 0), 0.0)
            old_im = jnp.where(keep, pltpu.roll(im, amount, 0), 0.0)
            a, b = state_rows[g, 0, j : j + 1, :], state_rows[g, 1, j : j + 1, :]
            re, im = re + a * old_re - b * old_im, im + a * old_im + b * old_re
        amount = rows - 1 if backward else 1
        keep = row_in_seq < chunks - 1 if backward else row_in_seq >= 1
        re = jnp.where(keep, pltpu.roll(re, amount, 0), 0.0)
        im = jnp.where(keep, pltpu.roll(im, amount, 0), 0.0)
        a, b = state_rows[g, 0, 6:7, :], state_rows[g, 1, 6:7, :]
        return a * re - b * im, -(a * im + b * re)

    def long_conv(source, target, backward):
        enter, leave = (0, 2) if backward else (2, 0)

        def per_group(g, _):
            base = g * GROUP
            for c in range(GROUP):
                at = pl.ds(pl.multiple_of(g * wide + c * modes, modes), modes)
                for half in range(2):
                    spot = slice(half * wide + c * modes, half * wide + (c + 1) * modes)
                    for part in range(2):
                        diag[part, spot, c * LANES : (c + 1) * LANES] = bank[2 * (enter + half) + part, at, :]
            local = jnp.zeros((rows, 2 * wide), F32)
            for c in range(GROUP):
                u = split(source[pl.ds(base + c, rows, stride=slab), :])
                staged[0, base + c], staged[1, base + c] = u
                at = slice(c * LANES, (c + 1) * LANES)
                local = local + three(nt, u, (diag[0, :, at], diag[1, :, at]))
            re, im = scan(local[:, :wide], local[:, wide:], g, backward)
            state = split(jnp.concatenate([re, im], axis=1))
            for c in range(GROUP):
                u = (staged[0, base + c], staged[1, base + c])
                at = slice(c * LANES, (c + 1) * LANES)
                band = (toeplitz[0, base + c], toeplitz[1, base + c])
                out = three(nt if backward else nn, u, band)
                mine = slice(c * modes, (c + 1) * modes)
                held = [jnp.concatenate([p[:, mine], p[:, wide + c * modes : wide + (c + 1) * modes]], axis=1) for p in state]
                rows_at = pl.ds(pl.multiple_of(g * wide + c * modes, modes), modes)
                pole = [
                    jnp.concatenate([bank[2 * leave + part, rows_at, :], bank[2 * (leave + 1) + part, rows_at, :]], axis=0)
                    for part in range(2)
                ]
                out = out + three(nn, held, pole)
                target[pl.ds(base + c, rows, stride=slab), :] = out
            return 0

        lax.fori_loop(0, groups, per_group, 0, unroll=2)

    long_conv(mix, long_out, False)

    def emit(place):
        at = slab_rows(place)
        q = query[at, :]
        encode(mixed_out, place, q * long_out[at, :])
        value_in = real(cot_in[place, :slab, :], cot_in[place, slab:, :])
        cot[at, :] = value_in
        mix[at, :] = value_in * q

    def emit_send(place, where):
        send(mixed_out.at[place, sent_rows], mixer.at[me, sent_rows], mixer_sems, where)

    most = pl.ds(0, rows - 1)
    wait_bytes(cot_in.at[most, sent_rows], cot_sems.at[1])
    def emit_step(step, _):
        for i in range(8):
            emit(step * 8 + i)
        return 0

    lax.fori_loop(0, rows // 8, emit_step, 0)
    each_peer(emit_send)
    mixer[me] = mixed_out[me]

    grad_mixed = query
    long_conv(mix, grad_mixed, True)

    def scatter(step, carry):
        next_one, next_two, total = carry
        r0 = rows - UNROLL - step * UNROLL
        fresh = (r0 % chunks) == chunks - UNROLL
        next_one = jnp.where(fresh, 0.0, next_one)
        next_two = jnp.where(fresh, 0.0, next_two)
        pieces, hots = [None] * UNROLL, [None] * UNROLL
        for i in reversed(range(UNROLL)):
            at = pl.ds(pl.multiple_of((r0 + i) * slab, slab), slab)
            gm = grad_mixed[at, :]
            gq = cot[at, :] * long_out[at, :]
            gk = gm * value[at, :]
            gv = gm * key[at, :]
            zeroth, first, second = (taps[j] * gq + taps[3 + j] * gk + taps[6 + j] * gv for j in range(3))
            one = pltpu.roll(first, LANES - 1, 1)
            two = pltpu.roll(second, LANES - 2, 1)
            gx = (
                zeroth
                + jnp.where(lane_c >= LANES - 1, next_one, one)
                + jnp.where(lane_c >= LANES - 2, next_two, two)
            )
            next_one, next_two = one, two
            hots[i], bank_of = token_parts(r0 + i)
            both = jnp.concatenate(split(gx), axis=0)
            mask = [jnp.where(bank_of == b, 1.0, 0.0).astype(BF16) for b in range(banks)]
            pieces[i] = jnp.concatenate([both * m for m in mask], axis=0)
        hot = jnp.concatenate(hots, axis=1)
        return next_one, next_two, total + nt(jnp.concatenate(pieces, axis=1), hot)

    _, _, total = lax.fori_loop(
        0, rows // UNROLL, scatter, (zero, zero, jnp.zeros((2 * slab * banks, LANES), F32))
    )
    step = 2 * slab
    pieces = [total[b * step : b * step + slab] + total[b * step + slab : (b + 1) * step] for b in range(banks)]
    gather_grad(
        pieces, chunks, quarters, columns_of, every, turn_sems, send_sems, recv_sems
    )
    wait_bytes(cot_in.at[most, sent_rows], cot_sems.at[0])
    wait_bytes(tok.at[pl.ds(0, chunks - 1)], tok_sems.at[0, 0])
    wait_bytes(own_half, tok_sems.at[1, 0])
    for end in range(2):
        wait_bytes(mixer.at[most, sent_rows], mixer_sems.at[end])


def run_block(tok, embedding, conv_taps, gains, residues, decays, seeds, cot, chunks):
    modes, width = residues.shape
    vocab = embedding.shape[0]
    rows = width // (embedding.shape[1] // chunks)
    slab = width // rows
    tall = rows * slab
    side = round(chunks ** (1 / 3))
    vmem = pl.BlockSpec(memory_space=pltpu.VMEM)
    hbm = pl.BlockSpec(memory_space=pl.ANY)
    dma = pltpu.SemaphoreType.DMA
    return pl.pallas_call(
        functools.partial(block_kernel, chunks, chunks * LANES),
        out_shape=(
            jax.ShapeDtypeStruct((rows, slab + 16, LANES), jnp.int16),
            jax.ShapeDtypeStruct((side,) * 3 + (LANES // 16 + 1, 16, LANES), jnp.int16),
        ),
        in_specs=[vmem, hbm, hbm, vmem, hbm, hbm, hbm, hbm],
        out_specs=(vmem, vmem),
        scratch_shapes=[pltpu.VMEM((tall, LANES), F32)] * 6
        + [pltpu.VMEM((rows, slab + 16, LANES), jnp.int16)] * 3
        + [
            pltpu.VMEM((rows, 1, LANES), jnp.int32),
            pltpu.VMEM((2, slab, LANES, LANES), BF16),
            pltpu.VMEM((vocab // LANES * slab, LANES), BF16),
            pltpu.VMEM((10, slab, LANES), F32),
            pltpu.VMEM((modes, LANES), F32),
            pltpu.VMEM((modes, LANES), F32),
            pltpu.VMEM((modes, LANES), jnp.int32),
            pltpu.VMEM((vocab, LANES), BF16),
            pltpu.VMEM((LANES, vocab), F32),
            pltpu.VMEM((3, 3, LANES), F32),
            pltpu.VMEM((8, slab * modes, LANES), BF16),
            pltpu.VMEM((2, slab, LANES, LANES), BF16),
            pltpu.VMEM((2, 2 * GROUP * modes, GROUP * LANES), BF16),
            pltpu.VMEM((slab // GROUP, 2, 8, LANES), F32),
            pltpu.VMEM((side, slab, LANES), F32),
            pltpu.VMEM((LANES, LANES), F32),
            dma((6,)), dma((2, 2)), dma((2,)), dma((2,)), dma((2, 3)), dma((3, 3, 3)), dma((3, 3, 3)),
        ],
        compiler_params=pltpu.CompilerParams(
            vmem_limit_bytes=56 * 1024 * 1024, collective_id=0, has_side_effects=True
        ),
        name="hyena_block",
    )(tok, embedding, conv_taps, gains, residues, decays, seeds, cot)


def finish_kernel(every, powers, mixer, grad_out, mixer_out):
    height = grad_out.shape[0]
    for z in range(every.shape[0]):
        for x in range(every.shape[1]):
            n = z * every.shape[1] + x
            grad_out[:, n * LANES : (n + 1) * LANES] = real(every[z, x, 0].reshape(height, LANES), powers[z, x, 0, 0])
    slab = mixer.shape[1] - 16
    for n in range(mixer.shape[0]):
        mixer_out[n * slab : (n + 1) * slab, :] = real(mixer[n, :slab, :], mixer[n, slab:, :])


def finish(mixer, every):
    a, b, c, tiles, height = every.shape[:5]
    blocks, slab = mixer.shape[0], mixer.shape[1] - 16
    tall = blocks * slab
    cuts = 1
    part = (tiles - 1) // cuts
    steps = c * cuts
    return pl.pallas_call(
        finish_kernel,
        grid=(steps,),
        out_shape=(
            jax.ShapeDtypeStruct((c * LANES, a * b * LANES), F32),
            jax.ShapeDtypeStruct((tall, LANES), F32),
        ),
        in_specs=[
            pl.BlockSpec((a, b, 1, part, height, LANES), lambda n: (0, 0, n // cuts, n % cuts, 0, 0)),
            pl.BlockSpec((a, b, 1, 1, height, LANES), lambda n: (0, 0, n // cuts, tiles - 1, 0, 0)),
            pl.BlockSpec((blocks // steps, *mixer.shape[1:]), lambda n: (n, 0, 0)),
        ],
        out_specs=(
            pl.BlockSpec((LANES // cuts, a * b * LANES), lambda n: (n, 0)),
            pl.BlockSpec((tall // steps, LANES), lambda n: (n, 0)),
        ),
        name="finish",
    )(every, every, mixer)


def body(token_ids, embedding, conv_taps, residues, decays, filter_seed, skip_gain, cotangent):
    ctx_size = lax.axis_size("ctx")
    width = conv_taps.shape[2]
    tok_block = token_ids.shape[1]
    packed = run_block(
        token_ids, embedding, conv_taps, skip_gain.reshape(-1, LANES),
        residues.T, decays.T, filter_seed.T, cotangent.reshape(width, tok_block), ctx_size,
    )
    grad, mixer = finish(*packed)
    return mixer.reshape(cotangent.shape), grad


def solution(mesh):
    placed = (P("fsdp", "ctx"), P(None, "fsdp"), P(), P(), P(), P(), P(), P("fsdp", None, "ctx"))
    return jax.shard_map(
        body,
        mesh=mesh,
        in_specs=placed,
        out_specs=(P("fsdp", None, "ctx"), P(None, "fsdp")),
        check_vma=False,
    )
```

```python
import functools
import math

import jax
import jax.numpy as jnp
from jax import lax
from jax.experimental import pallas as pl
from jax.experimental.pallas import tpu as pltpu
from jax.sharding import PartitionSpec as P

PERIOD = 4096
F32 = jnp.float32
BF16 = jnp.bfloat16
LANES = 128
GROUP = 8


def iota(shape, dim):
    return lax.broadcasted_iota(jnp.int32, shape, dim)


def split(value):
    high = value.astype(BF16)
    return high, (value - high.astype(F32)).astype(BF16)


def cis(phase):
    quarter = PERIOD // 4
    turn = (phase + quarter // 2) // quarter
    a = (phase - turn * quarter).astype(F32) * (2.0 * math.pi / PERIOD)
    b = a * a
    s = a * (1.0 + b * (-1 / 6 + b * (1 / 120 + b * (-1 / 5040 + b * (1 / 362880)))))
    c = 1.0 + b * (-0.5 + b * (1 / 24 + b * (-1 / 720 + b * (1 / 40320))))
    odd = turn % 2 == 1
    re = jnp.where(odd, s, c)
    im = jnp.where(odd, c, s)
    re = jnp.where((turn == 1) | (turn == 2), -re, re)
    im = jnp.where((turn == 2) | (turn == 3), -im, im)
    return re, im


def power(rate, seed, steps):
    mag = jnp.exp(-rate * steps.astype(F32))
    re, im = cis((seed * steps) % PERIOD)
    return mag * re, mag * im


def nn(a, b):
    return jnp.dot(a, b, preferred_element_type=F32)


def nt(a, b):
    return lax.dot_general(a, b, (((1,), (1,)), ((), ())), preferred_element_type=F32)


def three(dot, left, right):
    left_high, left_low = left
    right_high, right_low = right
    rows = left_high.shape[0]
    both = dot(jnp.concatenate([left_high, left_low], axis=0), right_high)
    return both[:rows] + both[rows:] + dot(left_high, right_low)


MESH = pl.DeviceIdType.MESH


LEVELS = 32767.0


def fixed(block):
    peak = jnp.maximum(jnp.max(jnp.abs(block), axis=0, keepdims=True), 1e-30)
    power_of = jnp.ceil(jnp.log2(peak * (1.0 / LEVELS)))
    code = jnp.clip(jnp.round(block * jnp.exp2(-power_of)), -LEVELS, LEVELS)
    return code.astype(jnp.int32).astype(jnp.int16), power_of


def real(code, power_of):
    scale = jnp.exp2(power_of.astype(jnp.int32)[:1].astype(F32))
    return code.astype(jnp.int32).astype(F32) * scale


def gather_grad(pieces, chunks, quarters, columns_of, every, turn_sems, send_sems, recv_sems):
    sides = every.shape[:3]
    ctx = lax.axis_index("ctx")
    fsdp = lax.axis_index("fsdp")
    spans = (sides[1] * sides[2], sides[2], 1)
    here = [lax.rem(ctx // span, side) for span, side in zip(spans, sides)]
    slab = pieces[0].shape[0]
    sent = []

    def neighbour(axis, hop):
        there = lax.rem(here[axis] + hop + sides[axis], sides[axis])
        return there, (fsdp, ctx + (there - here[axis]) * spans[axis])

    def send(source, target, sender, receiver, where):
        made = pltpu.make_async_remote_copy(
            src_ref=source, dst_ref=target, send_sem=sender, recv_sem=receiver,
            device_id=where, device_id_type=MESH,
        )
        made.start()
        sent.append(made)

    def landed(place, sem):
        pltpu.make_async_copy(place, place, sem).wait()

    for j in range(sides[2]):
        quarters[j] = pieces[j]
    strip = pl.ds(pl.multiple_of(here[2] * slab, slab), slab)
    for n, hop in enumerate((1, -1, 2)):
        there, where = neighbour(2, hop)
        send(quarters.at[there], columns_of.at[strip], turn_sems.at[0, n], turn_sems.at[1, n], where)
    columns_of[strip, :] = quarters[here[2]]
    for n, hop in enumerate((-1, 1, 2)):
        there = neighbour(2, hop)[0]
        landed(columns_of.at[pl.ds(pl.multiple_of(there * slab, slab), slab)], turn_sems.at[1, n])
    block = columns_of[...].T
    code, power_of = fixed(block)
    tiles, height = every.shape[3] - 1, every.shape[4]
    every[here[0], here[1], here[2], :tiles] = code.reshape(tiles, height, LANES)
    every[here[0], here[1], here[2], tiles] = jnp.broadcast_to(power_of, (height, LANES)).astype(jnp.int32).astype(jnp.int16)

    def at(axis, hop, done, part):
        index = []
        for n in range(3):
            if n == axis:
                index.append(pl.ds(lax.rem(here[n] + hop + sides[n], sides[n]), 1))
            elif n in done:
                index.append(slice(None))
            else:
                index.append(pl.ds(here[n], 1))
        third = (tiles + 1) // 3
        return every.at[(*index, pl.ds(part * third, third))]

    for phase in range(3):
        plan = [((2 - part + phase) % 3, [(2 - part + n) % 3 for n in range(phase)]) for part in range(3)]
        for part, (axis, done) in enumerate(plan):
            mine = at(axis, 0, done, part)
            for n, hop in enumerate((2, 1, -1)):
                send(mine, mine, send_sems.at[part, phase, n], recv_sems.at[part, phase, n], neighbour(axis, hop)[1])
        for part, (axis, done) in enumerate(plan):
            for n, hop in enumerate((2, -1, 1)):
                landed(at(axis, hop, done, part), recv_sems.at[part, phase, n])
    for made in sent:
        made.wait_send()


def block_kernel(
    chunks, seq_len,
    tok_mine, embedding, conv_taps, gains, residue_all, decay_all, seed_all, cot_mine,
    mixer, every,
    query, key, value, mix, long_out, cot, cot_away, cot_out, cot_in, mixed_out, mixed_in, tok,
    staged, table, taps, residues, decays, seeds, raw_table, turned, raw_taps,
    bank, toeplitz, diag, state_rows, quarters, columns_of,
    load_sems, tok_sems, cot_sems, mixer_sems, relay_sems, own_sem, turn_sems, send_sems, recv_sems,
):
    vocab = embedding.shape[0]
    rows = tok.shape[0]
    slab = cot.shape[0] // rows
    modes = residues.shape[0]
    groups = slab // GROUP
    wide = GROUP * modes
    ctx = lax.axis_index("ctx")
    fsdp = lax.axis_index("fsdp")
    me = fsdp * chunks + ctx
    per_tile = LANES // slab

    def slab_rows(index):
        return pl.ds(pl.multiple_of(index * slab, slab), slab)

    sibling = (1 - fsdp, ctx)

    def each_peer(action):
        def step(i, _):
            there = ctx + i
            there = jnp.where(there >= chunks, there - chunks, there)
            action(there, (fsdp, there))
            return 0

        lax.fori_loop(1, chunks, step, 0, unroll=7)

    def send(source, target, sems, where):
        pltpu.make_async_remote_copy(
            src_ref=source, dst_ref=target, send_sem=sems.at[0], recv_sem=sems.at[1],
            device_id=where, device_id_type=MESH,
        ).start()

    barrier = pltpu.get_barrier_semaphore()
    load_cot = pltpu.make_async_copy(cot_mine, cot, load_sems.at[5])
    load_cot.start()
    pl.semaphore_signal(barrier, inc=1, device_id=sibling, device_id_type=MESH)
    each_peer(lambda place, where: pl.semaphore_signal(barrier, inc=1, device_id=where, device_id_type=MESH))

    lane_tile = pl.ds(pl.multiple_of(ctx // per_tile * LANES, LANES), LANES)
    wide_tile = pl.ds(pl.multiple_of(me // per_tile * LANES, LANES), LANES)
    loads = [
        pltpu.make_async_copy(source, target, load_sems.at[n])
        for n, (source, target) in enumerate((
            (residue_all.at[:, wide_tile], residues),
            (decay_all.at[:, wide_tile], decays),
            (seed_all.at[:, wide_tile], seeds),
            (conv_taps.at[:, :, wide_tile], raw_taps),
            (embedding.at[:, lane_tile], raw_table),
        ))
    ]
    for load in loads:
        load.start()

    sent_rows = pl.ds(0, slab + 2)

    def encode(target, block):
        code, power_of = fixed(block)
        target[:slab, :] = code
        target[slab:, :] = jnp.broadcast_to(power_of, (16, LANES)).astype(jnp.int32).astype(jnp.int16)

    tok[me] = tok_mine[...]
    load_cot.wait()

    def pack(half, target, step, _):
        for i in range(16):
            c = step * 16 + i
            encode(target.at[c], cot[slab_rows(half * chunks + c), :])
        return 0

    lax.fori_loop(0, chunks // 16, functools.partial(pack, 1 - fsdp, cot_away), 0)
    pl.semaphore_wait(barrier, chunks)
    send(cot_away.at[:, sent_rows], cot_out.at[:, fsdp, sent_rows], relay_sems.at[0], sibling)
    each_peer(lambda place, where: send(tok_mine, tok.at[me], tok_sems.at[0], where))
    lax.fori_loop(0, chunks // 16, functools.partial(pack, fsdp, cot_out.at[:, fsdp]), 0)

    def wait_bytes(ref, sem):
        pltpu.make_async_copy(ref, ref, sem).wait()

    wait_bytes(cot_out.at[:, 1 - fsdp, sent_rows], relay_sems.at[0, 1])
    each_peer(
        lambda place, where: send(cot_out.at[place, :, sent_rows], cot_in.at[ctx, :, sent_rows], cot_sems, where)
    )
    cot_in[ctx] = cot_out[ctx]
    for load in loads:
        load.wait()
    sub = pl.ds(pl.multiple_of(lax.rem(ctx, per_tile) * slab, slab), slab)
    turned[...] = raw_table[...].astype(F32).T
    for b in range(vocab // LANES):
        table[b * slab : (b + 1) * slab, :] = turned[sub, b * LANES : (b + 1) * LANES].astype(BF16)
    pieces = [residues[...], decays[...], seeds[...].astype(F32)]
    pieces += [raw_taps[s, j : j + 1, :] for s in range(3) for j in range(3)]
    pieces.append(gains[pl.ds(me // per_tile, 1), :])
    pieces.append(jnp.zeros((LANES - 10 - 3 * modes, LANES), F32))
    turned[:, :LANES] = jnp.concatenate(pieces, axis=0).T
    columns = turned[sub, :LANES]
    for j in range(10):
        taps[j] = jnp.broadcast_to(columns[:, 3 * modes + j : 3 * modes + j + 1], (slab, LANES))

    spread = (iota((slab * modes, slab), 0) // modes == iota((slab * modes, slab), 1)).astype(F32)
    pick = iota((slab * modes, modes), 0) % modes == iota((slab * modes, modes), 1)

    def column(part):
        wide_part = jnp.dot(spread, part, precision=lax.Precision.HIGHEST, preferred_element_type=F32)
        return jnp.sum(jnp.where(pick, wide_part, 0.0), axis=1, keepdims=True)

    rate = column(columns[:, modes : 2 * modes])
    seed = column(columns[:, 2 * modes : 3 * modes])
    res = column(columns[:, :modes])
    weight = res * jnp.sqrt(rate + 1.0 / seq_len)
    seed_int = (seed + 0.5).astype(jnp.int32)
    rate_b = jnp.broadcast_to(rate, (slab * modes, LANES))
    seed_b = jnp.broadcast_to(seed_int, (slab * modes, LANES))
    lane = iota((slab * modes, LANES), 1)
    up = power(rate_b, seed_b, lane)
    down = power(rate_b, seed_b, LANES - 1 - lane)
    for place, part in enumerate((*up, *down)):
        high, low = split(part)
        bank[2 * place] = high
        bank[2 * place + 1] = low
    kernel_head = jnp.sum((up[0] * weight).reshape(slab, modes, LANES), axis=1)
    kernel_head = kernel_head + jnp.where(iota((slab, LANES), 1) == 0, taps[9], 0.0)

    upper = iota((LANES, LANES), 1) >= iota((LANES, LANES), 0)
    for c in range(slab):
        line = jnp.broadcast_to(kernel_head[c : c + 1], (LANES, LANES))
        rolled = pltpu.roll(line, 0, 1, stride=1, stride_axis=0)
        high, low = split(jnp.where(upper, rolled, 0.0))
        toeplitz[0, c] = high
        toeplitz[1, c] = low

    eye = iota((wide, LANES), 0) == iota((wide, LANES), 1)
    step_row = iota((8, LANES), 0)
    steps = jnp.where(step_row == 6, 1, LANES * (1 << jnp.minimum(step_row, 5)))
    for g in range(groups):
        def row(part):
            piece = jnp.broadcast_to(part[g * wide : (g + 1) * wide], (wide, LANES))
            return jnp.sum(jnp.where(eye, piece, 0.0), axis=0, keepdims=True)

        rate_row = jnp.broadcast_to(row(rate), (8, LANES))
        seed_row = jnp.broadcast_to((row(seed) + 0.5).astype(jnp.int32), (8, LANES))
        weight_row = row(weight)
        re, im = power(rate_row, seed_row, steps)
        scale = jnp.where(step_row == 6, jnp.broadcast_to(weight_row, (8, LANES)), 1.0)
        state_rows[g, 0] = re * scale
        state_rows[g, 1] = im * scale

    diag[...] = jnp.zeros_like(diag)

    wait_bytes(tok.at[pl.ds(0, chunks - 1)], tok_sems.at[0, 1])
    own_half = tok.at[pl.ds(pl.multiple_of(fsdp * chunks, chunks), chunks)]
    send(own_half, own_half, tok_sems.at[1], sibling)
    lane_c = iota((slab, LANES), 1)
    low_row = iota((LANES, LANES), 0)
    banks = vocab // LANES

    def token_parts(r):
        token = tok[r]
        bank_of = token // LANES
        hot = jnp.where(low_row == token - bank_of * LANES, 1.0, 0.0).astype(BF16)
        return hot, bank_of

    UNROLL = 16

    def gather(base, step, carry):
        last_one, last_two = carry
        r0 = base + step * UNROLL
        parts = [token_parts(r0 + i) for i in range(UNROLL)]
        found = nn(table[...], jnp.concatenate([hot for hot, _ in parts], axis=1))
        for i in range(UNROLL):
            bank_of = parts[i][1]
            x = found[:slab, i * LANES : (i + 1) * LANES]
            for b in range(1, banks):
                x = jnp.where(bank_of == b, found[b * slab : (b + 1) * slab, i * LANES : (i + 1) * LANES], x)
            one = pltpu.roll(x, 1, 1)
            two = pltpu.roll(x, 2, 1)
            x1 = jnp.where(lane_c < 1, last_one, one)
            x2 = jnp.where(lane_c < 2, last_two, two)
            last_one, last_two = one, two
            q, k, v = (taps[3 * s] * x + taps[3 * s + 1] * x1 + taps[3 * s + 2] * x2 for s in range(3))
            at = pl.ds(pl.multiple_of((r0 + i) * slab, slab), slab)
            query[at, :] = q
            key[at, :] = k
            value[at, :] = v
            mix[at, :] = k * v
        return last_one, last_two

    zero = jnp.zeros((slab, LANES), F32)
    per_sequence = chunks // UNROLL
    lax.fori_loop(0, per_sequence, functools.partial(gather, fsdp * chunks), (zero, zero))
    wait_bytes(own_half, tok_sems.at[1, 1])
    lax.fori_loop(0, per_sequence, functools.partial(gather, (1 - fsdp) * chunks), (zero, zero))

    row_in_seq = iota((rows, LANES), 0) % chunks

    def scan(re, im, g, backward):
        for j in range(max(1, (chunks - 1).bit_length())):
            shift = 1 << j
            amount = rows - shift if backward else shift
            keep = row_in_seq < chunks - shift if backward else row_in_seq >= shift
            old_re = jnp.where(keep, pltpu.roll(re, amount, 0), 0.0)
            old_im = jnp.where(keep, pltpu.roll(im, amount, 0), 0.0)
            a, b = state_rows[g, 0, j : j + 1, :], state_rows[g, 1, j : j + 1, :]
            re, im = re + a * old_re - b * old_im, im + a * old_im + b * old_re
        amount = rows - 1 if backward else 1
        keep = row_in_seq < chunks - 1 if backward else row_in_seq >= 1
        re = jnp.where(keep, pltpu.roll(re, amount, 0), 0.0)
        im = jnp.where(keep, pltpu.roll(im, amount, 0), 0.0)
        a, b = state_rows[g, 0, 6:7, :], state_rows[g, 1, 6:7, :]
        return a * re - b * im, -(a * im + b * re)

    def long_conv(source, target, backward):
        enter, leave = (0, 2) if backward else (2, 0)

        def per_group(g, _):
            base = g * GROUP
            for c in range(GROUP):
                at = pl.ds(pl.multiple_of(g * wide + c * modes, modes), modes)
                for half in range(2):
                    spot = slice(half * wide + c * modes, half * wide + (c + 1) * modes)
                    for part in range(2):
                        diag[part, spot, c * LANES : (c + 1) * LANES] = bank[2 * (enter + half) + part, at, :]
            local = jnp.zeros((rows, 2 * wide), F32)
            for c in range(GROUP):
                u = split(source[pl.ds(base + c, rows, stride=slab), :])
                staged[0, base + c], staged[1, base + c] = u
                at = slice(c * LANES, (c + 1) * LANES)
                local = local + three(nt, u, (diag[0, :, at], diag[1, :, at]))
            re, im = scan(local[:, :wide], local[:, wide:], g, backward)
            state = split(jnp.concatenate([re, im], axis=1))
            for c in range(GROUP):
                u = (staged[0, base + c], staged[1, base + c])
                at = slice(c * LANES, (c + 1) * LANES)
                band = (toeplitz[0, base + c], toeplitz[1, base + c])
                out = three(nt if backward else nn, u, band)
                mine = slice(c * modes, (c + 1) * modes)
                held = [jnp.concatenate([p[:, mine], p[:, wide + c * modes : wide + (c + 1) * modes]], axis=1) for p in state]
                rows_at = pl.ds(pl.multiple_of(g * wide + c * modes, modes), modes)
                pole = [
                    jnp.concatenate([bank[2 * leave + part, rows_at, :], bank[2 * (leave + 1) + part, rows_at, :]], axis=0)
                    for part in range(2)
                ]
                out = out + three(nn, held, pole)
                target[pl.ds(base + c, rows, stride=slab), :] = out
            return 0

        lax.fori_loop(0, groups, per_group, 0, unroll=2)

    long_conv(mix, long_out, False)

    def emit(seq, c):
        at = slab_rows(seq * chunks + c)
        q = query[at, :]
        encode(mixed_out.at[c, seq], q * long_out[at, :])
        value_in = real(cot_in[c, seq, :slab, :], cot_in[c, seq, slab:, :])
        cot[at, :] = value_in
        mix[at, :] = value_in * q

    most = pl.ds(0, chunks - 1)
    wait_bytes(cot_in.at[most, :, sent_rows], cot_sems.at[1])

    def emit_step(step, _):
        for i in range(4):
            for seq in range(2):
                emit(seq, step * 4 + i)
        return 0

    lax.fori_loop(0, chunks // 4, emit_step, 0)
    each_peer(
        lambda place, where: send(mixed_out.at[place, :, sent_rows], mixed_in.at[ctx, :, sent_rows], mixer_sems, where)
    )
    mixed_in[ctx] = mixed_out[ctx]

    grad_mixed = query
    long_conv(mix, grad_mixed, True)

    def scatter(step, carry):
        next_one, next_two, total = carry
        r0 = rows - UNROLL - step * UNROLL
        fresh = (r0 % chunks) == chunks - UNROLL
        next_one = jnp.where(fresh, 0.0, next_one)
        next_two = jnp.where(fresh, 0.0, next_two)
        pieces, hots = [None] * UNROLL, [None] * UNROLL
        for i in reversed(range(UNROLL)):
            at = pl.ds(pl.multiple_of((r0 + i) * slab, slab), slab)
            gm = grad_mixed[at, :]
            gq = cot[at, :] * long_out[at, :]
            gk = gm * value[at, :]
            gv = gm * key[at, :]
            zeroth, first, second = (taps[j] * gq + taps[3 + j] * gk + taps[6 + j] * gv for j in range(3))
            one = pltpu.roll(first, LANES - 1, 1)
            two = pltpu.roll(second, LANES - 2, 1)
            gx = (
                zeroth
                + jnp.where(lane_c >= LANES - 1, next_one, one)
                + jnp.where(lane_c >= LANES - 2, next_two, two)
            )
            next_one, next_two = one, two
            hots[i], bank_of = token_parts(r0 + i)
            both = jnp.concatenate(split(gx), axis=0)
            mask = [jnp.where(bank_of == b, 1.0, 0.0).astype(BF16) for b in range(banks)]
            pieces[i] = jnp.concatenate([both * m for m in mask], axis=0)
        hot = jnp.concatenate(hots, axis=1)
        return next_one, next_two, total + nt(jnp.concatenate(pieces, axis=1), hot)

    _, _, total = lax.fori_loop(
        0, rows // UNROLL, scatter, (zero, zero, jnp.zeros((2 * slab * banks, LANES), F32))
    )
    step = 2 * slab
    pieces = [total[b * step : b * step + slab] + total[b * step + slab : (b + 1) * step] for b in range(banks)]
    wait_bytes(mixed_in.at[most, :, sent_rows], mixer_sems.at[1])
    send(mixed_in.at[:, 1 - fsdp, sent_rows], mixer.at[fsdp, :, sent_rows], relay_sems.at[1], sibling)
    keep = pltpu.make_async_copy(mixed_in.at[:, fsdp, sent_rows], mixer.at[fsdp, :, sent_rows], own_sem)
    keep.start()
    gather_grad(
        pieces, chunks, quarters, columns_of, every, turn_sems, send_sems, recv_sems
    )
    wait_bytes(tok.at[pl.ds(0, chunks - 1)], tok_sems.at[0, 0])
    wait_bytes(own_half, tok_sems.at[1, 0])
    wait_bytes(cot_away.at[:, sent_rows], relay_sems.at[0, 0])
    wait_bytes(cot_in.at[most, :, sent_rows], cot_sems.at[0])
    wait_bytes(mixed_in.at[most, :, sent_rows], mixer_sems.at[0])
    keep.wait()
    for end in range(2):
        wait_bytes(mixer.at[1 - fsdp, :, sent_rows], relay_sems.at[1, end])


def run_block(tok, embedding, conv_taps, gains, residues, decays, seeds, cot, chunks):
    modes, width = residues.shape
    vocab = embedding.shape[0]
    rows = width // (embedding.shape[1] // chunks)
    slab = width // rows
    tall = rows * slab
    side = round(chunks ** (1 / 3))
    vmem = pl.BlockSpec(memory_space=pltpu.VMEM)
    hbm = pl.BlockSpec(memory_space=pl.ANY)
    dma = pltpu.SemaphoreType.DMA
    return pl.pallas_call(
        functools.partial(block_kernel, chunks, chunks * LANES),
        out_shape=(
            jax.ShapeDtypeStruct((2, chunks, slab + 16, LANES), jnp.int16),
            jax.ShapeDtypeStruct((side,) * 3 + (LANES // 16 + 1, 16, LANES), jnp.int16),
        ),
        in_specs=[vmem, hbm, hbm, vmem, hbm, hbm, hbm, hbm],
        out_specs=(vmem, vmem),
        scratch_shapes=[pltpu.VMEM((tall, LANES), F32)] * 6
        + [pltpu.VMEM((chunks, slab + 16, LANES), jnp.int16)]
        + [pltpu.VMEM((chunks, 2, slab + 16, LANES), jnp.int16)] * 4
        + [
            pltpu.VMEM((rows, 1, LANES), jnp.int32),
            pltpu.VMEM((2, slab, LANES, LANES), BF16),
            pltpu.VMEM((vocab // LANES * slab, LANES), BF16),
            pltpu.VMEM((10, slab, LANES), F32),
            pltpu.VMEM((modes, LANES), F32),
            pltpu.VMEM((modes, LANES), F32),
            pltpu.VMEM((modes, LANES), jnp.int32),
            pltpu.VMEM((vocab, LANES), BF16),
            pltpu.VMEM((LANES, vocab), F32),
            pltpu.VMEM((3, 3, LANES), F32),
            pltpu.VMEM((8, slab * modes, LANES), BF16),
            pltpu.VMEM((2, slab, LANES, LANES), BF16),
            pltpu.VMEM((2, 2 * GROUP * modes, GROUP * LANES), BF16),
            pltpu.VMEM((slab // GROUP, 2, 8, LANES), F32),
            pltpu.VMEM((side, slab, LANES), F32),
            pltpu.VMEM((LANES, LANES), F32),
            dma((6,)), dma((2, 2)), dma((2,)), dma((2,)), dma((2, 2)), dma, dma((2, 3)), dma((3, 3, 3)), dma((3, 3, 3)),
        ],
        compiler_params=pltpu.CompilerParams(
            vmem_limit_bytes=56 * 1024 * 1024, collective_id=0, has_side_effects=True
        ),
        name="hyena_block",
    )(tok, embedding, conv_taps, gains, residues, decays, seeds, cot)


def finish_kernel(every, powers, mixer, grad_out, mixer_out):
    height = grad_out.shape[0]
    for z in range(every.shape[0]):
        for x in range(every.shape[1]):
            n = z * every.shape[1] + x
            grad_out[:, n * LANES : (n + 1) * LANES] = real(every[z, x, 0].reshape(height, LANES), powers[z, x, 0, 0])
    slab = mixer.shape[1] - 16
    for n in range(mixer.shape[0]):
        mixer_out[n * slab : (n + 1) * slab, :] = real(mixer[n, :slab, :], mixer[n, slab:, :])


def finish(mixer, every):
    a, b, c, tiles, height = every.shape[:5]
    mixer = mixer.reshape(-1, *mixer.shape[2:])
    blocks, slab = mixer.shape[0], mixer.shape[1] - 16
    tall = blocks * slab
    cuts = 1
    part = (tiles - 1) // cuts
    steps = c * cuts
    return pl.pallas_call(
        finish_kernel,
        grid=(steps,),
        out_shape=(
            jax.ShapeDtypeStruct((c * LANES, a * b * LANES), F32),
            jax.ShapeDtypeStruct((tall, LANES), F32),
        ),
        in_specs=[
            pl.BlockSpec((a, b, 1, part, height, LANES), lambda n: (0, 0, n // cuts, n % cuts, 0, 0)),
            pl.BlockSpec((a, b, 1, 1, height, LANES), lambda n: (0, 0, n // cuts, tiles - 1, 0, 0)),
            pl.BlockSpec((blocks // steps, *mixer.shape[1:]), lambda n: (n, 0, 0)),
        ],
        out_specs=(
            pl.BlockSpec((LANES // cuts, a * b * LANES), lambda n: (n, 0)),
            pl.BlockSpec((tall // steps, LANES), lambda n: (n, 0)),
        ),
        name="finish",
    )(every, every, mixer)


def body(token_ids, embedding, conv_taps, residues, decays, filter_seed, skip_gain, cotangent):
    ctx_size = lax.axis_size("ctx")
    width = conv_taps.shape[2]
    tok_block = token_ids.shape[1]
    packed = run_block(
        token_ids, embedding, conv_taps, skip_gain.reshape(-1, LANES),
        residues.T, decays.T, filter_seed.T, cotangent.reshape(width, tok_block), ctx_size,
    )
    grad, mixer = finish(*packed)
    return mixer.reshape(cotangent.shape), grad


def solution(mesh):
    placed = (P("fsdp", "ctx"), P(None, "fsdp"), P(), P(), P(), P(), P(), P("fsdp", None, "ctx"))
    return jax.shard_map(
        body,
        mesh=mesh,
        in_specs=placed,
        out_specs=(P("fsdp", None, "ctx"), P(None, "fsdp")),
        check_vma=False,
    )
```

```python
import functools
import math

import jax
import jax.numpy as jnp
from jax import lax
from jax.experimental import pallas as pl
from jax.experimental.pallas import tpu as pltpu
from jax.sharding import PartitionSpec as P

PERIOD = 4096
F32 = jnp.float32
BF16 = jnp.bfloat16
LANES = 128
GROUP = 8


def iota(shape, dim):
    return lax.broadcasted_iota(jnp.int32, shape, dim)


def split(value):
    high = value.astype(BF16)
    return high, (value - high.astype(F32)).astype(BF16)


def cis(phase):
    quarter = PERIOD // 4
    turn = (phase + quarter // 2) // quarter
    a = (phase - turn * quarter).astype(F32) * (2.0 * math.pi / PERIOD)
    b = a * a
    s = a * (1.0 + b * (-1 / 6 + b * (1 / 120 + b * (-1 / 5040 + b * (1 / 362880)))))
    c = 1.0 + b * (-0.5 + b * (1 / 24 + b * (-1 / 720 + b * (1 / 40320))))
    odd = turn % 2 == 1
    re = jnp.where(odd, s, c)
    im = jnp.where(odd, c, s)
    re = jnp.where((turn == 1) | (turn == 2), -re, re)
    im = jnp.where((turn == 2) | (turn == 3), -im, im)
    return re, im


def power(rate, seed, steps):
    mag = jnp.exp(-rate * steps.astype(F32))
    re, im = cis((seed * steps) % PERIOD)
    return mag * re, mag * im


def nn(a, b):
    return jnp.dot(a, b, preferred_element_type=F32)


def nt(a, b):
    return lax.dot_general(a, b, (((1,), (1,)), ((), ())), preferred_element_type=F32)


def three(dot, left, right):
    left_high, left_low = left
    right_high, right_low = right
    rows = left_high.shape[0]
    both = dot(jnp.concatenate([left_high, left_low], axis=0), right_high)
    return both[:rows] + both[rows:] + dot(left_high, right_low)


MESH = pl.DeviceIdType.MESH


LEVELS = 32767.0


def fixed(block):
    peak = jnp.maximum(jnp.max(jnp.abs(block), axis=0, keepdims=True), 1e-30)
    power_of = jnp.ceil(jnp.log2(peak * (1.0 / LEVELS)))
    code = jnp.clip(jnp.round(block * jnp.exp2(-power_of)), -LEVELS, LEVELS)
    return code.astype(jnp.int32).astype(jnp.int16), power_of


def real(code, power_of):
    scale = jnp.exp2(power_of.astype(jnp.int32)[:1].astype(F32))
    return code.astype(jnp.int32).astype(F32) * scale


def gather_grad(pieces, chunks, quarters, columns_of, every, turn_sems, send_sems, recv_sems):
    sides = every.shape[:3]
    ctx = lax.axis_index("ctx")
    fsdp = lax.axis_index("fsdp")
    spans = (sides[1] * sides[2], sides[2], 1)
    here = [lax.rem(ctx // span, side) for span, side in zip(spans, sides)]
    slab = pieces[0].shape[0]
    sent = []

    def neighbour(axis, hop):
        there = lax.rem(here[axis] + hop + sides[axis], sides[axis])
        return there, (fsdp, ctx + (there - here[axis]) * spans[axis])

    def send(source, target, sender, receiver, where):
        made = pltpu.make_async_remote_copy(
            src_ref=source, dst_ref=target, send_sem=sender, recv_sem=receiver,
            device_id=where, device_id_type=MESH,
        )
        made.start()
        sent.append(made)

    def landed(place, sem):
        pltpu.make_async_copy(place, place, sem).wait()

    for j in range(sides[2]):
        quarters[j] = pieces[j]
    strip = pl.ds(pl.multiple_of(here[2] * slab, slab), slab)
    for n, hop in enumerate((1, -1, 2)):
        there, where = neighbour(2, hop)
        send(quarters.at[there], columns_of.at[strip], turn_sems.at[0, n], turn_sems.at[1, n], where)
    columns_of[strip, :] = quarters[here[2]]
    for n, hop in enumerate((-1, 1, 2)):
        there = neighbour(2, hop)[0]
        landed(columns_of.at[pl.ds(pl.multiple_of(there * slab, slab), slab)], turn_sems.at[1, n])
    block = columns_of[...].T
    code, power_of = fixed(block)
    tiles, height = every.shape[3] - 1, every.shape[4]
    every[here[0], here[1], here[2], :tiles] = code.reshape(tiles, height, LANES)
    every[here[0], here[1], here[2], tiles] = jnp.broadcast_to(power_of, (height, LANES)).astype(jnp.int32).astype(jnp.int16)

    def at(axis, hop, done, part):
        index = []
        for n in range(3):
            if n == axis:
                index.append(pl.ds(lax.rem(here[n] + hop + sides[n], sides[n]), 1))
            elif n in done:
                index.append(slice(None))
            else:
                index.append(pl.ds(here[n], 1))
        third = (tiles + 1) // 3
        return every.at[(*index, pl.ds(part * third, third))]

    for phase in range(3):
        plan = [((2 - part + phase) % 3, [(2 - part + n) % 3 for n in range(phase)]) for part in range(3)]
        for part, (axis, done) in enumerate(plan):
            mine = at(axis, 0, done, part)
            for n, hop in enumerate((2, 1, -1)):
                send(mine, mine, send_sems.at[part, phase, n], recv_sems.at[part, phase, n], neighbour(axis, hop)[1])
        for part, (axis, done) in enumerate(plan):
            for n, hop in enumerate((2, -1, 1)):
                landed(at(axis, hop, done, part), recv_sems.at[part, phase, n])
    for made in sent:
        made.wait_send()


def block_kernel(
    chunks, seq_len,
    tok_mine, embedding, conv_taps, gains, residue_all, decay_all, seed_all, cot_mine,
    mixer, every,
    query, key, value, mix, long_out, cot, cot_out, cot_in, mixed_out, tok,
    staged, table, taps, residues, decays, seeds, raw_table, turned, raw_taps,
    bank, toeplitz, diag, state_rows, quarters, columns_of,
    load_sems, tok_sems, cot_sems, mixer_sems, turn_sems, send_sems, recv_sems,
):
    vocab = embedding.shape[0]
    rows = tok.shape[0]
    slab = cot.shape[0] // rows
    modes = residues.shape[0]
    groups = slab // GROUP
    wide = GROUP * modes
    ctx = lax.axis_index("ctx")
    fsdp = lax.axis_index("fsdp")
    me = fsdp * chunks + ctx
    per_tile = LANES // slab

    def slab_rows(index):
        return pl.ds(pl.multiple_of(index * slab, slab), slab)

    def each_peer(action):
        action((1 - fsdp) * chunks + ctx, (1 - fsdp, ctx))

        def step(i, _):
            there = ctx + i
            there = jnp.where(there >= chunks, there - chunks, there)
            for side in (fsdp, 1 - fsdp):
                action(side * chunks + there, (side, there))
            return 0

        lax.fori_loop(1, chunks, step, 0, unroll=7)

    def send(source, target, sems, where):
        pltpu.make_async_remote_copy(
            src_ref=source, dst_ref=target, send_sem=sems.at[0], recv_sem=sems.at[1],
            device_id=where, device_id_type=MESH,
        ).start()

    barrier = pltpu.get_barrier_semaphore()
    load_cot = pltpu.make_async_copy(cot_mine, cot, load_sems.at[5])
    load_cot.start()
    each_peer(lambda place, where: pl.semaphore_signal(barrier, inc=1, device_id=where, device_id_type=MESH))

    lane_tile = pl.ds(pl.multiple_of(ctx // per_tile * LANES, LANES), LANES)
    wide_tile = pl.ds(pl.multiple_of(me // per_tile * LANES, LANES), LANES)
    loads = [
        pltpu.make_async_copy(source, target, load_sems.at[n])
        for n, (source, target) in enumerate((
            (residue_all.at[:, wide_tile], residues),
            (decay_all.at[:, wide_tile], decays),
            (seed_all.at[:, wide_tile], seeds),
            (conv_taps.at[:, :, wide_tile], raw_taps),
            (embedding.at[:, lane_tile], raw_table),
        ))
    ]
    for load in loads:
        load.start()

    sent_rows = pl.ds(0, slab + 2)

    def encode(target, place, block):
        code, power_of = fixed(block)
        target[place, :slab, :] = code
        target[place, slab:, :] = jnp.broadcast_to(power_of, (16, LANES)).astype(jnp.int32).astype(jnp.int16)

    own_tok = tok_mine[...]
    load_cot.wait()

    def pack(step, _):
        for i in range(16):
            r = step * 16 + i
            encode(cot_out, r, cot[slab_rows(r), :])
        return 0

    lax.fori_loop(0, rows // 16, pack, 0)
    pl.semaphore_wait(barrier, rows - 1)
    tok[me] = own_tok

    def send_tok(i, _):
        there = ctx + i
        there = jnp.where(there >= chunks, there - chunks, there)
        send(tok_mine, tok.at[me], tok_sems.at[0], (fsdp, there))
        return 0

    lax.fori_loop(1, chunks, send_tok, 0, unroll=7)
    def send_cot(place, where):
        send(cot_out.at[place, sent_rows], cot_in.at[me, sent_rows], cot_sems, where)

    each_peer(send_cot)

    def wait_bytes(ref, sem):
        pltpu.make_async_copy(ref, ref, sem).wait()

    for load in loads:
        load.wait()
    sub = pl.ds(pl.multiple_of(lax.rem(ctx, per_tile) * slab, slab), slab)
    turned[...] = raw_table[...].astype(F32).T
    for b in range(vocab // LANES):
        table[b * slab : (b + 1) * slab, :] = turned[sub, b * LANES : (b + 1) * LANES].astype(BF16)
    pieces = [residues[...], decays[...], seeds[...].astype(F32)]
    pieces += [raw_taps[s, j : j + 1, :] for s in range(3) for j in range(3)]
    pieces.append(gains[pl.ds(me // per_tile, 1), :])
    pieces.append(jnp.zeros((LANES - 10 - 3 * modes, LANES), F32))
    turned[:, :LANES] = jnp.concatenate(pieces, axis=0).T
    columns = turned[sub, :LANES]
    for j in range(10):
        taps[j] = jnp.broadcast_to(columns[:, 3 * modes + j : 3 * modes + j + 1], (slab, LANES))

    spread = (iota((slab * modes, slab), 0) // modes == iota((slab * modes, slab), 1)).astype(F32)
    pick = iota((slab * modes, modes), 0) % modes == iota((slab * modes, modes), 1)

    def column(part):
        wide_part = jnp.dot(spread, part, precision=lax.Precision.HIGHEST, preferred_element_type=F32)
        return jnp.sum(jnp.where(pick, wide_part, 0.0), axis=1, keepdims=True)

    rate = column(columns[:, modes : 2 * modes])
    seed = column(columns[:, 2 * modes : 3 * modes])
    res = column(columns[:, :modes])
    weight = res * jnp.sqrt(rate + 1.0 / seq_len)
    seed_int = (seed + 0.5).astype(jnp.int32)
    rate_b = jnp.broadcast_to(rate, (slab * modes, LANES))
    seed_b = jnp.broadcast_to(seed_int, (slab * modes, LANES))
    lane = iota((slab * modes, LANES), 1)
    up = power(rate_b, seed_b, lane)
    down = power(rate_b, seed_b, LANES - 1 - lane)
    for place, part in enumerate((*up, *down)):
        high, low = split(part)
        bank[2 * place] = high
        bank[2 * place + 1] = low
    kernel_head = jnp.sum((up[0] * weight).reshape(slab, modes, LANES), axis=1)
    kernel_head = kernel_head + jnp.where(iota((slab, LANES), 1) == 0, taps[9], 0.0)

    upper = iota((LANES, LANES), 1) >= iota((LANES, LANES), 0)
    for c in range(slab):
        line = jnp.broadcast_to(kernel_head[c : c + 1], (LANES, LANES))
        rolled = pltpu.roll(line, 0, 1, stride=1, stride_axis=0)
        high, low = split(jnp.where(upper, rolled, 0.0))
        toeplitz[0, c] = high
        toeplitz[1, c] = low

    eye = iota((wide, LANES), 0) == iota((wide, LANES), 1)
    step_row = iota((8, LANES), 0)
    steps = jnp.where(step_row == 6, 1, LANES * (1 << jnp.minimum(step_row, 5)))
    for g in range(groups):
        def row(part):
            piece = jnp.broadcast_to(part[g * wide : (g + 1) * wide], (wide, LANES))
            return jnp.sum(jnp.where(eye, piece, 0.0), axis=0, keepdims=True)

        rate_row = jnp.broadcast_to(row(rate), (8, LANES))
        seed_row = jnp.broadcast_to((row(seed) + 0.5).astype(jnp.int32), (8, LANES))
        weight_row = row(weight)
        re, im = power(rate_row, seed_row, steps)
        scale = jnp.where(step_row == 6, jnp.broadcast_to(weight_row, (8, LANES)), 1.0)
        state_rows[g, 0] = re * scale
        state_rows[g, 1] = im * scale

    diag[...] = jnp.zeros_like(diag)

    wait_bytes(tok.at[pl.ds(0, chunks - 1)], tok_sems.at[0, 1])
    own_half = tok.at[pl.ds(pl.multiple_of(fsdp * chunks, chunks), chunks)]
    send(own_half, own_half, tok_sems.at[1], (1 - fsdp, ctx))
    lane_c = iota((slab, LANES), 1)
    low_row = iota((LANES, LANES), 0)
    banks = vocab // LANES

    def token_parts(r):
        token = tok[r]
        bank_of = token // LANES
        hot = jnp.where(low_row == token - bank_of * LANES, 1.0, 0.0).astype(BF16)
        return hot, bank_of

    UNROLL = 32

    def gather(base, step, carry):
        last_one, last_two = carry
        r0 = base + step * UNROLL
        parts = [token_parts(r0 + i) for i in range(UNROLL)]
        found = nn(table[...], jnp.concatenate([hot for hot, _ in parts], axis=1))
        for i in range(UNROLL):
            bank_of = parts[i][1]
            x = found[:slab, i * LANES : (i + 1) * LANES]
            for b in range(1, banks):
                x = jnp.where(bank_of == b, found[b * slab : (b + 1) * slab, i * LANES : (i + 1) * LANES], x)
            one = pltpu.roll(x, 1, 1)
            two = pltpu.roll(x, 2, 1)
            x1 = jnp.where(lane_c < 1, last_one, one)
            x2 = jnp.where(lane_c < 2, last_two, two)
            last_one, last_two = one, two
            q, k, v = (taps[3 * s] * x + taps[3 * s + 1] * x1 + taps[3 * s + 2] * x2 for s in range(3))
            at = pl.ds(pl.multiple_of((r0 + i) * slab, slab), slab)
            query[at, :] = q
            key[at, :] = k
            value[at, :] = v
            mix[at, :] = k * v
        return last_one, last_two

    zero = jnp.zeros((slab, LANES), F32)
    cot_in[me] = cot_out[me]
    per_sequence = chunks // UNROLL
    lax.fori_loop(0, per_sequence, functools.partial(gather, fsdp * chunks), (zero, zero))
    wait_bytes(own_half, tok_sems.at[1, 1])
    lax.fori_loop(0, per_sequence, functools.partial(gather, (1 - fsdp) * chunks), (zero, zero))

    row_in_seq = iota((rows, LANES), 0) % chunks

    def scan(re, im, g, backward):
        for j in range(max(1, (chunks - 1).bit_length())):
            shift = 1 << j
            amount = rows - shift if backward else shift
            keep = row_in_seq < chunks - shift if backward else row_in_seq >= shift
            old_re = jnp.where(keep, pltpu.roll(re, amount, 0), 0.0)
            old_im = jnp.where(keep, pltpu.roll(im, amount, 0), 0.0)
            a, b = state_rows[g, 0, j : j + 1, :], state_rows[g, 1, j : j + 1, :]
            re, im = re + a * old_re - b * old_im, im + a * old_im + b * old_re
        amount = rows - 1 if backward else 1
        keep = row_in_seq < chunks - 1 if backward else row_in_seq >= 1
        re = jnp.where(keep, pltpu.roll(re, amount, 0), 0.0)
        im = jnp.where(keep, pltpu.roll(im, amount, 0), 0.0)
        a, b = state_rows[g, 0, 6:7, :], state_rows[g, 1, 6:7, :]
        return a * re - b * im, -(a * im + b * re)

    def long_conv(source, target, backward):
        enter, leave = (0, 2) if backward else (2, 0)

        def per_group(g, _):
            base = g * GROUP
            for c in range(GROUP):
                at = pl.ds(pl.multiple_of(g * wide + c * modes, modes), modes)
                for half in range(2):
                    spot = slice(half * wide + c * modes, half * wide + (c + 1) * modes)
                    for part in range(2):
                        diag[part, spot, c * LANES : (c + 1) * LANES] = bank[2 * (enter + half) + part, at, :]
            local = jnp.zeros((rows, 2 * wide), F32)
            for c in range(GROUP):
                u = split(source[pl.ds(base + c, rows, stride=slab), :])
                staged[0, base + c], staged[1, base + c] = u
                at = slice(c * LANES, (c + 1) * LANES)
                local = local + three(nt, u, (diag[0, :, at], diag[1, :, at]))
            re, im = scan(local[:, :wide], local[:, wide:], g, backward)
            state = split(jnp.concatenate([re, im], axis=1))
            for c in range(GROUP):
                u = (staged[0, base + c], staged[1, base + c])
                at = slice(c * LANES, (c + 1) * LANES)
                band = (toeplitz[0, base + c], toeplitz[1, base + c])
                out = three(nt if backward else nn, u, band)
                mine = slice(c * modes, (c + 1) * modes)
                held = [jnp.concatenate([p[:, mine], p[:, wide + c * modes : wide + (c + 1) * modes]], axis=1) for p in state]
                rows_at = pl.ds(pl.multiple_of(g * wide + c * modes, modes), modes)
                pole = [
                    jnp.concatenate([bank[2 * leave + part, rows_at, :], bank[2 * (leave + 1) + part, rows_at, :]], axis=0)
                    for part in range(2)
                ]
                out = out + three(nn, held, pole)
                target[pl.ds(base + c, rows, stride=slab), :] = out
            return 0

        lax.fori_loop(0, groups, per_group, 0, unroll=True)

    long_conv(mix, long_out, False)

    def emit(step, _):
        for i in range(8):
            r = step * 8 + i
            at = slab_rows(r)
            encode(mixed_out, r, query[at, :] * long_out[at, :])
        return 0

    def weigh(step, _):
        for i in range(8):
            r = step * 8 + i
            at = slab_rows(r)
            value_in = real(cot_in[r, :slab, :], cot_in[r, slab:, :])
            cot[at, :] = value_in
            mix[at, :] = value_in * query[at, :]
        return 0

    def send_mixed(place, where):
        send(mixed_out.at[place, sent_rows], mixer.at[me, sent_rows], mixer_sems, where)

    lax.fori_loop(0, rows // 8, emit, 0)
    each_peer(send_mixed)
    mixer[me] = mixed_out[me]
    most = pl.ds(0, rows - 1)
    wait_bytes(cot_in.at[most, sent_rows], cot_sems.at[1])
    lax.fori_loop(0, rows // 8, weigh, 0)

    grad_mixed = query
    long_conv(mix, grad_mixed, True)

    def scatter(step, carry):
        next_one, next_two, total = carry
        r0 = rows - UNROLL - step * UNROLL
        fresh = (r0 % chunks) == chunks - UNROLL
        next_one = jnp.where(fresh, 0.0, next_one)
        next_two = jnp.where(fresh, 0.0, next_two)
        pieces, hots = [None] * UNROLL, [None] * UNROLL
        for i in reversed(range(UNROLL)):
            at = pl.ds(pl.multiple_of((r0 + i) * slab, slab), slab)
            gm = grad_mixed[at, :]
            gq = cot[at, :] * long_out[at, :]
            gk = gm * value[at, :]
            gv = gm * key[at, :]
            zeroth, first, second = (taps[j] * gq + taps[3 + j] * gk + taps[6 + j] * gv for j in range(3))
            one = pltpu.roll(first, LANES - 1, 1)
            two = pltpu.roll(second, LANES - 2, 1)
            gx = (
                zeroth
                + jnp.where(lane_c >= LANES - 1, next_one, one)
                + jnp.where(lane_c >= LANES - 2, next_two, two)
            )
            next_one, next_two = one, two
            hots[i], bank_of = token_parts(r0 + i)
            both = jnp.concatenate(split(gx), axis=0)
            mask = [jnp.where(bank_of == b, 1.0, 0.0).astype(BF16) for b in range(banks)]
            pieces[i] = jnp.concatenate([both * m for m in mask], axis=0)
        hot = jnp.concatenate(hots, axis=1)
        return next_one, next_two, total + nt(jnp.concatenate(pieces, axis=1), hot)

    _, _, total = lax.fori_loop(
        0, rows // UNROLL, scatter, (zero, zero, jnp.zeros((2 * slab * banks, LANES), F32))
    )
    step = 2 * slab
    pieces = [total[b * step : b * step + slab] + total[b * step + slab : (b + 1) * step] for b in range(banks)]
    gather_grad(
        pieces, chunks, quarters, columns_of, every, turn_sems, send_sems, recv_sems
    )
    wait_bytes(cot_in.at[most, sent_rows], cot_sems.at[0])
    wait_bytes(tok.at[pl.ds(0, chunks - 1)], tok_sems.at[0, 0])
    wait_bytes(own_half, tok_sems.at[1, 0])
    for end in range(2):
        wait_bytes(mixer.at[most, sent_rows], mixer_sems.at[end])


def run_block(tok, embedding, conv_taps, gains, residues, decays, seeds, cot, chunks):
    modes, width = residues.shape
    vocab = embedding.shape[0]
    rows = width // (embedding.shape[1] // chunks)
    slab = width // rows
    tall = rows * slab
    side = round(chunks ** (1 / 3))
    vmem = pl.BlockSpec(memory_space=pltpu.VMEM)
    hbm = pl.BlockSpec(memory_space=pl.ANY)
    dma = pltpu.SemaphoreType.DMA
    return pl.pallas_call(
        functools.partial(block_kernel, chunks, chunks * LANES),
        out_shape=(
            jax.ShapeDtypeStruct((rows, slab + 16, LANES), jnp.int16),
            jax.ShapeDtypeStruct((side,) * 3 + (LANES // 16 + 1, 16, LANES), jnp.int16),
        ),
        in_specs=[vmem, hbm, hbm, vmem, hbm, hbm, hbm, hbm],
        out_specs=(vmem, vmem),
        scratch_shapes=[pltpu.VMEM((tall, LANES), F32)] * 6
        + [pltpu.VMEM((rows, slab + 16, LANES), jnp.int16)] * 3
        + [
            pltpu.VMEM((rows, 1, LANES), jnp.int32),
            pltpu.VMEM((2, slab, LANES, LANES), BF16),
            pltpu.VMEM((vocab // LANES * slab, LANES), BF16),
            pltpu.VMEM((10, slab, LANES), F32),
            pltpu.VMEM((modes, LANES), F32),
            pltpu.VMEM((modes, LANES), F32),
            pltpu.VMEM((modes, LANES), jnp.int32),
            pltpu.VMEM((vocab, LANES), BF16),
            pltpu.VMEM((LANES, vocab), F32),
            pltpu.VMEM((3, 3, LANES), F32),
            pltpu.VMEM((8, slab * modes, LANES), BF16),
            pltpu.VMEM((2, slab, LANES, LANES), BF16),
            pltpu.VMEM((2, 2 * GROUP * modes, GROUP * LANES), BF16),
            pltpu.VMEM((slab // GROUP, 2, 8, LANES), F32),
            pltpu.VMEM((side, slab, LANES), F32),
            pltpu.VMEM((LANES, LANES), F32),
            dma((6,)), dma((2, 2)), dma((2,)), dma((2,)), dma((2, 3)), dma((3, 3, 3)), dma((3, 3, 3)),
        ],
        compiler_params=pltpu.CompilerParams(
            vmem_limit_bytes=56 * 1024 * 1024, collective_id=0, has_side_effects=True
        ),
        name="hyena_block",
    )(tok, embedding, conv_taps, gains, residues, decays, seeds, cot)


def finish_kernel(every, mixer, grad_out, mixer_out):
    tiles = every.shape[3] - 1
    for z in range(every.shape[0]):
        for x in range(every.shape[1]):
            n = z * every.shape[1] + x
            for y in range(every.shape[2]):
                grad_out[y * LANES : (y + 1) * LANES, n * LANES : (n + 1) * LANES] = real(
                    every[z, x, y, :tiles].reshape(LANES, LANES), every[z, x, y, tiles]
                )
    slab = mixer.shape[1] - 16
    for n in range(mixer.shape[0]):
        mixer_out[n * slab : (n + 1) * slab, :] = real(mixer[n, :slab, :], mixer[n, slab:, :])


def finish(mixer, every):
    a, b, c, tiles, height = every.shape[:5]
    blocks, slab = mixer.shape[0], mixer.shape[1] - 16
    tall = blocks * slab
    fold = 2
    steps = c // fold
    return pl.pallas_call(
        finish_kernel,
        grid=(steps,),
        out_shape=(
            jax.ShapeDtypeStruct((c * LANES, a * b * LANES), F32),
            jax.ShapeDtypeStruct((tall, LANES), F32),
        ),
        in_specs=[
            pl.BlockSpec((a, b, fold, tiles, height, LANES), lambda n: (0, 0, n, 0, 0, 0)),
            pl.BlockSpec((blocks // steps, *mixer.shape[1:]), lambda n: (n, 0, 0)),
        ],
        out_specs=(
            pl.BlockSpec((fold * LANES, a * b * LANES), lambda n: (n, 0)),
            pl.BlockSpec((tall // steps, LANES), lambda n: (n, 0)),
        ),
        name="finish",
    )(every, mixer)


def body(token_ids, embedding, conv_taps, residues, decays, filter_seed, skip_gain, cotangent):
    ctx_size = lax.axis_size("ctx")
    width = conv_taps.shape[2]
    tok_block = token_ids.shape[1]
    packed = run_block(
        token_ids, embedding, conv_taps, skip_gain.reshape(-1, LANES),
        residues.T, decays.T, filter_seed.T, cotangent.reshape(width, tok_block), ctx_size,
    )
    grad, mixer = finish(*packed)
    return mixer.reshape(cotangent.shape), grad


def solution(mesh):
    placed = (P("fsdp", "ctx"), P(None, "fsdp"), P(), P(), P(), P(), P(), P("fsdp", None, "ctx"))
    return jax.shard_map(
        body,
        mesh=mesh,
        in_specs=placed,
        out_specs=(P("fsdp", None, "ctx"), P(None, "fsdp")),
        check_vma=False,
    )
```

```python
import functools
import math

import jax
import jax.numpy as jnp
from jax import lax
from jax.experimental import pallas as pl
from jax.experimental.pallas import tpu as pltpu
from jax.sharding import PartitionSpec as P

PERIOD = 4096
F32 = jnp.float32
BF16 = jnp.bfloat16
LANES = 128
GROUP = 8


def iota(shape, dim):
    return lax.broadcasted_iota(jnp.int32, shape, dim)


def split(value):
    high = value.astype(BF16)
    return high, (value - high.astype(F32)).astype(BF16)


def cis(phase):
    quarter = PERIOD // 4
    turn = (phase + quarter // 2) // quarter
    a = (phase - turn * quarter).astype(F32) * (2.0 * math.pi / PERIOD)
    b = a * a
    s = a * (1.0 + b * (-1 / 6 + b * (1 / 120 + b * (-1 / 5040 + b * (1 / 362880)))))
    c = 1.0 + b * (-0.5 + b * (1 / 24 + b * (-1 / 720 + b * (1 / 40320))))
    odd = turn % 2 == 1
    re = jnp.where(odd, s, c)
    im = jnp.where(odd, c, s)
    re = jnp.where((turn == 1) | (turn == 2), -re, re)
    im = jnp.where((turn == 2) | (turn == 3), -im, im)
    return re, im


def power(rate, seed, steps):
    mag = jnp.exp(-rate * steps.astype(F32))
    re, im = cis((seed * steps) % PERIOD)
    return mag * re, mag * im


def nn(a, b):
    return jnp.dot(a, b, preferred_element_type=F32)


def nt(a, b):
    return lax.dot_general(a, b, (((1,), (1,)), ((), ())), preferred_element_type=F32)


def three(dot, left, right):
    left_high, left_low = left
    right_high, right_low = right
    rows = left_high.shape[0]
    both = dot(jnp.concatenate([left_high, left_low], axis=0), right_high)
    return both[:rows] + both[rows:] + dot(left_high, right_low)


MESH = pl.DeviceIdType.MESH


LEVELS = 32767.0


def fixed(block):
    peak = jnp.maximum(jnp.max(jnp.abs(block), axis=0, keepdims=True), 1e-30)
    power_of = jnp.ceil(jnp.log2(peak * (1.0 / LEVELS)))
    code = jnp.clip(jnp.round(block * jnp.exp2(-power_of)), -LEVELS, LEVELS)
    return code.astype(jnp.int32).astype(jnp.int16), power_of


def real(code, power_of):
    scale = jnp.exp2(power_of.astype(jnp.int32)[:1].astype(F32))
    return code.astype(jnp.int32).astype(F32) * scale


def gather_grad(pieces, chunks, quarters, columns_of, every, turn_sems, send_sems, recv_sems):
    sides = every.shape[:3]
    ctx = lax.axis_index("ctx")
    fsdp = lax.axis_index("fsdp")
    spans = (sides[1] * sides[2], sides[2], 1)
    here = [lax.rem(ctx // span, side) for span, side in zip(spans, sides)]
    slab = pieces[0].shape[0]
    sent = []

    def neighbour(axis, hop):
        there = lax.rem(here[axis] + hop + sides[axis], sides[axis])
        return there, (fsdp, ctx + (there - here[axis]) * spans[axis])

    def send(source, target, sender, receiver, where):
        made = pltpu.make_async_remote_copy(
            src_ref=source, dst_ref=target, send_sem=sender, recv_sem=receiver,
            device_id=where, device_id_type=MESH,
        )
        made.start()
        sent.append(made)

    def landed(place, sem):
        pltpu.make_async_copy(place, place, sem).wait()

    for j in range(sides[2]):
        quarters[j] = pieces[j]
    strip = pl.ds(pl.multiple_of(here[2] * slab, slab), slab)
    for n, hop in enumerate((1, -1, 2)):
        there, where = neighbour(2, hop)
        send(quarters.at[there], columns_of.at[strip], turn_sems.at[0, n], turn_sems.at[1, n], where)
    columns_of[strip, :] = quarters[here[2]]
    for n, hop in enumerate((-1, 1, 2)):
        there = neighbour(2, hop)[0]
        landed(columns_of.at[pl.ds(pl.multiple_of(there * slab, slab), slab)], turn_sems.at[1, n])
    block = columns_of[...].T
    code, power_of = fixed(block)
    tiles, height = every.shape[3] - 1, every.shape[4]
    every[here[0], here[1], here[2], :tiles] = code.reshape(tiles, height, LANES)
    every[here[0], here[1], here[2], tiles] = jnp.broadcast_to(power_of, (height, LANES)).astype(jnp.int32).astype(jnp.int16)

    def at(axis, hop, done, part):
        index = []
        for n in range(3):
            if n == axis:
                index.append(pl.ds(lax.rem(here[n] + hop + sides[n], sides[n]), 1))
            elif n in done:
                index.append(slice(None))
            else:
                index.append(pl.ds(here[n], 1))
        third = (tiles + 1) // 3
        return every.at[(*index, pl.ds(part * third, third))]

    for phase in range(3):
        plan = [((2 - part + phase) % 3, [(2 - part + n) % 3 for n in range(phase)]) for part in range(3)]
        for part, (axis, done) in enumerate(plan):
            mine = at(axis, 0, done, part)
            for n, hop in enumerate((2, 1, -1)):
                send(mine, mine, send_sems.at[part, phase, n], recv_sems.at[part, phase, n], neighbour(axis, hop)[1])
        for part, (axis, done) in enumerate(plan):
            for n, hop in enumerate((2, -1, 1)):
                landed(at(axis, hop, done, part), recv_sems.at[part, phase, n])
    for made in sent:
        made.wait_send()


def block_kernel(
    chunks, seq_len,
    tok_mine, embedding, conv_taps, gains, residue_all, decay_all, seed_all, cot_mine,
    mixer, every,
    query, key, value, mix, long_out, cot, cot_out, cot_in, mixed_out, tok,
    staged, table, taps, residues, decays, seeds, raw_table, turned, raw_taps,
    bank, toeplitz, diag, state_rows, quarters, columns_of,
    load_sems, tok_sems, cot_sems, mixer_sems, turn_sems, send_sems, recv_sems,
):
    vocab = embedding.shape[0]
    rows = tok.shape[0]
    slab = cot.shape[0] // rows
    modes = residues.shape[0]
    groups = slab // GROUP
    wide = GROUP * modes
    ctx = lax.axis_index("ctx")
    fsdp = lax.axis_index("fsdp")
    me = fsdp * chunks + ctx
    per_tile = LANES // slab

    def slab_rows(index):
        return pl.ds(pl.multiple_of(index * slab, slab), slab)

    def each_peer(action):
        action((1 - fsdp) * chunks + ctx, (1 - fsdp, ctx))

        def step(i, _):
            there = ctx + i
            there = jnp.where(there >= chunks, there - chunks, there)
            for side in (fsdp, 1 - fsdp):
                action(side * chunks + there, (side, there))
            return 0

        lax.fori_loop(1, chunks, step, 0, unroll=7)

    def send(source, target, sems, where):
        pltpu.make_async_remote_copy(
            src_ref=source, dst_ref=target, send_sem=sems.at[0], recv_sem=sems.at[1],
            device_id=where, device_id_type=MESH,
        ).start()

    barrier = pltpu.get_barrier_semaphore()
    load_cot = pltpu.make_async_copy(cot_mine, cot, load_sems.at[5])
    load_cot.start()
    each_peer(lambda place, where: pl.semaphore_signal(barrier, inc=1, device_id=where, device_id_type=MESH))

    lane_tile = pl.ds(pl.multiple_of(ctx // per_tile * LANES, LANES), LANES)
    wide_tile = pl.ds(pl.multiple_of(me // per_tile * LANES, LANES), LANES)
    loads = [
        pltpu.make_async_copy(source, target, load_sems.at[n])
        for n, (source, target) in enumerate((
            (residue_all.at[:, wide_tile], residues),
            (decay_all.at[:, wide_tile], decays),
            (seed_all.at[:, wide_tile], seeds),
            (conv_taps.at[:, :, wide_tile], raw_taps),
            (embedding.at[:, lane_tile], raw_table),
        ))
    ]
    for load in loads:
        load.start()

    sent_rows = pl.ds(0, slab + 2)

    def encode(target, place, block):
        code, power_of = fixed(block)
        target[place, :slab, :] = code
        target[place, slab:, :] = jnp.broadcast_to(power_of, (16, LANES)).astype(jnp.int32).astype(jnp.int16)

    own_tok = tok_mine[...]
    load_cot.wait()

    def pack(step, _):
        for i in range(16):
            r = step * 16 + i
            encode(cot_out, r, cot[slab_rows(r), :])
        return 0

    lax.fori_loop(0, rows // 16, pack, 0)
    pl.semaphore_wait(barrier, rows - 1)
    tok[me] = own_tok

    def send_tok(i, _):
        there = ctx + i
        there = jnp.where(there >= chunks, there - chunks, there)
        send(tok_mine, tok.at[me], tok_sems.at[0], (fsdp, there))
        return 0

    lax.fori_loop(1, chunks, send_tok, 0, unroll=7)
    def send_cot(place, where):
        send(cot_out.at[place, sent_rows], cot_in.at[me, sent_rows], cot_sems, where)

    each_peer(send_cot)

    def wait_bytes(ref, sem):
        pltpu.make_async_copy(ref, ref, sem).wait()

    for load in loads:
        load.wait()
    sub = pl.ds(pl.multiple_of(lax.rem(ctx, per_tile) * slab, slab), slab)
    turned[...] = raw_table[...].astype(F32).T
    for b in range(vocab // LANES):
        table[b * slab : (b + 1) * slab, :] = turned[sub, b * LANES : (b + 1) * LANES].astype(BF16)
    pieces = [residues[...], decays[...], seeds[...].astype(F32)]
    pieces += [raw_taps[s, j : j + 1, :] for s in range(3) for j in range(3)]
    pieces.append(gains[pl.ds(me // per_tile, 1), :])
    pieces.append(jnp.zeros((LANES - 10 - 3 * modes, LANES), F32))
    turned[:, :LANES] = jnp.concatenate(pieces, axis=0).T
    columns = turned[sub, :LANES]
    for j in range(10):
        taps[j] = jnp.broadcast_to(columns[:, 3 * modes + j : 3 * modes + j + 1], (slab, LANES))

    spread = (iota((slab * modes, slab), 0) // modes == iota((slab * modes, slab), 1)).astype(F32)
    pick = iota((slab * modes, modes), 0) % modes == iota((slab * modes, modes), 1)

    def column(part):
        wide_part = jnp.dot(spread, part, precision=lax.Precision.HIGHEST, preferred_element_type=F32)
        return jnp.sum(jnp.where(pick, wide_part, 0.0), axis=1, keepdims=True)

    rate = column(columns[:, modes : 2 * modes])
    seed = column(columns[:, 2 * modes : 3 * modes])
    res = column(columns[:, :modes])
    weight = res * jnp.sqrt(rate + 1.0 / seq_len)
    seed_int = (seed + 0.5).astype(jnp.int32)
    rate_b = jnp.broadcast_to(rate, (slab * modes, LANES))
    seed_b = jnp.broadcast_to(seed_int, (slab * modes, LANES))
    lane = iota((slab * modes, LANES), 1)
    up = power(rate_b, seed_b, lane)
    down = power(rate_b, seed_b, LANES - 1 - lane)
    for place, part in enumerate((*up, *down)):
        high, low = split(part)
        bank[2 * place] = high
        bank[2 * place + 1] = low
    kernel_head = jnp.sum((up[0] * weight).reshape(slab, modes, LANES), axis=1)
    kernel_head = kernel_head + jnp.where(iota((slab, LANES), 1) == 0, taps[9], 0.0)

    upper = iota((LANES, LANES), 1) >= iota((LANES, LANES), 0)
    for c in range(slab):
        line = jnp.broadcast_to(kernel_head[c : c + 1], (LANES, LANES))
        rolled = pltpu.roll(line, 0, 1, stride=1, stride_axis=0)
        high, low = split(jnp.where(upper, rolled, 0.0))
        toeplitz[0, c] = high
        toeplitz[1, c] = low

    eye = iota((wide, LANES), 0) == iota((wide, LANES), 1)
    step_row = iota((8, LANES), 0)
    steps = jnp.where(step_row == 6, 1, LANES * (1 << jnp.minimum(step_row, 5)))
    for g in range(groups):
        def row(part):
            piece = jnp.broadcast_to(part[g * wide : (g + 1) * wide], (wide, LANES))
            return jnp.sum(jnp.where(eye, piece, 0.0), axis=0, keepdims=True)

        rate_row = jnp.broadcast_to(row(rate), (8, LANES))
        seed_row = jnp.broadcast_to((row(seed) + 0.5).astype(jnp.int32), (8, LANES))
        weight_row = row(weight)
        re, im = power(rate_row, seed_row, steps)
        scale = jnp.where(step_row == 6, jnp.broadcast_to(weight_row, (8, LANES)), 1.0)
        state_rows[g, 0] = re * scale
        state_rows[g, 1] = im * scale

    diag[...] = jnp.zeros_like(diag)

    wait_bytes(tok.at[pl.ds(0, chunks - 1)], tok_sems.at[0, 1])
    own_half = tok.at[pl.ds(pl.multiple_of(fsdp * chunks, chunks), chunks)]
    send(own_half, own_half, tok_sems.at[1], (1 - fsdp, ctx))
    lane_c = iota((slab, LANES), 1)
    low_row = iota((LANES, LANES), 0)
    banks = vocab // LANES

    def token_parts(r):
        token = tok[r]
        bank_of = token // LANES
        hot = jnp.where(low_row == token - bank_of * LANES, 1.0, 0.0).astype(BF16)
        return hot, bank_of

    UNROLL = 32

    def gather(base, step, carry):
        last_one, last_two = carry
        r0 = base + step * UNROLL
        parts = [token_parts(r0 + i) for i in range(UNROLL)]
        found = nn(table[...], jnp.concatenate([hot for hot, _ in parts], axis=1))
        for i in range(UNROLL):
            bank_of = parts[i][1]
            x = found[:slab, i * LANES : (i + 1) * LANES]
            for b in range(1, banks):
                x = jnp.where(bank_of == b, found[b * slab : (b + 1) * slab, i * LANES : (i + 1) * LANES], x)
            one = pltpu.roll(x, 1, 1)
            two = pltpu.roll(x, 2, 1)
            x1 = jnp.where(lane_c < 1, last_one, one)
            x2 = jnp.where(lane_c < 2, last_two, two)
            last_one, last_two = one, two
            q, k, v = (taps[3 * s] * x + taps[3 * s + 1] * x1 + taps[3 * s + 2] * x2 for s in range(3))
            at = pl.ds(pl.multiple_of((r0 + i) * slab, slab), slab)
            query[at, :] = q
            key[at, :] = k
            value[at, :] = v
            mix[at, :] = k * v
        return last_one, last_two

    zero = jnp.zeros((slab, LANES), F32)
    cot_in[me] = cot_out[me]
    per_sequence = chunks // UNROLL
    lax.fori_loop(0, per_sequence, functools.partial(gather, fsdp * chunks), (zero, zero))
    wait_bytes(own_half, tok_sems.at[1, 1])
    lax.fori_loop(0, per_sequence, functools.partial(gather, (1 - fsdp) * chunks), (zero, zero))

    row_in_seq = iota((rows, LANES), 0) % chunks

    def scan(re, im, g, backward):
        for j in range(max(1, (chunks - 1).bit_length())):
            shift = 1 << j
            amount = rows - shift if backward else shift
            keep = row_in_seq < chunks - shift if backward else row_in_seq >= shift
            old_re = jnp.where(keep, pltpu.roll(re, amount, 0), 0.0)
            old_im = jnp.where(keep, pltpu.roll(im, amount, 0), 0.0)
            a, b = state_rows[g, 0, j : j + 1, :], state_rows[g, 1, j : j + 1, :]
            re, im = re + a * old_re - b * old_im, im + a * old_im + b * old_re
        amount = rows - 1 if backward else 1
        keep = row_in_seq < chunks - 1 if backward else row_in_seq >= 1
        re = jnp.where(keep, pltpu.roll(re, amount, 0), 0.0)
        im = jnp.where(keep, pltpu.roll(im, amount, 0), 0.0)
        a, b = state_rows[g, 0, 6:7, :], state_rows[g, 1, 6:7, :]
        return a * re - b * im, -(a * im + b * re)

    def long_conv(source, target, backward):
        enter, leave = (0, 2) if backward else (2, 0)

        def per_group(g, _):
            base = g * GROUP
            for c in range(GROUP):
                at = pl.ds(pl.multiple_of(g * wide + c * modes, modes), modes)
                for half in range(2):
                    spot = slice(half * wide + c * modes, half * wide + (c + 1) * modes)
                    for part in range(2):
                        diag[part, spot, c * LANES : (c + 1) * LANES] = bank[2 * (enter + half) + part, at, :]
            local = jnp.zeros((rows, 2 * wide), F32)
            for c in range(GROUP):
                u = split(source[pl.ds(base + c, rows, stride=slab), :])
                staged[0, base + c], staged[1, base + c] = u
                at = slice(c * LANES, (c + 1) * LANES)
                local = local + three(nt, u, (diag[0, :, at], diag[1, :, at]))
            re, im = scan(local[:, :wide], local[:, wide:], g, backward)
            state = split(jnp.concatenate([re, im], axis=1))
            for c in range(GROUP):
                u = (staged[0, base + c], staged[1, base + c])
                at = slice(c * LANES, (c + 1) * LANES)
                band = (toeplitz[0, base + c], toeplitz[1, base + c])
                out = three(nt if backward else nn, u, band)
                mine = slice(c * modes, (c + 1) * modes)
                held = [jnp.concatenate([p[:, mine], p[:, wide + c * modes : wide + (c + 1) * modes]], axis=1) for p in state]
                rows_at = pl.ds(pl.multiple_of(g * wide + c * modes, modes), modes)
                pole = [
                    jnp.concatenate([bank[2 * leave + part, rows_at, :], bank[2 * (leave + 1) + part, rows_at, :]], axis=0)
                    for part in range(2)
                ]
                out = out + three(nn, held, pole)
                target[pl.ds(base + c, rows, stride=slab), :] = out
            return 0

        lax.fori_loop(0, groups, per_group, 0, unroll=True)

    long_conv(mix, long_out, False)

    def emit(step, _):
        for i in range(32):
            r = step * 32 + i
            at = slab_rows(r)
            encode(mixed_out, r, query[at, :] * long_out[at, :])
        return 0

    def weigh(step, _):
        for i in range(16):
            r = step * 16 + i
            at = slab_rows(r)
            value_in = real(cot_in[r, :slab, :], cot_in[r, slab:, :])
            cot[at, :] = value_in
            mix[at, :] = value_in * query[at, :]
        return 0

    def send_mixed(place, where):
        send(mixed_out.at[place, sent_rows], mixer.at[me, sent_rows], mixer_sems, where)

    lax.fori_loop(0, rows // 32, emit, 0)
    each_peer(send_mixed)
    mixer[me] = mixed_out[me]
    most = pl.ds(0, rows - 1)
    wait_bytes(cot_in.at[most, sent_rows], cot_sems.at[1])
    lax.fori_loop(0, rows // 16, weigh, 0)

    grad_mixed = query
    long_conv(mix, grad_mixed, True)

    def scatter(step, carry):
        next_one, next_two, total = carry
        r0 = rows - UNROLL - step * UNROLL
        fresh = (r0 % chunks) == chunks - UNROLL
        next_one = jnp.where(fresh, 0.0, next_one)
        next_two = jnp.where(fresh, 0.0, next_two)
        pieces, hots = [None] * UNROLL, [None] * UNROLL
        for i in reversed(range(UNROLL)):
            at = pl.ds(pl.multiple_of((r0 + i) * slab, slab), slab)
            gm = grad_mixed[at, :]
            gq = cot[at, :] * long_out[at, :]
            gk = gm * value[at, :]
            gv = gm * key[at, :]
            zeroth, first, second = (taps[j] * gq + taps[3 + j] * gk + taps[6 + j] * gv for j in range(3))
            one = pltpu.roll(first, LANES - 1, 1)
            two = pltpu.roll(second, LANES - 2, 1)
            gx = (
                zeroth
                + jnp.where(lane_c >= LANES - 1, next_one, one)
                + jnp.where(lane_c >= LANES - 2, next_two, two)
            )
            next_one, next_two = one, two
            hots[i], bank_of = token_parts(r0 + i)
            both = jnp.concatenate(split(gx), axis=0)
            mask = [jnp.where(bank_of == b, 1.0, 0.0).astype(BF16) for b in range(banks)]
            pieces[i] = jnp.concatenate([both * m for m in mask], axis=0)
        hot = jnp.concatenate(hots, axis=1)
        return next_one, next_two, total + nt(jnp.concatenate(pieces, axis=1), hot)

    _, _, total = lax.fori_loop(
        0, rows // UNROLL, scatter, (zero, zero, jnp.zeros((2 * slab * banks, LANES), F32))
    )
    step = 2 * slab
    pieces = [total[b * step : b * step + slab] + total[b * step + slab : (b + 1) * step] for b in range(banks)]
    gather_grad(
        pieces, chunks, quarters, columns_of, every, turn_sems, send_sems, recv_sems
    )
    wait_bytes(cot_in.at[most, sent_rows], cot_sems.at[0])
    wait_bytes(tok.at[pl.ds(0, chunks - 1)], tok_sems.at[0, 0])
    wait_bytes(own_half, tok_sems.at[1, 0])
    for end in range(2):
        wait_bytes(mixer.at[most, sent_rows], mixer_sems.at[end])


def run_block(tok, embedding, conv_taps, gains, residues, decays, seeds, cot, chunks):
    modes, width = residues.shape
    vocab = embedding.shape[0]
    rows = width // (embedding.shape[1] // chunks)
    slab = width // rows
    tall = rows * slab
    side = round(chunks ** (1 / 3))
    vmem = pl.BlockSpec(memory_space=pltpu.VMEM)
    hbm = pl.BlockSpec(memory_space=pl.ANY)
    dma = pltpu.SemaphoreType.DMA
    return pl.pallas_call(
        functools.partial(block_kernel, chunks, chunks * LANES),
        out_shape=(
            jax.ShapeDtypeStruct((rows, slab + 16, LANES), jnp.int16),
            jax.ShapeDtypeStruct((side,) * 3 + (LANES // 16 + 1, 16, LANES), jnp.int16),
        ),
        in_specs=[vmem, hbm, hbm, vmem, hbm, hbm, hbm, hbm],
        out_specs=(vmem, vmem),
        scratch_shapes=[pltpu.VMEM((tall, LANES), F32)] * 6
        + [pltpu.VMEM((rows, slab + 16, LANES), jnp.int16)] * 3
        + [
            pltpu.VMEM((rows, 1, LANES), jnp.int32),
            pltpu.VMEM((2, slab, LANES, LANES), BF16),
            pltpu.VMEM((vocab // LANES * slab, LANES), BF16),
            pltpu.VMEM((10, slab, LANES), F32),
            pltpu.VMEM((modes, LANES), F32),
            pltpu.VMEM((modes, LANES), F32),
            pltpu.VMEM((modes, LANES), jnp.int32),
            pltpu.VMEM((vocab, LANES), BF16),
            pltpu.VMEM((LANES, vocab), F32),
            pltpu.VMEM((3, 3, LANES), F32),
            pltpu.VMEM((8, slab * modes, LANES), BF16),
            pltpu.VMEM((2, slab, LANES, LANES), BF16),
            pltpu.VMEM((2, 2 * GROUP * modes, GROUP * LANES), BF16),
            pltpu.VMEM((slab // GROUP, 2, 8, LANES), F32),
            pltpu.VMEM((side, slab, LANES), F32),
            pltpu.VMEM((LANES, LANES), F32),
            dma((6,)), dma((2, 2)), dma((2,)), dma((2,)), dma((2, 3)), dma((3, 3, 3)), dma((3, 3, 3)),
        ],
        compiler_params=pltpu.CompilerParams(
            vmem_limit_bytes=56 * 1024 * 1024, collective_id=0, has_side_effects=True
        ),
        name="hyena_block",
    )(tok, embedding, conv_taps, gains, residues, decays, seeds, cot)


def finish_kernel(every, mixer, grad_out, mixer_out):
    tiles = every.shape[3] - 1
    for z in range(every.shape[0]):
        for x in range(every.shape[1]):
            n = z * every.shape[1] + x
            for y in range(every.shape[2]):
                grad_out[y * LANES : (y + 1) * LANES, n * LANES : (n + 1) * LANES] = real(
                    every[z, x, y, :tiles].reshape(LANES, LANES), every[z, x, y, tiles]
                )
    slab = mixer.shape[1] - 16
    for n in range(mixer.shape[0]):
        mixer_out[n * slab : (n + 1) * slab, :] = real(mixer[n, :slab, :], mixer[n, slab:, :])


def finish(mixer, every):
    a, b, c, tiles, height = every.shape[:5]
    blocks, slab = mixer.shape[0], mixer.shape[1] - 16
    tall = blocks * slab
    fold = 2
    steps = c // fold
    return pl.pallas_call(
        finish_kernel,
        grid=(steps,),
        out_shape=(
            jax.ShapeDtypeStruct((c * LANES, a * b * LANES), F32),
            jax.ShapeDtypeStruct((tall, LANES), F32),
        ),
        in_specs=[
            pl.BlockSpec((a, b, fold, tiles, height, LANES), lambda n: (0, 0, n, 0, 0, 0)),
            pl.BlockSpec((blocks // steps, *mixer.shape[1:]), lambda n: (n, 0, 0)),
        ],
        out_specs=(
            pl.BlockSpec((fold * LANES, a * b * LANES), lambda n: (n, 0)),
            pl.BlockSpec((tall // steps, LANES), lambda n: (n, 0)),
        ),
        name="finish",
    )(every, mixer)


def body(token_ids, embedding, conv_taps, residues, decays, filter_seed, skip_gain, cotangent):
    ctx_size = lax.axis_size("ctx")
    width = conv_taps.shape[2]
    tok_block = token_ids.shape[1]
    packed = run_block(
        token_ids, embedding, conv_taps, skip_gain.reshape(-1, LANES),
        residues.T, decays.T, filter_seed.T, cotangent.reshape(width, tok_block), ctx_size,
    )
    grad, mixer = finish(*packed)
    return mixer.reshape(cotangent.shape), grad


def solution(mesh):
    placed = (P("fsdp", "ctx"), P(None, "fsdp"), P(), P(), P(), P(), P(), P("fsdp", None, "ctx"))
    return jax.shard_map(
        body,
        mesh=mesh,
        in_specs=placed,
        out_specs=(P("fsdp", None, "ctx"), P(None, "fsdp")),
        check_vma=False,
    )
```

```python
import functools
import math

import jax
import jax.numpy as jnp
from jax import lax
from jax.experimental import pallas as pl
from jax.experimental.pallas import tpu as pltpu
from jax.sharding import PartitionSpec as P

PERIOD = 4096
F32 = jnp.float32
BF16 = jnp.bfloat16
LANES = 128
GROUP = 8


def iota(shape, dim):
    return lax.broadcasted_iota(jnp.int32, shape, dim)


def split(value):
    high = value.astype(BF16)
    return high, (value - high.astype(F32)).astype(BF16)


def cis(phase):
    quarter = PERIOD // 4
    turn = (phase + quarter // 2) // quarter
    a = (phase - turn * quarter).astype(F32) * (2.0 * math.pi / PERIOD)
    b = a * a
    s = a * (1.0 + b * (-1 / 6 + b * (1 / 120 + b * (-1 / 5040 + b * (1 / 362880)))))
    c = 1.0 + b * (-0.5 + b * (1 / 24 + b * (-1 / 720 + b * (1 / 40320))))
    odd = turn % 2 == 1
    re = jnp.where(odd, s, c)
    im = jnp.where(odd, c, s)
    re = jnp.where((turn == 1) | (turn == 2), -re, re)
    im = jnp.where((turn == 2) | (turn == 3), -im, im)
    return re, im


def power(rate, seed, steps):
    mag = jnp.exp(-rate * steps.astype(F32))
    re, im = cis((seed * steps) % PERIOD)
    return mag * re, mag * im


def nn(a, b):
    return jnp.dot(a, b, preferred_element_type=F32)


def nt(a, b):
    return lax.dot_general(a, b, (((1,), (1,)), ((), ())), preferred_element_type=F32)


def three(dot, left, right):
    left_high, left_low = left
    right_high, right_low = right
    rows = left_high.shape[0]
    both = dot(jnp.concatenate([left_high, left_low], axis=0), right_high)
    return both[:rows] + both[rows:] + dot(left_high, right_low)


MESH = pl.DeviceIdType.MESH


LEVELS = 32767.0


def fixed(block):
    peak = jnp.maximum(jnp.max(jnp.abs(block), axis=0, keepdims=True), 1e-30)
    power_of = jnp.ceil(jnp.log2(peak * (1.0 / LEVELS)))
    code = jnp.clip(jnp.round(block * jnp.exp2(-power_of)), -LEVELS, LEVELS)
    return code.astype(jnp.int32).astype(jnp.int16), power_of


def real(code, power_of):
    scale = jnp.exp2(power_of.astype(jnp.int32)[:1].astype(F32))
    return code.astype(jnp.int32).astype(F32) * scale


def gather_grad(pieces, chunks, quarters, columns_of, every, turn_sems, send_sems, recv_sems):
    sides = every.shape[:3]
    ctx = lax.axis_index("ctx")
    fsdp = lax.axis_index("fsdp")
    spans = (sides[1] * sides[2], sides[2], 1)
    here = [lax.rem(ctx // span, side) for span, side in zip(spans, sides)]
    slab = pieces[0].shape[0]
    sent = []

    def neighbour(axis, hop):
        there = lax.rem(here[axis] + hop + sides[axis], sides[axis])
        return there, (fsdp, ctx + (there - here[axis]) * spans[axis])

    def send(source, target, sender, receiver, where):
        made = pltpu.make_async_remote_copy(
            src_ref=source, dst_ref=target, send_sem=sender, recv_sem=receiver,
            device_id=where, device_id_type=MESH,
        )
        made.start()
        sent.append(made)

    def landed(place, sem):
        pltpu.make_async_copy(place, place, sem).wait()

    for j in range(sides[2]):
        quarters[j] = pieces[j]
    strip = pl.ds(pl.multiple_of(here[2] * slab, slab), slab)
    for n, hop in enumerate((1, -1, 2)):
        there, where = neighbour(2, hop)
        send(quarters.at[there], columns_of.at[strip], turn_sems.at[0, n], turn_sems.at[1, n], where)
    columns_of[strip, :] = quarters[here[2]]
    for n, hop in enumerate((-1, 1, 2)):
        there = neighbour(2, hop)[0]
        landed(columns_of.at[pl.ds(pl.multiple_of(there * slab, slab), slab)], turn_sems.at[1, n])
    block = columns_of[...].T
    code, power_of = fixed(block)
    tiles, height = every.shape[3] - 1, every.shape[4]
    every[here[0], here[1], here[2], :tiles] = code.reshape(tiles, height, LANES)
    every[here[0], here[1], here[2], tiles] = jnp.broadcast_to(power_of, (height, LANES)).astype(jnp.int32).astype(jnp.int16)

    def at(axis, hop, done, part):
        index = []
        for n in range(3):
            if n == axis:
                index.append(pl.ds(lax.rem(here[n] + hop + sides[n], sides[n]), 1))
            elif n in done:
                index.append(slice(None))
            else:
                index.append(pl.ds(here[n], 1))
        third = (tiles + 1) // 3
        return every.at[(*index, pl.ds(part * third, third))]

    for phase in range(3):
        plan = [((2 - part + phase) % 3, [(2 - part + n) % 3 for n in range(phase)]) for part in range(3)]
        for part, (axis, done) in enumerate(plan):
            mine = at(axis, 0, done, part)
            for n, hop in enumerate((2, 1, -1)):
                send(mine, mine, send_sems.at[part, phase, n], recv_sems.at[part, phase, n], neighbour(axis, hop)[1])
        for part, (axis, done) in enumerate(plan):
            for n, hop in enumerate((2, -1, 1)):
                landed(at(axis, hop, done, part), recv_sems.at[part, phase, n])
    for made in sent:
        made.wait_send()


def block_kernel(
    chunks, seq_len,
    tok_mine, embedding, conv_taps, gains, residue_all, decay_all, seed_all, cot_mine,
    mixer, every,
    query, key, value, mix, long_out, cot, cot_out, cot_in, mixed_out, tok,
    staged, table, taps, residues, decays, seeds, raw_table, turned, raw_taps,
    bank, toeplitz, diag, state_rows, quarters, columns_of,
    load_sems, tok_sems, cot_sems, mixer_sems, turn_sems, send_sems, recv_sems,
):
    vocab = embedding.shape[0]
    rows = tok.shape[0]
    slab = cot.shape[0] // rows
    modes = residues.shape[0]
    groups = slab // GROUP
    wide = GROUP * modes
    ctx = lax.axis_index("ctx")
    fsdp = lax.axis_index("fsdp")
    me = fsdp * chunks + ctx
    per_tile = LANES // slab

    def slab_rows(index):
        return pl.ds(pl.multiple_of(index * slab, slab), slab)

    def each_peer(action):
        action((1 - fsdp) * chunks + ctx, (1 - fsdp, ctx))

        def step(i, _):
            there = ctx + i
            there = jnp.where(there >= chunks, there - chunks, there)
            for side in (fsdp, 1 - fsdp):
                action(side * chunks + there, (side, there))
            return 0

        lax.fori_loop(1, chunks, step, 0, unroll=21)

    def send(source, target, sems, where):
        pltpu.make_async_remote_copy(
            src_ref=source, dst_ref=target, send_sem=sems.at[0], recv_sem=sems.at[1],
            device_id=where, device_id_type=MESH,
        ).start()

    barrier = pltpu.get_barrier_semaphore()
    load_cot = pltpu.make_async_copy(cot_mine, cot, load_sems.at[5])
    load_cot.start()
    each_peer(lambda place, where: pl.semaphore_signal(barrier, inc=1, device_id=where, device_id_type=MESH))

    lane_tile = pl.ds(pl.multiple_of(ctx // per_tile * LANES, LANES), LANES)
    wide_tile = pl.ds(pl.multiple_of(me // per_tile * LANES, LANES), LANES)
    loads = [
        pltpu.make_async_copy(source, target, load_sems.at[n])
        for n, (source, target) in enumerate((
            (residue_all.at[:, wide_tile], residues),
            (decay_all.at[:, wide_tile], decays),
            (seed_all.at[:, wide_tile], seeds),
            (conv_taps.at[:, :, wide_tile], raw_taps),
            (embedding.at[:, lane_tile], raw_table),
        ))
    ]
    for load in loads:
        load.start()

    sent_rows = pl.ds(0, slab + 2)

    def encode(target, place, block):
        code, power_of = fixed(block)
        target[place, :slab, :] = code
        target[place, slab:, :] = jnp.broadcast_to(power_of, (16, LANES)).astype(jnp.int32).astype(jnp.int16)

    own_tok = tok_mine[...]
    load_cot.wait()

    def pack(step, _):
        for i in range(16):
            r = step * 16 + i
            encode(cot_out, r, cot[slab_rows(r), :])
        return 0

    lax.fori_loop(0, rows // 16, pack, 0)
    pl.semaphore_wait(barrier, rows - 1)
    tok[me] = own_tok

    def send_tok(i, _):
        there = ctx + i
        there = jnp.where(there >= chunks, there - chunks, there)
        send(tok_mine, tok.at[me], tok_sems.at[0], (fsdp, there))
        return 0

    lax.fori_loop(1, chunks, send_tok, 0, unroll=7)
    def send_cot(place, where):
        send(cot_out.at[place, sent_rows], cot_in.at[me, sent_rows], cot_sems, where)

    each_peer(send_cot)

    def wait_bytes(ref, sem):
        pltpu.make_async_copy(ref, ref, sem).wait()

    for load in loads:
        load.wait()
    sub = pl.ds(pl.multiple_of(lax.rem(ctx, per_tile) * slab, slab), slab)
    turned[...] = raw_table[...].astype(F32).T
    for b in range(vocab // LANES):
        table[b * slab : (b + 1) * slab, :] = turned[sub, b * LANES : (b + 1) * LANES].astype(BF16)
    pieces = [residues[...], decays[...], seeds[...].astype(F32)]
    pieces += [raw_taps[s, j : j + 1, :] for s in range(3) for j in range(3)]
    pieces.append(gains[pl.ds(me // per_tile, 1), :])
    pieces.append(jnp.zeros((LANES - 10 - 3 * modes, LANES), F32))
    turned[:, :LANES] = jnp.concatenate(pieces, axis=0).T
    columns = turned[sub, :LANES]
    for j in range(10):
        taps[j] = jnp.broadcast_to(columns[:, 3 * modes + j : 3 * modes + j + 1], (slab, LANES))

    spread = (iota((slab * modes, slab), 0) // modes == iota((slab * modes, slab), 1)).astype(F32)
    pick = iota((slab * modes, modes), 0) % modes == iota((slab * modes, modes), 1)

    def column(part):
        wide_part = jnp.dot(spread, part, precision=lax.Precision.HIGHEST, preferred_element_type=F32)
        return jnp.sum(jnp.where(pick, wide_part, 0.0), axis=1, keepdims=True)

    rate = column(columns[:, modes : 2 * modes])
    seed = column(columns[:, 2 * modes : 3 * modes])
    res = column(columns[:, :modes])
    weight = res * jnp.sqrt(rate + 1.0 / seq_len)
    seed_int = (seed + 0.5).astype(jnp.int32)
    rate_b = jnp.broadcast_to(rate, (slab * modes, LANES))
    seed_b = jnp.broadcast_to(seed_int, (slab * modes, LANES))
    lane = iota((slab * modes, LANES), 1)
    up = power(rate_b, seed_b, lane)
    down = power(rate_b, seed_b, LANES - 1 - lane)
    for place, part in enumerate((*up, *down)):
        high, low = split(part)
        bank[2 * place] = high
        bank[2 * place + 1] = low
    kernel_head = jnp.sum((up[0] * weight).reshape(slab, modes, LANES), axis=1)
    kernel_head = kernel_head + jnp.where(iota((slab, LANES), 1) == 0, taps[9], 0.0)

    upper = iota((LANES, LANES), 1) >= iota((LANES, LANES), 0)
    for c in range(slab):
        line = jnp.broadcast_to(kernel_head[c : c + 1], (LANES, LANES))
        rolled = pltpu.roll(line, 0, 1, stride=1, stride_axis=0)
        high, low = split(jnp.where(upper, rolled, 0.0))
        toeplitz[0, c] = high
        toeplitz[1, c] = low

    eye = iota((wide, LANES), 0) == iota((wide, LANES), 1)
    step_row = iota((8, LANES), 0)
    steps = jnp.where(step_row == 6, 1, LANES * (1 << jnp.minimum(step_row, 5)))
    for g in range(groups):
        def row(part):
            piece = jnp.broadcast_to(part[g * wide : (g + 1) * wide], (wide, LANES))
            return jnp.sum(jnp.where(eye, piece, 0.0), axis=0, keepdims=True)

        rate_row = jnp.broadcast_to(row(rate), (8, LANES))
        seed_row = jnp.broadcast_to((row(seed) + 0.5).astype(jnp.int32), (8, LANES))
        weight_row = row(weight)
        re, im = power(rate_row, seed_row, steps)
        scale = jnp.where(step_row == 6, jnp.broadcast_to(weight_row, (8, LANES)), 1.0)
        state_rows[g, 0] = re * scale
        state_rows[g, 1] = im * scale

    diag[...] = jnp.zeros_like(diag)

    wait_bytes(tok.at[pl.ds(0, chunks - 1)], tok_sems.at[0, 1])
    own_half = tok.at[pl.ds(pl.multiple_of(fsdp * chunks, chunks), chunks)]
    send(own_half, own_half, tok_sems.at[1], (1 - fsdp, ctx))
    lane_c = iota((slab, LANES), 1)
    low_row = iota((LANES, LANES), 0)
    banks = vocab // LANES

    def token_parts(r):
        token = tok[r]
        bank_of = token // LANES
        hot = jnp.where(low_row == token - bank_of * LANES, 1.0, 0.0).astype(BF16)
        return hot, bank_of

    UNROLL = 32

    def gather(base, step, carry):
        last_one, last_two = carry
        r0 = base + step * UNROLL
        parts = [token_parts(r0 + i) for i in range(UNROLL)]
        found = nn(table[...], jnp.concatenate([hot for hot, _ in parts], axis=1))
        for i in range(UNROLL):
            bank_of = parts[i][1]
            x = found[:slab, i * LANES : (i + 1) * LANES]
            for b in range(1, banks):
                x = jnp.where(bank_of == b, found[b * slab : (b + 1) * slab, i * LANES : (i + 1) * LANES], x)
            one = pltpu.roll(x, 1, 1)
            two = pltpu.roll(x, 2, 1)
            x1 = jnp.where(lane_c < 1, last_one, one)
            x2 = jnp.where(lane_c < 2, last_two, two)
            last_one, last_two = one, two
            q, k, v = (taps[3 * s] * x + taps[3 * s + 1] * x1 + taps[3 * s + 2] * x2 for s in range(3))
            at = pl.ds(pl.multiple_of((r0 + i) * slab, slab), slab)
            query[at, :] = q
            key[at, :] = k
            value[at, :] = v
            mix[at, :] = k * v
        return last_one, last_two

    zero = jnp.zeros((slab, LANES), F32)
    cot_in[me] = cot_out[me]
    per_sequence = chunks // UNROLL
    lax.fori_loop(0, per_sequence, functools.partial(gather, fsdp * chunks), (zero, zero))
    wait_bytes(own_half, tok_sems.at[1, 1])
    lax.fori_loop(0, per_sequence, functools.partial(gather, (1 - fsdp) * chunks), (zero, zero))

    row_in_seq = iota((rows, LANES), 0) % chunks

    def scan(re, im, g, backward):
        for j in range(max(1, (chunks - 1).bit_length())):
            shift = 1 << j
            amount = rows - shift if backward else shift
            keep = row_in_seq < chunks - shift if backward else row_in_seq >= shift
            old_re = jnp.where(keep, pltpu.roll(re, amount, 0), 0.0)
            old_im = jnp.where(keep, pltpu.roll(im, amount, 0), 0.0)
            a, b = state_rows[g, 0, j : j + 1, :], state_rows[g, 1, j : j + 1, :]
            re, im = re + a * old_re - b * old_im, im + a * old_im + b * old_re
        amount = rows - 1 if backward else 1
        keep = row_in_seq < chunks - 1 if backward else row_in_seq >= 1
        re = jnp.where(keep, pltpu.roll(re, amount, 0), 0.0)
        im = jnp.where(keep, pltpu.roll(im, amount, 0), 0.0)
        a, b = state_rows[g, 0, 6:7, :], state_rows[g, 1, 6:7, :]
        return a * re - b * im, -(a * im + b * re)

    def long_conv(source, target, backward):
        enter, leave = (0, 2) if backward else (2, 0)

        def per_group(g, _):
            base = g * GROUP
            for c in range(GROUP):
                at = pl.ds(pl.multiple_of(g * wide + c * modes, modes), modes)
                for half in range(2):
                    spot = slice(half * wide + c * modes, half * wide + (c + 1) * modes)
                    for part in range(2):
                        diag[part, spot, c * LANES : (c + 1) * LANES] = bank[2 * (enter + half) + part, at, :]
            local = jnp.zeros((rows, 2 * wide), F32)
            for c in range(GROUP):
                u = split(source[pl.ds(base + c, rows, stride=slab), :])
                staged[0, base + c], staged[1, base + c] = u
                at = slice(c * LANES, (c + 1) * LANES)
                local = local + three(nt, u, (diag[0, :, at], diag[1, :, at]))
            re, im = scan(local[:, :wide], local[:, wide:], g, backward)
            state = split(jnp.concatenate([re, im], axis=1))
            for c in range(GROUP):
                u = (staged[0, base + c], staged[1, base + c])
                at = slice(c * LANES, (c + 1) * LANES)
                band = (toeplitz[0, base + c], toeplitz[1, base + c])
                out = three(nt if backward else nn, u, band)
                mine = slice(c * modes, (c + 1) * modes)
                held = [jnp.concatenate([p[:, mine], p[:, wide + c * modes : wide + (c + 1) * modes]], axis=1) for p in state]
                rows_at = pl.ds(pl.multiple_of(g * wide + c * modes, modes), modes)
                pole = [
                    jnp.concatenate([bank[2 * leave + part, rows_at, :], bank[2 * (leave + 1) + part, rows_at, :]], axis=0)
                    for part in range(2)
                ]
                out = out + three(nn, held, pole)
                target[pl.ds(base + c, rows, stride=slab), :] = out
            return 0

        lax.fori_loop(0, groups, per_group, 0, unroll=True)

    long_conv(mix, long_out, False)

    def emit(step, _):
        for i in range(32):
            r = step * 32 + i
            at = slab_rows(r)
            encode(mixed_out, r, query[at, :] * long_out[at, :])
        return 0

    def weigh(step, _):
        for i in range(16):
            r = step * 16 + i
            at = slab_rows(r)
            value_in = real(cot_in[r, :slab, :], cot_in[r, slab:, :])
            cot[at, :] = value_in
            mix[at, :] = value_in * query[at, :]
        return 0

    def send_mixed(place, where):
        send(mixed_out.at[place, sent_rows], mixer.at[me, sent_rows], mixer_sems, where)

    lax.fori_loop(0, rows // 32, emit, 0)
    each_peer(send_mixed)
    mixer[me] = mixed_out[me]
    most = pl.ds(0, rows - 1)
    wait_bytes(cot_in.at[most, sent_rows], cot_sems.at[1])
    lax.fori_loop(0, rows // 16, weigh, 0)

    grad_mixed = query
    long_conv(mix, grad_mixed, True)

    def scatter(step, carry):
        next_one, next_two, total = carry
        r0 = rows - UNROLL - step * UNROLL
        fresh = (r0 % chunks) == chunks - UNROLL
        next_one = jnp.where(fresh, 0.0, next_one)
        next_two = jnp.where(fresh, 0.0, next_two)
        pieces, hots = [None] * UNROLL, [None] * UNROLL
        for i in reversed(range(UNROLL)):
            at = pl.ds(pl.multiple_of((r0 + i) * slab, slab), slab)
            gm = grad_mixed[at, :]
            gq = cot[at, :] * long_out[at, :]
            gk = gm * value[at, :]
            gv = gm * key[at, :]
            zeroth, first, second = (taps[j] * gq + taps[3 + j] * gk + taps[6 + j] * gv for j in range(3))
            one = pltpu.roll(first, LANES - 1, 1)
            two = pltpu.roll(second, LANES - 2, 1)
            gx = (
                zeroth
                + jnp.where(lane_c >= LANES - 1, next_one, one)
                + jnp.where(lane_c >= LANES - 2, next_two, two)
            )
            next_one, next_two = one, two
            hots[i], bank_of = token_parts(r0 + i)
            both = jnp.concatenate(split(gx), axis=0)
            mask = [jnp.where(bank_of == b, 1.0, 0.0).astype(BF16) for b in range(banks)]
            pieces[i] = jnp.concatenate([both * m for m in mask], axis=0)
        hot = jnp.concatenate(hots, axis=1)
        return next_one, next_two, total + nt(jnp.concatenate(pieces, axis=1), hot)

    _, _, total = lax.fori_loop(
        0, rows // UNROLL, scatter, (zero, zero, jnp.zeros((2 * slab * banks, LANES), F32))
    )
    step = 2 * slab
    pieces = [total[b * step : b * step + slab] + total[b * step + slab : (b + 1) * step] for b in range(banks)]
    gather_grad(
        pieces, chunks, quarters, columns_of, every, turn_sems, send_sems, recv_sems
    )
    wait_bytes(cot_in.at[most, sent_rows], cot_sems.at[0])
    wait_bytes(tok.at[pl.ds(0, chunks - 1)], tok_sems.at[0, 0])
    wait_bytes(own_half, tok_sems.at[1, 0])
    for end in range(2):
        wait_bytes(mixer.at[most, sent_rows], mixer_sems.at[end])


def run_block(tok, embedding, conv_taps, gains, residues, decays, seeds, cot, chunks):
    modes, width = residues.shape
    vocab = embedding.shape[0]
    rows = width // (embedding.shape[1] // chunks)
    slab = width // rows
    tall = rows * slab
    side = round(chunks ** (1 / 3))
    vmem = pl.BlockSpec(memory_space=pltpu.VMEM)
    hbm = pl.BlockSpec(memory_space=pl.ANY)
    dma = pltpu.SemaphoreType.DMA
    return pl.pallas_call(
        functools.partial(block_kernel, chunks, chunks * LANES),
        out_shape=(
            jax.ShapeDtypeStruct((rows, slab + 16, LANES), jnp.int16),
            jax.ShapeDtypeStruct((side,) * 3 + (LANES // 16 + 1, 16, LANES), jnp.int16),
        ),
        in_specs=[vmem, hbm, hbm, vmem, hbm, hbm, hbm, hbm],
        out_specs=(vmem, vmem),
        scratch_shapes=[pltpu.VMEM((tall, LANES), F32)] * 6
        + [pltpu.VMEM((rows, slab + 16, LANES), jnp.int16)] * 3
        + [
            pltpu.VMEM((rows, 1, LANES), jnp.int32),
            pltpu.VMEM((2, slab, LANES, LANES), BF16),
            pltpu.VMEM((vocab // LANES * slab, LANES), BF16),
            pltpu.VMEM((10, slab, LANES), F32),
            pltpu.VMEM((modes, LANES), F32),
            pltpu.VMEM((modes, LANES), F32),
            pltpu.VMEM((modes, LANES), jnp.int32),
            pltpu.VMEM((vocab, LANES), BF16),
            pltpu.VMEM((LANES, vocab), F32),
            pltpu.VMEM((3, 3, LANES), F32),
            pltpu.VMEM((8, slab * modes, LANES), BF16),
            pltpu.VMEM((2, slab, LANES, LANES), BF16),
            pltpu.VMEM((2, 2 * GROUP * modes, GROUP * LANES), BF16),
            pltpu.VMEM((slab // GROUP, 2, 8, LANES), F32),
            pltpu.VMEM((side, slab, LANES), F32),
            pltpu.VMEM((LANES, LANES), F32),
            dma((6,)), dma((2, 2)), dma((2,)), dma((2,)), dma((2, 3)), dma((3, 3, 3)), dma((3, 3, 3)),
        ],
        compiler_params=pltpu.CompilerParams(
            vmem_limit_bytes=56 * 1024 * 1024, collective_id=0, has_side_effects=True
        ),
        name="hyena_block",
    )(tok, embedding, conv_taps, gains, residues, decays, seeds, cot)


def finish_kernel(every, mixer, grad_out, mixer_out):
    tiles = every.shape[3] - 1
    for z in range(every.shape[0]):
        for x in range(every.shape[1]):
            n = z * every.shape[1] + x
            for y in range(every.shape[2]):
                grad_out[y * LANES : (y + 1) * LANES, n * LANES : (n + 1) * LANES] = real(
                    every[z, x, y, :tiles].reshape(LANES, LANES), every[z, x, y, tiles]
                )
    slab = mixer.shape[1] - 16
    for n in range(mixer.shape[0]):
        mixer_out[n * slab : (n + 1) * slab, :] = real(mixer[n, :slab, :], mixer[n, slab:, :])


def finish(mixer, every):
    a, b, c, tiles, height = every.shape[:5]
    blocks, slab = mixer.shape[0], mixer.shape[1] - 16
    tall = blocks * slab
    fold = 2
    steps = c // fold
    return pl.pallas_call(
        finish_kernel,
        grid=(steps,),
        out_shape=(
            jax.ShapeDtypeStruct((c * LANES, a * b * LANES), F32),
            jax.ShapeDtypeStruct((tall, LANES), F32),
        ),
        in_specs=[
            pl.BlockSpec((a, b, fold, tiles, height, LANES), lambda n: (0, 0, n, 0, 0, 0)),
            pl.BlockSpec((blocks // steps, *mixer.shape[1:]), lambda n: (n, 0, 0)),
        ],
        out_specs=(
            pl.BlockSpec((fold * LANES, a * b * LANES), lambda n: (n, 0)),
            pl.BlockSpec((tall // steps, LANES), lambda n: (n, 0)),
        ),
        name="finish",
    )(every, mixer)


def body(token_ids, embedding, conv_taps, residues, decays, filter_seed, skip_gain, cotangent):
    ctx_size = lax.axis_size("ctx")
    width = conv_taps.shape[2]
    tok_block = token_ids.shape[1]
    packed = run_block(
        token_ids, embedding, conv_taps, skip_gain.reshape(-1, LANES),
        residues.T, decays.T, filter_seed.T, cotangent.reshape(width, tok_block), ctx_size,
    )
    grad, mixer = finish(*packed)
    return mixer.reshape(cotangent.shape), grad


def solution(mesh):
    placed = (P("fsdp", "ctx"), P(None, "fsdp"), P(), P(), P(), P(), P(), P("fsdp", None, "ctx"))
    return jax.shard_map(
        body,
        mesh=mesh,
        in_specs=placed,
        out_specs=(P("fsdp", None, "ctx"), P(None, "fsdp")),
        check_vma=False,
    )
```
